32 devices in a mesh: dp: 8 (over y, x, core), mp: 4 (over z).
Axes of the slice: x: 2, y: 2, z: 4, core: 2. Of those that a mesh axis runs over, the one named last changes fastest.
Arguments:
- block_in: float32 [9216, 1024], P(('dp', 'mp')), may hold values from -6 to 6
- out_grad: float32 [9216, 1024], P(('dp', 'mp')), may hold values from -6 to 6
- segment_ids: int32 [9216], P('dp'), may hold values from 0 to 31, never falling along the last dimension, each value on 1 to 576 neighbouring positions
- w_qkv: bfloat16 [3, 1024, 1024], P(None, 'dp', 'mp')
- w_out: bfloat16 [1024, 1024], P('mp', 'dp'), may hold values from -0.75 to 0.75
- w_up: bfloat16 [1024, 4096], P('dp', 'mp'), may hold values from -0.1875 to 0.1875
- w_down: bfloat16 [4096, 1024], P('mp', 'dp'), may hold values from -0.25 to 0.25
- ln1_gain: float32 [1024], P(('dp', 'mp')), may hold values from 0.5 to 1.5
- ln1_bias: float32 [1024], P(('dp', 'mp')), may hold values from -3 to 3
- bias_qv: float32 [2, 1024], P(None, ('dp', 'mp')), may hold values from -3 to 3
- bias_out: float32 [1024], P(('dp', 'mp')), may hold values from -3 to 3
- ln2_gain: float32 [1024], P(('dp', 'mp')), may hold values from 0.5 to 1.5
- ln2_bias: float32 [1024], P(('dp', 'mp')), may hold values from -3 to 3
- bias_up: float32 [4096], P(('dp', 'mp')), may hold values from -3 to 3
- bias_down: float32 [1024], P(('dp', 'mp')), may hold values from -3 to 3
Outputs:
- block_out: float32 [9216, 1024], P(('dp', 'mp'))
- in_grad: float32 [9216, 1024], P(('dp', 'mp'))
- grad_w_qkv: float32 [3, 1024, 1024], P(None, 'dp', 'mp')
- grad_w_out: float32 [1024, 1024], P('mp', 'dp')
- grad_w_up: float32 [1024, 4096], P('dp', 'mp')
- grad_w_down: float32 [4096, 1024], P('mp', 'dp')
- grad_ln1_gain: float32 [1024], P(('dp', 'mp'))
- grad_ln1_bias: float32 [1024], P(('dp', 'mp'))
- grad_bias_qv: float32 [2, 1024], P(None, ('dp', 'mp'))
- grad_bias_out: float32 [1024], P(('dp', 'mp'))
- grad_ln2_gain: float32 [1024], P(('dp', 'mp'))
- grad_ln2_bias: float32 [1024], P(('dp', 'mp'))
- grad_bias_up: float32 [4096], P(('dp', 'mp'))
- grad_bias_down: float32 [1024], P(('dp', 'mp'))
The draws below stay inside these ranges and needn't reach their ends.
Inputs may be any that keep to these rules, and one draw needn't show every extreme that they name: `segment_ids`: segment numbers never fall along the tokens; a segment spans 1 to 576 tokens.
All inputs are finite; a program needn't handle non-finite values.
Results may differ from the reference program's by a relative error of at most 0.011.
Values may be sent and summed in bfloat16 or wider, within the bound.
No kernel may reach another device: no remote copies, remote signals or barrier semaphores. Data moves between devices by JAX's collectives and lax.ppermute only.
A program may use at most 128 MiB of HBM per device.

```python
import math
import jax
import jax.numpy as jnp
import numpy as np
from jax import lax

D = 1024
H = 16
HD = 64
FF = 4096
L = 1152
QB = 576
TOKENS = 9216


def draw_w_qkv(key, part):
    base_key = jax.random.fold_in(key, 0)
    matrix = jax.random.normal(base_key, (3, D, D), jnp.float32) * D ** (-0.5)
    return matrix.astype(jnp.bfloat16)


def strengthened(values, rng, source, target, blocks, factor):
    def block_of(dim):
        return (jnp.arange(values.shape[dim]) // (values.shape[dim] // blocks)).reshape((-1,) + (1,) * (values.ndim - 1 - dim))

    near = jax.random.permutation(rng, blocks)[block_of(target)]
    second = (block_of(target) + blocks // 2) % blocks
    return jnp.where((block_of(source) == near) | (block_of(source) == second), factor * values, values)


def block_scale(stream_key, extent, shards, low, high):
    level = 1.0
    for axis_at, blocks in shards:
        heights = jax.random.uniform(jax.random.fold_in(jax.random.fold_in(stream_key, 6), axis_at), (blocks,), jnp.float32, low / len(shards), high / len(shards))
        level = level * jnp.repeat(jnp.exp(heights), extent[axis_at] // blocks).reshape((-1,) + (1,) * (len(extent) - 1 - axis_at))
    return level


def split_up(amount, total, reach, lean):
    loads = [(1 << 20) // math.isqrt(grade ** lean) + 1 for grade in range(2, amount + 1)]
    surplus, given = total - reach - (amount - 1), [1] * (amount - 1)
    while surplus > 0:
        free = [i for i in range(amount - 1) if given[i] < reach]
        whole, budget = sum([loads[i] for i in free]), surplus
        for i in free:
            more = min(reach - given[i], max(1, budget * loads[i] // whole), surplus)
            given[i] = given[i] + more
            surplus = surplus - more
    return np.array([reach] + given)


def ragged(own_key, count, total, most, slope):
    if count == 2:
        one = jax.random.randint(own_key, (), max(1, total - most), min(most, total - 1) + 1)
        return jnp.stack([one, total - one])
    lengths = jnp.asarray(split_up(count, total, most, slope), jnp.int32)
    twos = (count - 1) // 2
    giver, sink = lengths[1:1 + 2 * twos:2], lengths[2:2 + 2 * twos:2]
    slack = jnp.minimum(giver - 1, most - sink)
    passed = jax.random.randint(jax.random.fold_in(own_key, 1), (twos,), 0, 1 << 20) % (slack + 1)
    lengths = lengths.at[1:1 + 2 * twos:2].set(giver - passed).at[2:2 + 2 * twos:2].set(sink + passed)
    return lengths[jax.random.permutation(jax.random.fold_in(own_key, 2), count)]


def normal_values(own_key, extent, spread, reach, shards=(), held_as=jnp.bfloat16):
    result = spread * jax.random.normal(own_key, extent, jnp.float32)
    if shards:
        result = result * block_scale(own_key, extent, shards, -0.22, 0.18)
    return jnp.clip(result, -reach, reach).astype(held_as)


def noise_with(stream_key, shape, spread, limit, cuts, heavy, kind=jnp.bfloat16):
    values = spread * jax.random.normal(stream_key, shape, jnp.float32)
    if cuts:
        values = values * block_scale(stream_key, shape, cuts, -0.22, 0.18)
    return jnp.clip(strengthened(values, jax.random.fold_in(stream_key, 3), *heavy), -limit, limit).astype(kind)


def setup_inputs(seed: int = 0) -> dict:
    keys = jax.random.split(jax.random.key(seed), 16)
    return {
        "block_in": normal_values(keys[0], (TOKENS, D), 1.0, 6.0, ((0, 32),), jnp.float32),
        "out_grad": noise_with(keys[1], (TOKENS, D), 1.0, 6.0, ((0, 32),), (0, 1, 32, 2.75), jnp.float32),
        "segment_ids": jnp.searchsorted(jnp.cumsum(ragged(keys[2], TOKENS // (L // 4), TOKENS, L // 2, 1)), jnp.arange(TOKENS), side="right").astype(jnp.int32),
        "w_qkv": draw_w_qkv(jax.random.fold_in(keys[15], 71), 0),
        "w_out": normal_values(keys[4], (D, D), (D // 16) ** -0.5, 0.75, ((0, 4), (1, 8))),
        "w_up": normal_values(keys[5], (D, FF), D ** -0.5, 0.1875, ((0, 8), (1, 4))),
        "w_down": noise_with(keys[6], (FF, D), (FF // 4) ** -0.5, 0.25, ((0, 4), (1, 8)), (0, 1, 8, 2.0)),
        "ln1_gain": jnp.clip(1.0 + 0.1 * jax.random.normal(keys[7], (D,), jnp.float32), 0.5, 1.5),
        "ln1_bias": normal_values(keys[8], (D,), 0.3, 3.0, ((0, 32),), jnp.float32),
        "bias_qv": normal_values(keys[9], (2, D), 0.5, 3.0, ((1, 32),), jnp.float32),
        "bias_out": normal_values(keys[10], (D,), 0.3, 3.0, ((0, 32),), jnp.float32),
        "ln2_gain": jnp.clip(1.0 + 0.1 * jax.random.normal(keys[11], (D,), jnp.float32), 0.5, 1.5),
        "ln2_bias": normal_values(keys[12], (D,), 0.3, 3.0, ((0, 32),), jnp.float32),
        "bias_up": normal_values(keys[13], (FF,), 0.5, 3.0, ((0, 32),), jnp.float32),
        "bias_down": normal_values(keys[14], (D,), 0.3, 3.0, ((0, 32),), jnp.float32),
    }


NORM_EPS = 1e-05
GELU_SCALE = 0.7978845608028654
GELU_CUBE = 0.044715

def gelu_value(pre_act):
    inner = jnp.tanh(GELU_SCALE * (pre_act + GELU_CUBE * pre_act * pre_act * pre_act))
    return 0.5 * pre_act * (1.0 + inner)

def gelu_slope(pre_act):
    inner = jnp.tanh(GELU_SCALE * (pre_act + GELU_CUBE * pre_act * pre_act * pre_act))
    return 0.5 * (1.0 + inner) + 0.5 * pre_act * (1.0 - inner * inner) * GELU_SCALE * (1.0 + 3.0 * GELU_CUBE * pre_act * pre_act)

def norm_rows(inputs):
    center = inputs - lax.optimization_barrier(jnp.mean(inputs, axis=-1, keepdims=True))
    scale_inv = lax.rsqrt(lax.optimization_barrier(jnp.mean(center * center, axis=-1, keepdims=True)) + NORM_EPS)
    return (center * scale_inv, scale_inv)

def norm_back(norm_grad, x_hat, scale_inv, gain):
    scaled = norm_grad * gain
    return scale_inv * (scaled - lax.optimization_barrier(jnp.mean(scaled, axis=-1, keepdims=True)) - x_hat * lax.optimization_barrier(jnp.mean(scaled * x_hat, axis=-1, keepdims=True)))

def cross_dot(left, right):
    return lax.dot_general(left, right, (((0,), (0,)), ((), ())), preferred_element_type=jnp.float32)

def trans_dot(left, right):
    return lax.dot_general(left, right, (((1,), (1,)), ((), ())), preferred_element_type=jnp.float32)

def to_heads(flat, n_heads):
    return flat.reshape(flat.shape[0], n_heads, HD).transpose(1, 0, 2)

def from_heads(stacked):
    return stacked.transpose(1, 0, 2).reshape(stacked.shape[1], -1)

def head_scores(query_blk, key_rows, head_slope, row_start, seg_rows, seg_all):
    raw_scores = trans_dot(query_blk, key_rows) * HD ** (-0.5)
    row_pos = row_start + jnp.arange(query_blk.shape[0], dtype=jnp.int32)
    col_pos = jnp.arange(key_rows.shape[0], dtype=jnp.int32)
    distance = (row_pos[:, None] - col_pos[None, :]).astype(jnp.float32)
    allowed = (col_pos[None, :] <= row_pos[:, None]) & (seg_rows[:, None] == seg_all[None, :])
    return jnp.where(allowed, raw_scores - head_slope * distance, -1e+30)

def head_forward(query_rows, key_rows, value_rows, head_slope, seg_all):

    def one_block(block_id):
        row_start = block_id * QB
        query_blk = lax.dynamic_slice_in_dim(query_rows, row_start, QB, 0)
        seg_rows = lax.dynamic_slice_in_dim(seg_all, row_start, QB, 0)
        scores = head_scores(query_blk, key_rows, head_slope, row_start, seg_rows, seg_all)
        top_score = lax.optimization_barrier(jnp.max(scores, axis=1, keepdims=True))
        log_total = top_score + jnp.log(lax.optimization_barrier(jnp.sum(jnp.exp(scores - top_score), axis=1, keepdims=True)))
        prob_rows = jnp.exp(scores - log_total).astype(jnp.bfloat16)
        attended = jnp.dot(prob_rows, value_rows, preferred_element_type=jnp.float32).astype(jnp.bfloat16)
        return (attended, log_total[:, 0])
    attended, log_total = lax.map(one_block, jnp.arange(L // QB, dtype=jnp.int32))
    return (attended.reshape(L, HD), log_total.reshape(L))

def head_backward(query_rows, key_rows, value_rows, attended, attended_grad, log_total, head_slope, seg_all):
    delta_all = lax.optimization_barrier(jnp.sum(attended.astype(jnp.float32) * attended_grad.astype(jnp.float32), axis=1))
    score_scale = HD ** (-0.5)

    def one_block(running, block_id):
        key_grad, value_grad = running
        row_start = block_id * QB
        query_blk = lax.dynamic_slice_in_dim(query_rows, row_start, QB, 0)
        grad_blk = lax.dynamic_slice_in_dim(attended_grad, row_start, QB, 0)
        total_blk = lax.dynamic_slice_in_dim(log_total, row_start, QB, 0)
        delta_blk = lax.dynamic_slice_in_dim(delta_all, row_start, QB, 0)
        seg_rows = lax.dynamic_slice_in_dim(seg_all, row_start, QB, 0)
        scores = head_scores(query_blk, key_rows, head_slope, row_start, seg_rows, seg_all)
        prob_full = jnp.exp(scores - total_blk[:, None])
        prob_rows = prob_full.astype(jnp.bfloat16)
        value_grad = value_grad + cross_dot(prob_rows, grad_blk)
        prob_grad = trans_dot(grad_blk, value_rows)
        score_grad = (prob_full * (prob_grad - delta_blk[:, None])).astype(jnp.bfloat16)
        query_grad = jnp.dot(score_grad, key_rows, preferred_element_type=jnp.float32) * score_scale
        key_grad = key_grad + cross_dot(score_grad, query_blk) * score_scale
        return ((key_grad, value_grad), query_grad)
    empty = jnp.zeros(key_rows.shape, jnp.float32)
    (key_grad, value_grad), query_grad = lax.scan(one_block, (empty, empty), jnp.arange(L // QB, dtype=jnp.int32))
    return (query_grad.reshape(L, HD), key_grad, value_grad)

def layer_sequence(block_rows, grad_rows, seg_all, w_qkv, w_out, w_up, w_down, ln1_gain, ln1_bias, bias_qv, bias_out, ln2_gain, ln2_bias, bias_up, bias_down, slopes):
    hat_one, inv_one = norm_rows(block_rows)
    normed_one = (hat_one * ln1_gain + ln1_bias).astype(jnp.bfloat16)
    query_heads = to_heads((jnp.dot(normed_one, w_qkv[0], preferred_element_type=jnp.float32) + bias_qv[0]).astype(jnp.bfloat16), H)
    key_heads = to_heads(jnp.dot(normed_one, w_qkv[1], preferred_element_type=jnp.float32).astype(jnp.bfloat16), H)
    value_heads = to_heads((jnp.dot(normed_one, w_qkv[2], preferred_element_type=jnp.float32) + bias_qv[1]).astype(jnp.bfloat16), H)

    def one_head(packed):
        return head_forward(packed[0], packed[1], packed[2], packed[3], seg_all)
    attended_heads, total_heads = lax.map(one_head, (query_heads, key_heads, value_heads, slopes))
    attended = from_heads(attended_heads)
    resid = block_rows + jnp.dot(attended, w_out, preferred_element_type=jnp.float32) + bias_out
    hat_two, inv_two = norm_rows(resid)
    normed_two = (hat_two * ln2_gain + ln2_bias).astype(jnp.bfloat16)
    pre_act = jnp.dot(normed_two, w_up, preferred_element_type=jnp.float32) + bias_up
    hidden = gelu_value(pre_act).astype(jnp.bfloat16)
    block_out = resid + jnp.dot(hidden, w_down, preferred_element_type=jnp.float32) + bias_down
    grad_low = grad_rows.astype(jnp.bfloat16)
    grad_down = cross_dot(hidden, grad_low)
    pre_grad = trans_dot(grad_low, w_down) * gelu_slope(pre_act)
    pre_low = pre_grad.astype(jnp.bfloat16)
    grad_up = cross_dot(normed_two, pre_low)
    two_grad = trans_dot(pre_low, w_up)
    resid_grad = grad_rows + norm_back(two_grad, hat_two, inv_two, ln2_gain)
    resid_low = resid_grad.astype(jnp.bfloat16)
    grad_out = cross_dot(attended, resid_low)
    attended_grad = to_heads(trans_dot(resid_low, w_out).astype(jnp.bfloat16), H)

    def back_head(packed):
        return head_backward(packed[0], packed[1], packed[2], packed[3], packed[4], packed[5], packed[6], seg_all)
    query_grad, key_grad, value_grad = lax.map(back_head, (query_heads, key_heads, value_heads, attended_heads, attended_grad, total_heads, slopes))
    query_flat = from_heads(query_grad)
    key_flat = from_heads(key_grad)
    value_flat = from_heads(value_grad)
    qkv_low = [query_flat.astype(jnp.bfloat16), key_flat.astype(jnp.bfloat16), value_flat.astype(jnp.bfloat16)]
    grad_qkv = jnp.stack([cross_dot(normed_one, grad_part) for grad_part in qkv_low])
    one_grad = trans_dot(qkv_low[0], w_qkv[0]) + trans_dot(qkv_low[1], w_qkv[1]) + trans_dot(qkv_low[2], w_qkv[2])
    in_grad = resid_grad + norm_back(one_grad, hat_one, inv_one, ln1_gain)
    grads = (grad_qkv, grad_out, grad_up, grad_down, lax.optimization_barrier(jnp.sum(one_grad * hat_one, axis=0)), lax.optimization_barrier(jnp.sum(one_grad, axis=0)), jnp.stack([lax.optimization_barrier(jnp.sum(query_flat, axis=0)), lax.optimization_barrier(jnp.sum(value_flat, axis=0))]), lax.optimization_barrier(jnp.sum(resid_grad, axis=0)), lax.optimization_barrier(jnp.sum(two_grad * hat_two, axis=0)), lax.optimization_barrier(jnp.sum(two_grad, axis=0)), lax.optimization_barrier(jnp.sum(pre_grad, axis=0)), lax.optimization_barrier(jnp.sum(grad_rows, axis=0)))
    return (block_out, in_grad, grads)

def reference(block_in, out_grad, segment_ids, w_qkv, w_out, w_up, w_down, ln1_gain, ln1_bias, bias_qv, bias_out, ln2_gain, ln2_bias, bias_up, bias_down):
    n_rows = block_in.shape[0] // L
    slopes = jnp.exp2(-8.0 * (jnp.arange(H, dtype=jnp.int32) + 1).astype(jnp.float32) / H)
    inputs = (block_in.reshape(n_rows, L, D), out_grad.reshape(n_rows, L, D), segment_ids.reshape(n_rows, L))
    zeros = (jnp.zeros(w_qkv.shape, jnp.float32), jnp.zeros(w_out.shape, jnp.float32), jnp.zeros(w_up.shape, jnp.float32), jnp.zeros(w_down.shape, jnp.float32), jnp.zeros(ln1_gain.shape, jnp.float32), jnp.zeros(ln1_bias.shape, jnp.float32), jnp.zeros(bias_qv.shape, jnp.float32), jnp.zeros(bias_out.shape, jnp.float32), jnp.zeros(ln2_gain.shape, jnp.float32), jnp.zeros(ln2_bias.shape, jnp.float32), jnp.zeros(bias_up.shape, jnp.float32), jnp.zeros(bias_down.shape, jnp.float32))

    def one_row(totals, packed):
        block_out, in_grad, grads = layer_sequence(packed[0], packed[1], packed[2], w_qkv, w_out, w_up, w_down, ln1_gain, ln1_bias, bias_qv, bias_out, ln2_gain, ln2_bias, bias_up, bias_down, slopes)
        return (jax.tree.map(jnp.add, totals, grads), (block_out, in_grad))
    totals, (outputs, in_grads) = lax.scan(one_row, zeros, inputs)
    return (outputs.reshape(-1, D), in_grads.reshape(-1, D), totals[0], totals[1], totals[2], totals[3], totals[4], totals[5], totals[6], totals[7], totals[8], totals[9], totals[10], totals[11])
```

```python
import jax
import jax.numpy as jnp
from jax import lax
from jax.experimental import pallas as pl
from jax.experimental.pallas import tpu as pltpu
from jax.sharding import PartitionSpec as P

H = 16
HD = 64
L = 1152
BLK = 128
REACH = 5

NORM_EPS = 1e-05
GELU_SCALE = 0.7978845608028654
GELU_CUBE = 0.044715
BF = jnp.bfloat16
F32 = jnp.float32


def gelu_both(pre_act):
    inner = jnp.tanh(GELU_SCALE * (pre_act + GELU_CUBE * pre_act * pre_act * pre_act))
    value = 0.5 * pre_act * (1.0 + inner)
    slope = 0.5 * (1.0 + inner) + 0.5 * pre_act * (1.0 - inner * inner) * GELU_SCALE * (
        1.0 + 3.0 * GELU_CUBE * pre_act * pre_act
    )
    return value, slope


def norm_rows(inputs):
    center = inputs - jnp.mean(inputs, axis=-1, keepdims=True)
    scale_inv = lax.rsqrt(jnp.mean(center * center, axis=-1, keepdims=True) + NORM_EPS)
    return (center * scale_inv, scale_inv)


def norm_back(norm_grad, x_hat, scale_inv, gain):
    scaled = norm_grad * gain
    return scale_inv * (
        scaled
        - jnp.mean(scaled, axis=-1, keepdims=True)
        - x_hat * jnp.mean(scaled * x_hat, axis=-1, keepdims=True)
    )


def dot(left, right):
    return jnp.dot(left, right, preferred_element_type=F32)


def cross_dot(left, right):
    return lax.dot_general(left, right, (((0,), (0,)), ((), ())), preferred_element_type=F32)


def trans_dot(left, right):
    return lax.dot_general(left, right, (((1,), (1,)), ((), ())), preferred_element_type=F32)


def flip(x):
    return x.astype(F32).T


def load_rows(order_ref, src_ref, dst_ref, nb, rb):
    for k in range(nb):
        dst_ref[k * rb : (k + 1) * rb, :] = src_ref[order_ref[k]]


def half_masks(shape):
    lane = lax.broadcasted_iota(jnp.int32, shape, 1)
    return (lane < HD, lane >= HD)


def distances(b, segr_ref, segc_ref):
    w0 = max(0, b - REACH) * BLK
    w1 = (b + 1) * BLK
    keys = w0 + lax.broadcasted_iota(jnp.int32, (w1 - w0, BLK), 0)
    rows = b * BLK + lax.broadcasted_iota(jnp.int32, (w1 - w0, BLK), 1)
    same = segc_ref[w0:w1, :] == segr_ref[:, b * BLK : (b + 1) * BLK]
    gap = rows - keys
    dist = jnp.where(same & (gap >= 0), gap.astype(F32), 1e30)
    return w0, w1, dist


def attn_fwd_kernel(
    order_ref, slope_ref, segr_ref, segc_ref, q_ref, k_ref, v_ref, att_ref, lse_ref,
    q_s, k_s, v_s, vt_s, a_s, *, nb, rb,
):
    pair = pl.program_id(0)
    load_rows(order_ref, q_ref, q_s, nb, rb)
    load_rows(order_ref, k_ref, k_s, nb, rb)
    load_rows(order_ref, v_ref, v_s, nb, rb)
    vt_s[...] = flip(v_s[...]).astype(BF)
    halves = half_masks((BLK, 2 * HD))
    for b in range(L // BLK):
        r0 = b * BLK
        w0, w1, dist = distances(b, segr_ref, segc_ref)
        q_blk = q_s[r0 : r0 + BLK, :] * BF(HD ** (-0.5))
        outs = []
        for h in range(2):
            q_h = jnp.where(halves[h], q_blk, BF(0))
            s = trans_dot(k_s[w0:w1, :], q_h) - slope_ref[2 * pair + h] * dist
            top = jnp.max(s, axis=0, keepdims=True)
            e = jnp.exp(s - top)
            total = jnp.sum(e, axis=0, keepdims=True)
            lse_ref[0, h : h + 1, r0 : r0 + BLK] = top + jnp.log(total)
            prob = (e * (1.0 / total)).astype(BF)
            outs.append(dot(vt_s[h * HD : (h + 1) * HD, w0:w1], prob))
        a_s[r0 : r0 + BLK, :] = jnp.concatenate(outs, axis=0).T.astype(BF)
    for k in range(nb):
        att_ref[order_ref[k]] = a_s[k * rb : (k + 1) * rb, :]


def attn_bwd_kernel(
    order_ref, slope_ref, segr_ref, segc_ref, q_ref, k_ref, v_ref, att_ref, grad_ref, lse_ref,
    out_ref, sum_ref, q_s, k_s, v_s, kt_s, a_s, g_s, dq_s, dk_s, dv_s, *, nb, rb,
):
    pair = pl.program_id(0)
    load_rows(order_ref, q_ref, q_s, nb, rb)
    load_rows(order_ref, k_ref, k_s, nb, rb)
    load_rows(order_ref, v_ref, v_s, nb, rb)
    load_rows(order_ref, att_ref, a_s, nb, rb)
    load_rows(order_ref, grad_ref, g_s, nb, rb)
    kt_s[...] = flip(k_s[...]).astype(BF)
    dk_s[...] = jnp.zeros(dk_s.shape, F32)
    dv_s[...] = jnp.zeros(dv_s.shape, F32)
    halves = half_masks((BLK, 2 * HD))
    q_sum = jnp.zeros((1, 2 * HD), F32)
    for b in range(L // BLK):
        r0 = b * BLK
        w0, w1, dist = distances(b, segr_ref, segc_ref)
        q_blk = q_s[r0 : r0 + BLK, :] * BF(HD ** (-0.5))
        g_blk = g_s[r0 : r0 + BLK, :]
        prod = (a_s[r0 : r0 + BLK, :].astype(F32) * g_blk.astype(F32)).T
        probs, grads, q_hs, g_hs, dq_t = [], [], [], [], []
        for h in range(2):
            q_h = jnp.where(halves[h], q_blk, BF(0))
            g_h = jnp.where(halves[h], g_blk, BF(0))
            s = trans_dot(k_s[w0:w1, :], q_h) - slope_ref[2 * pair + h] * dist
            p = jnp.exp(s - lse_ref[0, h : h + 1, r0 : r0 + BLK])
            delta = jnp.sum(prod[h * HD : (h + 1) * HD, :], axis=0, keepdims=True)
            dp = trans_dot(v_s[w0:w1, :], g_h)
            ds = (p * (dp - delta)).astype(BF)
            dq_t.append(dot(kt_s[h * HD : (h + 1) * HD, w0:w1], ds))
            probs.append(p.astype(BF))
            grads.append(ds)
            q_hs.append(q_h)
            g_hs.append(g_h)
        dv_s[w0:w1, :] += dot(jnp.concatenate(probs, axis=1), jnp.concatenate(g_hs, axis=0))
        dk_s[w0:w1, :] += dot(jnp.concatenate(grads, axis=1), jnp.concatenate(q_hs, axis=0))
        dq = jnp.concatenate(dq_t, axis=0).T * HD ** (-0.5)
        q_sum = q_sum + jnp.sum(dq, axis=0, keepdims=True)
        dq_s[r0 : r0 + BLK, :] = dq.astype(BF)
    sum_ref[0, 0:1, :] = q_sum
    sum_ref[0, 1:2, :] = jnp.sum(dv_s[...], axis=0, keepdims=True)
    for k in range(nb):
        rows = slice(k * rb, (k + 1) * rb)
        out_ref[order_ref[k], :, 0 : 2 * HD] = dq_s[rows, :]
        out_ref[order_ref[k], :, 2 * HD : 4 * HD] = dk_s[rows, :].astype(BF)
        out_ref[order_ref[k], :, 4 * HD : 6 * HD] = dv_s[rows, :].astype(BF)


def attn_specs(nb, rb):
    smem = pl.BlockSpec(memory_space=pltpu.SMEM)
    col = lambda which: pl.BlockSpec((nb, rb, 2 * HD), lambda p: (0, 0, 3 * p + which))
    base = [
        smem,
        smem,
        pl.BlockSpec((1, L), lambda p: (0, 0)),
        pl.BlockSpec((L, 1), lambda p: (0, 0)),
        col(0),
        col(1),
        col(2),
    ]
    one = pl.BlockSpec((nb, rb, 2 * HD), lambda p: (0, 0, p))
    lse = pl.BlockSpec((1, 2, L), lambda p: (p, 0, 0))
    return base, one, lse


def attn_fwd(order, slopes, segs, qkv):
    nb, rb, cols = qkv.shape
    pairs = cols // (6 * HD)
    base, one, lse = attn_specs(nb, rb)
    rows = lambda: pltpu.VMEM((L, 2 * HD), BF)
    return pl.pallas_call(
        lambda *refs: attn_fwd_kernel(*refs, nb=nb, rb=rb),
        grid=(pairs,),
        in_specs=base,
        out_specs=[one, lse],
        out_shape=[
            jax.ShapeDtypeStruct((nb, rb, pairs * 2 * HD), BF),
            jax.ShapeDtypeStruct((pairs, 2, L), F32),
        ],
        scratch_shapes=[rows(), rows(), rows(), pltpu.VMEM((2 * HD, L), BF), rows()],
        name="attn_fwd",
    )(order, slopes, segs.reshape(1, L), segs.reshape(L, 1), qkv, qkv, qkv)


def attn_bwd(order, slopes, segs, qkv, att, att_grad, lse_rows):
    nb, rb, cols = qkv.shape
    pairs = cols // (6 * HD)
    base, one, lse = attn_specs(nb, rb)
    rows = lambda dt=BF: pltpu.VMEM((L, 2 * HD), dt)
    return pl.pallas_call(
        lambda *refs: attn_bwd_kernel(*refs, nb=nb, rb=rb),
        grid=(pairs,),
        in_specs=base + [one, one, lse],
        out_specs=[
            pl.BlockSpec((nb, rb, 6 * HD), lambda p: (0, 0, p)),
            pl.BlockSpec((1, 2, 2 * HD), lambda p: (p, 0, 0)),
        ],
        out_shape=[
            jax.ShapeDtypeStruct((nb, rb, cols), BF),
            jax.ShapeDtypeStruct((pairs, 2, 2 * HD), F32),
        ],
        scratch_shapes=[rows(), rows(), rows(), pltpu.VMEM((2 * HD, L), BF), rows(), rows(),
                        rows(), rows(F32), rows(F32)],
        name="attn_bwd",
    )(order, slopes, segs.reshape(1, L), segs.reshape(L, 1), qkv, qkv, qkv, att, att_grad, lse_rows)


def gather_vectors(vecs, n_dev):
    flat = jnp.concatenate([v.reshape(-1) for v in vecs])
    spread = jnp.broadcast_to(flat[None, :], (n_dev, flat.shape[0]))
    got = lax.all_to_all(spread, ("dp", "mp"), 0, 0, tiled=True)
    full, at = [], 0
    for v in vecs:
        n = v.size
        part = got[:, at : at + n]
        if v.ndim == 2:
            part = part.reshape(n_dev, v.shape[0], v.shape[1]).transpose(1, 0, 2)
            full.append(part.reshape(v.shape[0], -1))
        else:
            full.append(part.reshape(-1))
        at += n
    return full


def scatter_vectors(fulls, n_dev):
    parts, shapes = [], []
    for v in fulls:
        if v.ndim == 2:
            part = v.reshape(v.shape[0], n_dev, -1).transpose(1, 0, 2)
            shapes.append((v.shape[0], v.shape[1] // n_dev))
        else:
            part = v
            shapes.append((v.shape[0] // n_dev,))
        parts.append(part.reshape(n_dev, -1))
    got = lax.all_to_all(jnp.concatenate(parts, axis=1), ("dp", "mp"), 0, 0, tiled=True)
    flat = jnp.sum(got, axis=0)
    outs, at = [], 0
    for shape, part in zip(shapes, parts):
        n = part.shape[1]
        outs.append(flat[at : at + n].reshape(shape))
        at += n
    return outs


def head_slopes(numbers):
    return jnp.exp2(-8.0 * (numbers + 1).astype(F32) / H)


def pair_columns(parts):
    stacked = jnp.stack([p.reshape(p.shape[:-1] + (-1, 2 * HD)) for p in parts], axis=-2)
    return stacked.reshape(stacked.shape[:-3] + (-1,))


def local_any(n_dp, n_mp):
    n_dev = n_dp * n_mp

    def scatter_rows(part):
        return lax.psum_scatter(part.astype(BF), "mp", scatter_dimension=0, tiled=True).astype(F32)

    def scatter_grad(part, dim):
        return lax.psum_scatter(part.astype(BF), "dp", scatter_dimension=dim, tiled=True).astype(F32)

    def local(block_in, out_grad, segment_ids, w_qkv, w_out, w_up, w_down, *vecs):
        model_index = lax.axis_index("mp")
        gain_one, shift_one, qv_all, out_shift, gain_two, shift_two, up_all, down_shift = (
            gather_vectors(vecs, n_dev)
        )
        qkv_full = lax.all_gather(w_qkv, "dp", axis=1, tiled=True)
        out_full = lax.all_gather(w_out, "dp", axis=1, tiled=True)
        up_full = lax.all_gather(w_up, "dp", axis=0, tiled=True)
        down_full = lax.all_gather(w_down, "dp", axis=1, tiled=True)
        head_cols = qkv_full.shape[2]
        hid_cols = up_full.shape[1]
        n_heads = head_cols // HD
        qv_shift = lax.dynamic_slice_in_dim(qv_all, model_index * head_cols, head_cols, 1)
        up_shift = lax.dynamic_slice_in_dim(up_all, model_index * hid_cols, hid_cols, 0)
        slopes = head_slopes(model_index * n_heads + jnp.arange(n_heads, dtype=jnp.int32))
        order = jnp.zeros((1,), jnp.int32)
        w_local = pair_columns([qkv_full[0], qkv_full[1], qkv_full[2]])
        b_local = pair_columns([qv_shift[0], jnp.zeros_like(qv_shift[0]), qv_shift[1]])
        hat_one, inv_one = norm_rows(block_in)
        normed_one = (hat_one * gain_one + shift_one).astype(BF)
        rows_one = lax.all_gather(normed_one, "mp", axis=0, tiled=True)
        qkv = (dot(rows_one, w_local) + b_local).astype(BF)[None]
        att, lse = attn_fwd(order, slopes, segment_ids, qkv)
        resid = block_in + scatter_rows(dot(att[0], out_full)) + out_shift
        hat_two, inv_two = norm_rows(resid)
        normed_two = (hat_two * gain_two + shift_two).astype(BF)
        rows_two = lax.all_gather(normed_two, "mp", axis=0, tiled=True)
        value, slope = gelu_both(dot(rows_two, up_full) + up_shift)
        hidden = value.astype(BF)
        block_out = resid + scatter_rows(dot(hidden, down_full)) + down_shift
        grad_rows = lax.all_gather(out_grad.astype(BF), "mp", axis=0, tiled=True)
        down_share = scatter_grad(cross_dot(hidden, grad_rows), 1)
        pre_grad = trans_dot(grad_rows, down_full) * slope
        pre_low = pre_grad.astype(BF)
        up_share = scatter_grad(cross_dot(rows_two, pre_low), 0)
        two_grad = scatter_rows(trans_dot(pre_low, up_full))
        resid_grad = out_grad + norm_back(two_grad, hat_two, inv_two, gain_two)
        resid_rows = lax.all_gather(resid_grad.astype(BF), "mp", axis=0, tiled=True)
        out_share = scatter_grad(cross_dot(att[0], resid_rows), 1)
        att_grad = trans_dot(resid_rows, out_full).astype(BF)[None]
        d_qkv, sums = attn_bwd(order, slopes, segment_ids, qkv, att, att_grad, lse)
        grad_w = cross_dot(rows_one, d_qkv[0])
        grad_w = grad_w.reshape(grad_w.shape[0], -1, 3, 2 * HD).transpose(2, 0, 1, 3)
        qkv_share = scatter_grad(grad_w.reshape(3, grad_w.shape[1], -1), 1)
        one_grad = scatter_rows(trans_dot(d_qkv[0], w_local))
        in_grad = resid_grad + norm_back(one_grad, hat_one, inv_one, gain_one)
        qv_place = lax.dynamic_update_slice_in_dim(
            jnp.zeros(qv_all.shape, F32),
            sums.transpose(1, 0, 2).reshape(2, -1),
            model_index * head_cols,
            1,
        )
        up_place = lax.dynamic_update_slice_in_dim(
            jnp.zeros(up_all.shape, F32), jnp.sum(pre_grad, axis=0), model_index * hid_cols, 0
        )
        shares = scatter_vectors(
            [
                jnp.sum(one_grad * hat_one, axis=0),
                jnp.sum(one_grad, axis=0),
                qv_place,
                jnp.sum(resid_grad, axis=0),
                jnp.sum(two_grad * hat_two, axis=0),
                jnp.sum(two_grad, axis=0),
                up_place,
                jnp.sum(out_grad, axis=0),
            ],
            n_dev,
        )
        return (block_out, in_grad, qkv_share, out_share, up_share, down_share, *shares)

    return local


CHUNK_OF_T = (0, 3, 1, 2)
T_OF_CHUNK = (0, 2, 3, 1)
PLANE_OF_T = (0, 3, 1, 2)
GROUPS = [[0, 1, 2, 3], [4, 5, 6, 7]]
TO_PLANE = [
    ((4 * y + t) * 4 + z, (4 * y + T_OF_CHUNK[z]) * 4 + PLANE_OF_T[t])
    for y in range(2)
    for t in range(4)
    for z in range(4)
]
FROM_PLANE = [(b, a) for a, b in TO_PLANE]


def swap(x, bits):
    return lax.ppermute(x, "dp", [(i, i ^ bits) for i in range(8)])


def relocate(x):
    return lax.ppermute(x, ("dp", "mp"), TO_PLANE)


def bring_back(x):
    return lax.ppermute(x, ("dp", "mp"), FROM_PLANE)


def gather_t(x):
    near = swap(x, 1)
    far = swap(x, 2)
    return jnp.concatenate([x, near, far, swap(far, 1)], axis=0)


def scatter_t(part):
    n = part.shape[0] // 4
    low = part.astype(BF)
    near = swap(jnp.concatenate([low[n : 2 * n], low[3 * n :]], axis=0), 1)
    far = (part[2 * n : 3 * n] + near[n:].astype(F32)).astype(BF)
    return part[:n] + near[:n].astype(F32) + swap(far, 2).astype(F32)


def exchange_t(x):
    return lax.all_to_all(x, "dp", 0, 0, tiled=True, axis_index_groups=GROUPS)


def gather_yz(x, y_index):
    mine = lax.all_gather(x, "mp", axis=0, tiled=False)
    other = swap(mine, 4)
    first = jnp.where(y_index == 0, mine, other)
    second = jnp.where(y_index == 0, other, mine)
    return jnp.stack([first, second])


def scatter_yz(part, y_index):
    keep = jnp.where(y_index == 0, part[0], part[1])
    send = jnp.where(y_index == 0, part[1], part[0]).astype(BF)
    both = (keep.astype(F32) + swap(send, 4).astype(F32)).astype(BF)
    return lax.psum_scatter(both, "mp", scatter_dimension=0, tiled=False)


def local_plane(block_in, out_grad, segment_ids, w_qkv, w_out, w_up, w_down, *vecs):
    n_dev = 32
    d_index = lax.axis_index("dp")
    t_index = d_index % 4
    y_index = d_index // 4
    width = block_in.shape[1]
    sub = width // 2

    pack = jnp.concatenate(
        [
            w_qkv.reshape(3, -1, 4, HD).transpose(2, 1, 0, 3).reshape(4, -1, 3 * HD),
            w_out.reshape(4, HD, -1).transpose(0, 2, 1),
            w_up.reshape(w_up.shape[0], 4, -1).transpose(1, 0, 2),
            w_down.reshape(4, -1, w_down.shape[1]).transpose(0, 2, 1),
        ],
        axis=2,
    )
    pack = exchange_t(pack).reshape(sub, -1)
    heads = gather_yz(pack[:, : 4 * HD], y_index)
    hids = gather_yz(pack[:, 4 * HD :], y_index)
    heads = heads.reshape(2, 2, 2, sub, 4, HD).transpose(0, 3, 1, 4, 2, 5)
    heads = heads.reshape(width, 2, 4, 2 * HD)
    w_local = heads[:, :, :3].reshape(width, -1)
    w_out_t = heads[:, :, 3].reshape(width, -1)
    units = hids.shape[3] // 2
    up_local = hids[..., :units].transpose(0, 2, 1, 3).reshape(width, -1)
    down_t = hids[..., units:].transpose(0, 2, 1, 3).reshape(width, -1)

    gain_one, shift_one, qv_all, out_shift, gain_two, shift_two, up_all, down_shift = (
        gather_vectors(vecs, n_dev)
    )
    qv_mine = lax.dynamic_index_in_dim(qv_all.reshape(2, 4, 4, HD), t_index, 2, False)
    qv_mine = qv_mine.reshape(2, -1)
    b_local = pair_columns([qv_mine[0], jnp.zeros_like(qv_mine[0]), qv_mine[1]])
    up_shift = lax.dynamic_index_in_dim(up_all.reshape(4, 4, -1), t_index, 1, False).reshape(-1)
    slopes = head_slopes(4 * jnp.arange(4, dtype=jnp.int32) + t_index)
    chunk = jnp.asarray(CHUNK_OF_T, jnp.int32)[t_index]
    order = jnp.asarray(T_OF_CHUNK, jnp.int32)[jnp.arange(4, dtype=jnp.int32) ^ chunk]

    hat_one, inv_one = norm_rows(block_in)
    rows_one = gather_t(relocate((hat_one * gain_one + shift_one).astype(BF)))
    segs = relocate(segment_ids)
    block_here = relocate(block_in.astype(BF)).astype(F32)
    grad_low = relocate(out_grad.astype(BF))
    grad_here = grad_low.astype(F32)
    grad_rows = gather_t(grad_low)

    qkv = (dot(rows_one, w_local) + b_local).astype(BF).reshape(4, -1, w_local.shape[1])
    att, lse = attn_fwd(order, slopes, segs, qkv)
    att_rows = att.reshape(-1, att.shape[2])
    resid = block_here + scatter_t(trans_dot(att_rows, w_out_t)) + out_shift
    hat_two, inv_two = norm_rows(resid)
    rows_two = gather_t((hat_two * gain_two + shift_two).astype(BF))
    value, slope = gelu_both(dot(rows_two, up_local) + up_shift)
    hidden = value.astype(BF)
    pre_grad = dot(grad_rows, down_t) * slope
    pre_low = pre_grad.astype(BF)
    two_grad = scatter_t(trans_dot(pre_low, up_local))
    resid_grad = grad_here + norm_back(two_grad, hat_two, inv_two, gain_two)
    resid_low = resid_grad.astype(BF)
    resid_rows = gather_t(resid_low)

    block_out = resid + scatter_t(trans_dot(hidden, down_t)) + down_shift
    block_out = bring_back(block_out.astype(BF)).astype(F32)
    resid_back = bring_back(resid_low).astype(F32)

    g_up = cross_dot(rows_two, pre_low).astype(BF).reshape(2, sub, 4, units)
    g_down = cross_dot(grad_rows, hidden).astype(BF).reshape(2, sub, 4, units)
    g_hid = jnp.concatenate([g_up, g_down], axis=3).transpose(0, 2, 1, 3)
    g_hid = scatter_yz(g_hid, y_index).reshape(4, sub // 4, 2 * units)
    g_hid = exchange_t(g_hid).astype(F32)
    up_share = g_hid[..., :units].transpose(1, 0, 2).reshape(w_up.shape)
    down_share = g_hid[..., units:].transpose(0, 2, 1).reshape(w_down.shape)

    att_grad = dot(resid_rows, w_out_t).astype(BF).reshape(att.shape)
    d_qkv, sums = attn_bwd(order, slopes, segs, qkv, att, att_grad, lse)
    d_rows = d_qkv.reshape(-1, d_qkv.shape[2])
    one_grad = bring_back(scatter_t(trans_dot(d_rows, w_local)).astype(BF)).astype(F32)
    in_grad = resid_back + norm_back(one_grad, hat_one, inv_one, gain_one)

    g_qkv = cross_dot(rows_one, d_rows).astype(BF).reshape(2, sub, 2, 3, 2, HD)
    g_out = cross_dot(resid_rows, att_rows).astype(BF).reshape(2, sub, 2, 1, 2, HD)
    g_head = jnp.concatenate([g_qkv, g_out], axis=3).transpose(0, 2, 4, 1, 3, 5)
    g_head = scatter_yz(g_head.reshape(2, 4, sub, 4 * HD), y_index)
    g_head = exchange_t(g_head.reshape(4, sub // 4, 4 * HD)).astype(F32)
    g_head = g_head.reshape(4, sub // 4, 4, HD)
    qkv_share = g_head[:, :, :3].transpose(2, 1, 0, 3).reshape(w_qkv.shape)
    out_share = g_head[:, :, 3].transpose(0, 2, 1).reshape(w_out.shape)

    mine = jnp.arange(4, dtype=jnp.int32) == t_index
    qv_part = sums.transpose(1, 0, 2).reshape(2, 4, 1, HD)
    qv_place = jnp.where(mine[None, None, :, None], qv_part, 0.0).reshape(2, width)
    up_part = jnp.sum(pre_grad, axis=0).reshape(4, 1, units)
    up_place = jnp.where(mine[None, :, None], up_part, 0.0).reshape(-1)
    shares = scatter_vectors(
        [
            jnp.sum(one_grad * hat_one, axis=0),
            jnp.sum(one_grad, axis=0),
            qv_place,
            jnp.sum(resid_grad, axis=0),
            jnp.sum(two_grad * hat_two, axis=0),
            jnp.sum(two_grad, axis=0),
            up_place,
            jnp.sum(out_grad, axis=0),
        ],
        n_dev,
    )
    return (block_out, in_grad, qkv_share, out_share, up_share, down_share, *shares)


def solution(mesh):
    n_dp, n_mp = mesh.shape["dp"], mesh.shape["mp"]
    local = local_plane if (n_dp, n_mp) == (8, 4) else local_any(n_dp, n_mp)
    both = ("dp", "mp")
    weights = (P(None, "dp", "mp"), P("mp", "dp"), P("dp", "mp"), P("mp", "dp"))
    vectors = (P(both), P(both), P(None, both), P(both), P(both), P(both), P(both), P(both))
    return jax.shard_map(
        local,
        mesh=mesh,
        in_specs=(P(both, None), P(both, None), P("dp"), *weights, *vectors),
        out_specs=(P(both, None), P(both, None), *weights, *vectors),
        check_vma=False,
    )
```

```python
import jax
import jax.numpy as jnp
from jax import lax
from jax.experimental import pallas as pl
from jax.experimental.pallas import tpu as pltpu
from jax.sharding import PartitionSpec as P


H = 16
HD = 64
L = 1152
BLK = 128
REACH = 5

NORM_EPS = 1e-05
GELU_SCALE = 0.7978845608028654
GELU_CUBE = 0.044715

BF = jnp.bfloat16
F32 = jnp.float32


def gelu_both(pre_act):
    inner = jnp.tanh(GELU_SCALE * (pre_act + GELU_CUBE * pre_act * pre_act * pre_act))
    value = 0.5 * pre_act * (1.0 + inner)
    slope = 0.5 * (1.0 + inner) + 0.5 * pre_act * (1.0 - inner * inner) * GELU_SCALE * (
        1.0 + 3.0 * GELU_CUBE * pre_act * pre_act
    )
    return value, slope


def norm_rows(inputs):
    center = inputs - jnp.mean(inputs, axis=-1, keepdims=True)
    scale_inv = lax.rsqrt(jnp.mean(center * center, axis=-1, keepdims=True) + NORM_EPS)
    return (center * scale_inv, scale_inv)


def norm_back(norm_grad, x_hat, scale_inv, gain):
    scaled = norm_grad * gain
    return scale_inv * (
        scaled
        - jnp.mean(scaled, axis=-1, keepdims=True)
        - x_hat * jnp.mean(scaled * x_hat, axis=-1, keepdims=True)
    )


def dot(left, right):
    return jnp.dot(left, right, preferred_element_type=F32)


def cross_dot(left, right):
    return lax.dot_general(left, right, (((0,), (0,)), ((), ())), preferred_element_type=F32)


def trans_dot(left, right):
    return lax.dot_general(left, right, (((1,), (1,)), ((), ())), preferred_element_type=F32)


def flip(x):
    return x.astype(F32).T


def load_rows(order_ref, src_ref, dst_ref, nb, rb):
    for k in range(nb):
        dst_ref[k * rb : (k + 1) * rb, :] = src_ref[order_ref[k]]


def half_masks(shape):
    lane = lax.broadcasted_iota(jnp.int32, shape, 1)
    return (lane < HD, lane >= HD)


def distances(b, segr_ref, segc_ref):
    w0 = max(0, b - REACH) * BLK
    w1 = (b + 1) * BLK
    keys = w0 + lax.broadcasted_iota(jnp.int32, (w1 - w0, BLK), 0)
    rows = b * BLK + lax.broadcasted_iota(jnp.int32, (w1 - w0, BLK), 1)
    same = segc_ref[w0:w1, :] == segr_ref[:, b * BLK : (b + 1) * BLK]
    gap = rows - keys
    dist = jnp.where(same & (gap >= 0), gap.astype(F32), 1e30)
    return w0, w1, dist


def attn_fwd_kernel(
    order_ref, slope_ref, segr_ref, segc_ref, q_ref, k_ref, v_ref, att_ref, lse_ref,
    q_s, k_s, v_s, vt_s, a_s, *, nb, rb,
):
    pair = pl.program_id(0)
    load_rows(order_ref, q_ref, q_s, nb, rb)
    load_rows(order_ref, k_ref, k_s, nb, rb)
    load_rows(order_ref, v_ref, v_s, nb, rb)
    vt_s[...] = flip(v_s[...]).astype(BF)
    halves = half_masks((BLK, 2 * HD))
    for b in range(L // BLK):
        r0 = b * BLK
        w0, w1, dist = distances(b, segr_ref, segc_ref)
        q_blk = q_s[r0 : r0 + BLK, :] * BF(HD ** (-0.5))
        outs = []
        for h in range(2):
            q_h = jnp.where(halves[h], q_blk, BF(0))
            s = trans_dot(k_s[w0:w1, :], q_h) - slope_ref[2 * pair + h] * dist
            top = jnp.max(s, axis=0, keepdims=True)
            e = jnp.exp(s - top)
            total = jnp.sum(e, axis=0, keepdims=True)
            lse_ref[0, h : h + 1, r0 : r0 + BLK] = top + jnp.log(total)
            prob = (e * (1.0 / total)).astype(BF)
            outs.append(dot(vt_s[h * HD : (h + 1) * HD, w0:w1], prob))
        a_s[r0 : r0 + BLK, :] = jnp.concatenate(outs, axis=0).T.astype(BF)
    for k in range(nb):
        att_ref[order_ref[k]] = a_s[k * rb : (k + 1) * rb, :]


def attn_bwd_kernel(
    order_ref, slope_ref, segr_ref, segc_ref, q_ref, k_ref, v_ref, att_ref, grad_ref, lse_ref,
    out_ref, sum_ref, q_s, k_s, v_s, kt_s, a_s, g_s, dq_s, dk_s, dv_s, *, nb, rb,
):
    pair = pl.program_id(0)
    load_rows(order_ref, q_ref, q_s, nb, rb)
    load_rows(order_ref, k_ref, k_s, nb, rb)
    load_rows(order_ref, v_ref, v_s, nb, rb)
    load_rows(order_ref, att_ref, a_s, nb, rb)
    load_rows(order_ref, grad_ref, g_s, nb, rb)
    kt_s[...] = flip(k_s[...]).astype(BF)
    dk_s[...] = jnp.zeros(dk_s.shape, F32)
    dv_s[...] = jnp.zeros(dv_s.shape, F32)
    halves = half_masks((BLK, 2 * HD))
    q_sum = jnp.zeros((1, 2 * HD), F32)
    for b in range(L // BLK):
        r0 = b * BLK
        w0, w1, dist = distances(b, segr_ref, segc_ref)
        q_blk = q_s[r0 : r0 + BLK, :] * BF(HD ** (-0.5))
        g_blk = g_s[r0 : r0 + BLK, :]
        prod = (a_s[r0 : r0 + BLK, :].astype(F32) * g_blk.astype(F32)).T
        probs, grads, q_hs, g_hs, dq_t = [], [], [], [], []
        for h in range(2):
            q_h = jnp.where(halves[h], q_blk, BF(0))
            g_h = jnp.where(halves[h], g_blk, BF(0))
            s = trans_dot(k_s[w0:w1, :], q_h) - slope_ref[2 * pair + h] * dist
            p = jnp.exp(s - lse_ref[0, h : h + 1, r0 : r0 + BLK])
            delta = jnp.sum(prod[h * HD : (h + 1) * HD, :], axis=0, keepdims=True)
            dp = trans_dot(v_s[w0:w1, :], g_h)
            ds = (p * (dp - delta)).astype(BF)
            dq_t.append(dot(kt_s[h * HD : (h + 1) * HD, w0:w1], ds))
            probs.append(p.astype(BF))
            grads.append(ds)
            q_hs.append(q_h)
            g_hs.append(g_h)
        dv_s[w0:w1, :] += dot(jnp.concatenate(probs, axis=1), jnp.concatenate(g_hs, axis=0))
        dk_s[w0:w1, :] += dot(jnp.concatenate(grads, axis=1), jnp.concatenate(q_hs, axis=0))
        dq = jnp.concatenate(dq_t, axis=0).T * HD ** (-0.5)
        q_sum = q_sum + jnp.sum(dq, axis=0, keepdims=True)
        dq_s[r0 : r0 + BLK, :] = dq.astype(BF)
    sum_ref[0, 0:1, :] = q_sum
    sum_ref[0, 1:2, :] = jnp.sum(dv_s[...], axis=0, keepdims=True)
    for k in range(nb):
        rows = slice(k * rb, (k + 1) * rb)
        out_ref[order_ref[k], :, 0 : 2 * HD] = dq_s[rows, :]
        out_ref[order_ref[k], :, 2 * HD : 4 * HD] = dk_s[rows, :].astype(BF)
        out_ref[order_ref[k], :, 4 * HD : 6 * HD] = dv_s[rows, :].astype(BF)


def attn_specs(nb, rb):
    smem = pl.BlockSpec(memory_space=pltpu.SMEM)
    col = lambda which: pl.BlockSpec((nb, rb, 2 * HD), lambda p: (0, 0, 3 * p + which))
    base = [
        smem,
        smem,
        pl.BlockSpec((1, L), lambda p: (0, 0)),
        pl.BlockSpec((L, 1), lambda p: (0, 0)),
        col(0),
        col(1),
        col(2),
    ]
    one = pl.BlockSpec((nb, rb, 2 * HD), lambda p: (0, 0, p))
    lse = pl.BlockSpec((1, 2, L), lambda p: (p, 0, 0))
    return base, one, lse


def attn_fwd(order, slopes, segs, qkv):
    nb, rb, cols = qkv.shape
    pairs = cols // (6 * HD)
    base, one, lse = attn_specs(nb, rb)
    rows = lambda: pltpu.VMEM((L, 2 * HD), BF)
    return pl.pallas_call(
        lambda *refs: attn_fwd_kernel(*refs, nb=nb, rb=rb),
        grid=(pairs,),
        in_specs=base,
        out_specs=[one, lse],
        out_shape=[
            jax.ShapeDtypeStruct((nb, rb, pairs * 2 * HD), BF),
            jax.ShapeDtypeStruct((pairs, 2, L), F32),
        ],
        scratch_shapes=[rows(), rows(), rows(), pltpu.VMEM((2 * HD, L), BF), rows()],
        name="attn_fwd",
        cost_estimate=pl.CostEstimate(
            flops=pairs * 4 * L * L * HD * 4, transcendentals=pairs * L * L, bytes_accessed=1 << 24
        ),
    )(order, slopes, segs.reshape(1, L), segs.reshape(L, 1), qkv, qkv, qkv)


def attn_bwd(order, slopes, segs, qkv, att, att_grad, lse_rows):
    nb, rb, cols = qkv.shape
    pairs = cols // (6 * HD)
    base, one, lse = attn_specs(nb, rb)
    rows = lambda dt=BF: pltpu.VMEM((L, 2 * HD), dt)
    return pl.pallas_call(
        lambda *refs: attn_bwd_kernel(*refs, nb=nb, rb=rb),
        grid=(pairs,),
        in_specs=base + [one, one, lse],
        out_specs=[
            pl.BlockSpec((nb, rb, 6 * HD), lambda p: (0, 0, p)),
            pl.BlockSpec((1, 2, 2 * HD), lambda p: (p, 0, 0)),
        ],
        out_shape=[
            jax.ShapeDtypeStruct((nb, rb, cols), BF),
            jax.ShapeDtypeStruct((pairs, 2, 2 * HD), F32),
        ],
        scratch_shapes=[rows(), rows(), rows(), pltpu.VMEM((2 * HD, L), BF), rows(), rows(),
                        rows(), rows(F32), rows(F32)],
        name="attn_bwd",
        cost_estimate=pl.CostEstimate(
            flops=pairs * 8 * L * L * HD * 4, transcendentals=pairs * L * L, bytes_accessed=1 << 25
        ),
    )(order, slopes, segs.reshape(1, L), segs.reshape(L, 1), qkv, qkv, qkv, att, att_grad, lse_rows)


def gather_vectors(vecs, n_dev):
    flat = jnp.concatenate([v.reshape(-1) for v in vecs])
    spread = jnp.broadcast_to(flat[None, :], (n_dev, flat.shape[0]))
    got = lax.all_to_all(spread, ("dp", "mp"), 0, 0, tiled=True)
    full, at = [], 0
    for v in vecs:
        n = v.size
        part = got[:, at : at + n]
        if v.ndim == 2:
            part = part.reshape(n_dev, v.shape[0], v.shape[1]).transpose(1, 0, 2)
            full.append(part.reshape(v.shape[0], -1))
        else:
            full.append(part.reshape(-1))
        at += n
    return full


def cut_vectors(fulls, n_dev):
    parts, shapes = [], []
    for v in fulls:
        if v.ndim == 2:
            part = v.reshape(v.shape[0], n_dev, -1).transpose(1, 0, 2)
            shapes.append((v.shape[0], v.shape[1] // n_dev))
        else:
            part = v
            shapes.append((v.shape[0] // n_dev,))
        parts.append(part.reshape(n_dev, -1))
    return jnp.concatenate(parts, axis=1), shapes


def share_vectors(flat, shapes):
    outs, at = [], 0
    for shape in shapes:
        n = shape[0] * (shape[1] if len(shape) == 2 else 1)
        outs.append(flat[at : at + n].reshape(shape))
        at += n
    return outs


def scatter_vectors(fulls, n_dev):
    rows, shapes = cut_vectors(fulls, n_dev)
    got = lax.all_to_all(rows, ("dp", "mp"), 0, 0, tiled=True)
    return share_vectors(jnp.sum(got, axis=0), shapes)


def head_slopes(numbers):
    return jnp.exp2(-8.0 * (numbers + 1).astype(F32) / H)


def pair_columns(parts):
    stacked = jnp.stack([p.reshape(p.shape[:-1] + (-1, 2 * HD)) for p in parts], axis=-2)
    return stacked.reshape(stacked.shape[:-3] + (-1,))


def local_any(n_dp, n_mp):
    n_dev = n_dp * n_mp

    def scatter_rows(part):
        return lax.psum_scatter(part.astype(BF), "mp", scatter_dimension=0, tiled=True).astype(F32)

    def scatter_grad(part, dim):
        return lax.psum_scatter(part.astype(BF), "dp", scatter_dimension=dim, tiled=True).astype(F32)

    def local(block_in, out_grad, segment_ids, w_qkv, w_out, w_up, w_down, *vecs):
        model_index = lax.axis_index("mp")
        gain_one, shift_one, qv_all, out_shift, gain_two, shift_two, up_all, down_shift = (
            gather_vectors(vecs, n_dev)
        )
        qkv_full = lax.all_gather(w_qkv, "dp", axis=1, tiled=True)
        out_full = lax.all_gather(w_out, "dp", axis=1, tiled=True)
        up_full = lax.all_gather(w_up, "dp", axis=0, tiled=True)
        down_full = lax.all_gather(w_down, "dp", axis=1, tiled=True)
        head_cols = qkv_full.shape[2]
        hid_cols = up_full.shape[1]
        n_heads = head_cols // HD
        qv_shift = lax.dynamic_slice_in_dim(qv_all, model_index * head_cols, head_cols, 1)
        up_shift = lax.dynamic_slice_in_dim(up_all, model_index * hid_cols, hid_cols, 0)
        slopes = head_slopes(model_index * n_heads + jnp.arange(n_heads, dtype=jnp.int32))
        order = jnp.zeros((1,), jnp.int32)
        w_local = pair_columns([qkv_full[0], qkv_full[1], qkv_full[2]])
        b_local = pair_columns([qv_shift[0], jnp.zeros_like(qv_shift[0]), qv_shift[1]])
        hat_one, inv_one = norm_rows(block_in)
        normed_one = (hat_one * gain_one + shift_one).astype(BF)
        rows_one = lax.all_gather(normed_one, "mp", axis=0, tiled=True)
        qkv = (dot(rows_one, w_local) + b_local).astype(BF)[None]
        att, lse = attn_fwd(order, slopes, segment_ids, qkv)
        resid = block_in + scatter_rows(dot(att[0], out_full)) + out_shift
        hat_two, inv_two = norm_rows(resid)
        normed_two = (hat_two * gain_two + shift_two).astype(BF)
        rows_two = lax.all_gather(normed_two, "mp", axis=0, tiled=True)
        value, slope = gelu_both(dot(rows_two, up_full) + up_shift)
        hidden = value.astype(BF)
        block_out = resid + scatter_rows(dot(hidden, down_full)) + down_shift
        grad_rows = lax.all_gather(out_grad.astype(BF), "mp", axis=0, tiled=True)
        down_share = scatter_grad(cross_dot(hidden, grad_rows), 1)
        pre_grad = trans_dot(grad_rows, down_full) * slope
        pre_low = pre_grad.astype(BF)
        up_share = scatter_grad(cross_dot(rows_two, pre_low), 0)
        two_grad = scatter_rows(trans_dot(pre_low, up_full))
        resid_grad = out_grad + norm_back(two_grad, hat_two, inv_two, gain_two)
        resid_rows = lax.all_gather(resid_grad.astype(BF), "mp", axis=0, tiled=True)
        out_share = scatter_grad(cross_dot(att[0], resid_rows), 1)
        att_grad = trans_dot(resid_rows, out_full).astype(BF)[None]
        d_qkv, sums = attn_bwd(order, slopes, segment_ids, qkv, att, att_grad, lse)
        grad_w = cross_dot(rows_one, d_qkv[0])
        grad_w = grad_w.reshape(grad_w.shape[0], -1, 3, 2 * HD).transpose(2, 0, 1, 3)
        qkv_share = scatter_grad(grad_w.reshape(3, grad_w.shape[1], -1), 1)
        one_grad = scatter_rows(trans_dot(d_qkv[0], w_local))
        in_grad = resid_grad + norm_back(one_grad, hat_one, inv_one, gain_one)
        qv_place = lax.dynamic_update_slice_in_dim(
            jnp.zeros(qv_all.shape, F32),
            sums.transpose(1, 0, 2).reshape(2, -1),
            model_index * head_cols,
            1,
        )
        up_place = lax.dynamic_update_slice_in_dim(
            jnp.zeros(up_all.shape, F32), jnp.sum(pre_grad, axis=0), model_index * hid_cols, 0
        )
        shares = scatter_vectors(
            [
                jnp.sum(one_grad * hat_one, axis=0),
                jnp.sum(one_grad, axis=0),
                qv_place,
                jnp.sum(resid_grad, axis=0),
                jnp.sum(two_grad * hat_two, axis=0),
                jnp.sum(two_grad, axis=0),
                up_place,
                jnp.sum(out_grad, axis=0),
            ],
            n_dev,
        )
        return (block_out, in_grad, qkv_share, out_share, up_share, down_share, *shares)

    return local


CHUNK_OF_T = (0, 3, 1, 2)
T_OF_CHUNK = (0, 2, 3, 1)
PLANE_OF_T = (0, 3, 1, 2)
GROUPS = [[0, 1, 2, 3], [4, 5, 6, 7]]
TO_PLANE = [
    ((4 * y + t) * 4 + z, (4 * y + T_OF_CHUNK[z]) * 4 + PLANE_OF_T[t])
    for y in range(2)
    for t in range(4)
    for z in range(4)
]
FROM_PLANE = [(b, a) for a, b in TO_PLANE]


def swap(x, bits):
    return lax.ppermute(x, "dp", [(i, i ^ bits) for i in range(8)])


def relocate(x):
    return lax.ppermute(x, ("dp", "mp"), TO_PLANE)


def bring_back(x):
    return lax.ppermute(x, ("dp", "mp"), FROM_PLANE)


def gather_t(x, *fill):
    far = swap(x, 2)
    near = swap(x, 1)
    if fill:
        far, *fill = tie(far, *fill)
    rows = jnp.concatenate([x, near, far, swap(far, 1)], axis=0)
    return (rows, *fill) if fill else rows


def scatter_near(part):
    n = part.shape[0] // 4
    low = part.astype(BF)
    near = swap(jnp.concatenate([low[n : 2 * n], low[3 * n :]], axis=0), 1)
    far = (part[2 * n : 3 * n].astype(F32) + near[n:].astype(F32)).astype(BF)
    return part[:n], near[:n], far


def scatter_far(own, near, far):
    far = swap(far, 2)
    return own.astype(F32) + near.astype(F32) + far.astype(F32)


def scatter_t(part):
    return scatter_far(*scatter_near(part))


def exchange_t(x):
    return lax.all_to_all(x, "dp", 0, 0, tiled=True, axis_index_groups=GROUPS)


def exchange_swaps(x, t_index):
    got = [lax.dynamic_index_in_dim(x, t_index ^ j, 0, False) for j in range(4)]
    got = [got[0]] + [swap(got[j], j) for j in (1, 2, 3)]
    return jnp.stack(got)[jnp.arange(4, dtype=jnp.int32) ^ t_index]


def across(x, bits):
    return lax.ppermute(x, "mp", [(i, i ^ bits) for i in range(4)])


def gather_yz(x):
    mine = [x] + [across(x, k) for k in (1, 2, 3)]
    other = [swap(m, 4) for m in mine]
    return mine, other


def by_y(mine, other, y_index):
    mine, other = jnp.concatenate(mine, axis=1), jnp.concatenate(other, axis=1)
    first = jnp.where(y_index == 0, mine, other)
    second = jnp.where(y_index == 0, other, mine)
    return jnp.concatenate([first, second], axis=0)


def send_z(parts):
    return [parts[0]] + [across(parts[k], k) for k in (1, 2, 3)]


def total_z(parts):
    return sum(p.astype(F32) for p in parts).astype(BF)


def tie(*values):
    return lax.optimization_barrier(values)


def local_plane(block_in, out_grad, segment_ids, w_qkv, w_out, w_up, w_down, *vecs):
    n_dev = 32
    d_index = lax.axis_index("dp")
    t_index = d_index % 4
    y_index = d_index // 4
    width = block_in.shape[1]
    sub = width // 2
    rows_d = width // 8

    mean_one = jnp.mean(block_in, axis=-1, keepdims=True)
    center = block_in - mean_one
    inv_one = lax.rsqrt(jnp.mean(center * center, axis=-1, keepdims=True) + NORM_EPS)
    hat_low = relocate((center * inv_one).astype(BF))
    stats = relocate(jnp.concatenate([mean_one.reshape(1, -1), inv_one.reshape(1, -1)], axis=0))
    segs = relocate(segment_ids)

    heads = jnp.concatenate(
        [
            w_qkv.reshape(3, -1, 4, HD).transpose(2, 1, 0, 3).reshape(4, -1, 3 * HD),
            w_out.reshape(4, HD, -1).transpose(0, 2, 1),
        ],
        axis=2,
    )
    heads = lax.all_to_all(jnp.concatenate([heads, heads], axis=0), "dp", 0, 0, tiled=True)
    heads, *vecs = tie(heads, *vecs)
    gain_one, shift_one, qv_all, out_shift, gain_two, shift_two, up_all, down_shift = (
        gather_vectors(vecs, n_dev)
    )
    hat_low, stats, segs, gain_one = tie(hat_low, stats, segs, gain_one)
    hids = jnp.concatenate(
        [
            w_up.reshape(w_up.shape[0], 4, -1).transpose(1, 0, 2),
            w_down.reshape(4, -1, w_down.shape[1]).transpose(0, 2, 1),
        ],
        axis=2,
    )
    hids, shift_one = tie(hids, shift_one)
    hids = exchange_t(hids).reshape(sub, -1)
    mine, other = gather_yz(hids)
    heads = lax.all_gather(heads.reshape(width, 4 * HD), "mp", axis=0, tiled=False)
    heads = heads.reshape(2, 2, width, 4, HD).transpose(2, 0, 3, 1, 4)
    heads = heads.reshape(width, 2, 4, 2 * HD)
    w_local = heads[:, :, :3].reshape(width, -1)
    w_out_t = heads[:, :, 3].reshape(width, -1)
    units = hids.shape[1] // 2
    up_local = by_y([m[:, :units] for m in mine], [m[:, :units] for m in other], y_index)
    down_t = by_y([m[:, units:] for m in mine], [m[:, units:] for m in other], y_index)

    qv_mine = lax.dynamic_index_in_dim(qv_all.reshape(2, 4, 4, HD), t_index, 2, False)
    qv_mine = qv_mine.reshape(2, -1)
    b_local = pair_columns([qv_mine[0], jnp.zeros_like(qv_mine[0]), qv_mine[1]])
    up_shift = lax.dynamic_index_in_dim(up_all.reshape(4, 4, -1), t_index, 1, False)
    z_order = jnp.arange(4, dtype=jnp.int32) ^ lax.axis_index("mp")
    up_shift = up_shift[z_order].reshape(-1)
    slopes = head_slopes(4 * jnp.arange(4, dtype=jnp.int32) + t_index)
    chunk = jnp.asarray(CHUNK_OF_T, jnp.int32)[t_index]
    order = jnp.asarray(T_OF_CHUNK, jnp.int32)[jnp.arange(4, dtype=jnp.int32) ^ chunk]

    out_low, hat_low = tie(out_grad.astype(BF), hat_low)
    hat_one = hat_low.astype(F32)
    mean_here, inv_here = stats[0][:, None], stats[1][:, None]
    block_here = hat_one * (1.0 / inv_here) + mean_here
    rows_one = gather_t((hat_one * gain_one + shift_one).astype(BF))
    grad_low, rows_one = tie(relocate(out_low), rows_one)
    grad_rows = gather_t(grad_low)
    grad_here = grad_low.astype(F32)

    qkv = (dot(rows_one, w_local) + b_local).astype(BF).reshape(4, -1, w_local.shape[1])
    att, lse = attn_fwd(order, slopes, segs, qkv)
    att, grad_rows = tie(att, grad_rows)
    att_rows = att.reshape(-1, att.shape[2])
    resid = block_here + scatter_t(trans_dot(att_rows, w_out_t)) + out_shift
    hat_two, inv_two = norm_rows(resid)
    rows_two = gather_t((hat_two * gain_two + shift_two).astype(BF))
    value, slope = gelu_both(dot(rows_two, up_local) + up_shift)
    hidden = value.astype(BF)
    g_down = cross_dot(grad_rows, hidden).astype(BF)
    pre_grad = dot(grad_rows, down_t) * slope
    pre_low = pre_grad.astype(BF)
    two_part = trans_dot(pre_low, up_local).astype(BF)
    own, near, far = scatter_near(two_part)

    far, pre_low = tie(far, pre_low)
    g_up = cross_dot(rows_two, pre_low).astype(BF)

    def to_y(grad):
        halves = grad[:sub], grad[sub:]
        keep = jnp.where(y_index == 0, *halves)
        send = jnp.where(y_index == 0, halves[1], halves[0])
        return keep, swap(send, 4)

    def to_z(keep, got):
        both = (keep.astype(F32) + got.astype(F32)).astype(BF)
        return send_z([both[:, k * units : (k + 1) * units] for k in range(4)])

    down_keep, down_got = to_y(g_down)
    up_keep, up_got = to_y(g_up)
    two_grad, up_keep = tie(scatter_far(own, near, far), up_keep)

    resid_grad = grad_here + norm_back(two_grad, hat_two, inv_two, gain_two)
    resid_low = resid_grad.astype(BF)
    resid_low, hidden = tie(resid_low, hidden)
    down_part = trans_dot(hidden, down_t).astype(BF)
    resid_rows, down_part = gather_t(resid_low, down_part)
    resid_rows, down_got = tie(resid_rows, down_got)
    down_parts = to_z(down_keep, down_got)
    block_sum = scatter_t(down_part)
    block_low = (resid + block_sum + down_shift).astype(BF)

    att_grad = dot(resid_rows, w_out_t).astype(BF).reshape(att.shape)
    d_qkv, sums = attn_bwd(order, slopes, segs, qkv, att, att_grad, lse)
    d_rows = d_qkv.reshape(-1, d_qkv.shape[2])
    one_part = trans_dot(d_rows, w_local).astype(BF)
    one_part, d_rows, block_low = tie(one_part, d_rows, block_low)
    own, near, far = scatter_near(one_part)
    far, up_got = tie(far, up_got)
    up_parts = to_z(up_keep, up_got)

    block_back = bring_back(block_low)
    g_qkv = cross_dot(rows_one, d_rows).astype(BF)
    g_qkv = g_qkv.reshape(2, 4, rows_d, 2, 3, 2, HD)
    g_out = cross_dot(resid_rows, att_rows).astype(BF).reshape(2, 4, rows_d, 2, 1, 2, HD)
    g_head = jnp.concatenate([g_qkv, g_out], axis=4).transpose(0, 1, 3, 5, 2, 4, 6)
    g_head = g_head.reshape(n_dev, rows_d, 4 * HD)
    one_grad = scatter_far(own, near, far)
    one_grad, block_back, *down_parts = tie(one_grad, block_back, *down_parts)
    in_grad = resid_grad + norm_back(one_grad, hat_one, inv_here, gain_one)
    in_back = bring_back(in_grad.astype(BF))
    in_back, *parts = tie(in_back, *up_parts, *down_parts)
    g_hid = jnp.concatenate([total_z(parts[:4]), total_z(parts[4:])], axis=1)
    g_hid = exchange_swaps(g_hid.reshape(4, rows_d, 2 * units), t_index).astype(F32)

    mine = jnp.arange(4, dtype=jnp.int32) == t_index
    qv_part = sums.transpose(1, 0, 2).reshape(2, 4, 1, HD)
    qv_place = jnp.where(mine[None, None, :, None], qv_part, 0.0).reshape(2, width)
    up_part = jnp.sum(pre_grad, axis=0).reshape(4, units)[z_order][:, None, :]
    up_place = jnp.where(mine[None, :, None], up_part, 0.0).reshape(-1)
    sums = [
        jnp.sum(one_grad * hat_one, axis=0),
        jnp.sum(one_grad, axis=0),
        qv_place,
        jnp.sum(resid_grad, axis=0),
        jnp.sum(two_grad * hat_two, axis=0),
        jnp.sum(two_grad, axis=0),
        up_place,
        jnp.sum(out_grad, axis=0),
    ]
    rows, shapes = cut_vectors(sums, n_dev)
    rows_hi = rows.astype(BF)
    rows_lo = (rows - rows_hi.astype(F32)).astype(BF)
    n_vec = rows.shape[1]
    rows = jnp.concatenate([rows_hi, rows_lo], axis=1)
    rows = jnp.pad(rows, ((0, 0), (0, 16 * 4 * HD - 2 * n_vec))).reshape(n_dev, 16, 4 * HD)
    g_head = lax.all_to_all(jnp.concatenate([g_head, rows], axis=1), ("dp", "mp"), 0, 0, tiled=True)
    flat = jnp.sum(g_head[:, rows_d:].reshape(n_dev, -1)[:, : 2 * n_vec].astype(F32), axis=0)
    shares = share_vectors(flat[:n_vec] + flat[n_vec:], shapes)
    g_head = g_head[:, :rows_d]
    g_head = jnp.sum(g_head.reshape(2, 4, 4, rows_d, 4, HD).astype(F32), axis=(0, 2))
    qkv_share = g_head[:, :, :3].transpose(2, 1, 0, 3).reshape(w_qkv.shape)
    out_share = g_head[:, :, 3].transpose(0, 2, 1).reshape(w_out.shape)

    up_share = g_hid[..., :units].transpose(1, 0, 2).reshape(w_up.shape)
    down_share = g_hid[..., units:].transpose(0, 2, 1).reshape(w_down.shape)

    block_out = block_back.astype(F32)
    return (block_out, in_back.astype(F32), qkv_share, out_share, up_share, down_share, *shares)


def solution(mesh):
    n_dp, n_mp = mesh.shape["dp"], mesh.shape["mp"]
    plane = (n_dp, n_mp) == (8, 4)
    local = local_plane if plane else local_any(n_dp, n_mp)
    both = ("dp", "mp")
    weights = (P(None, "dp", "mp"), P("mp", "dp"), P("dp", "mp"), P("mp", "dp"))
    vectors = (P(both), P(both), P(None, both), P(both), P(both), P(both), P(both), P(both))
    return jax.shard_map(
        local,
        mesh=mesh,
        in_specs=(P(both, None), P(both, None), P("dp"), *weights, *vectors),
        out_specs=(P(both, None), P(both, None), *weights, *vectors),
        check_vma=False,
    )
```

```python
import jax
import jax.numpy as jnp
from jax import lax
from jax.experimental import pallas as pl
from jax.experimental.pallas import tpu as pltpu
from jax.sharding import PartitionSpec as P


H = 16
HD = 64
L = 1152
BLK = 128
REACH = 5

NORM_EPS = 1e-05
GELU_SCALE = 0.7978845608028654
GELU_CUBE = 0.044715

BF = jnp.bfloat16
F32 = jnp.float32


def gelu_both(pre_act):
    inner = jnp.tanh(GELU_SCALE * (pre_act + GELU_CUBE * pre_act * pre_act * pre_act))
    value = 0.5 * pre_act * (1.0 + inner)
    slope = 0.5 * (1.0 + inner) + 0.5 * pre_act * (1.0 - inner * inner) * GELU_SCALE * (
        1.0 + 3.0 * GELU_CUBE * pre_act * pre_act
    )
    return value, slope


def norm_rows(inputs):
    center = inputs - jnp.mean(inputs, axis=-1, keepdims=True)
    scale_inv = lax.rsqrt(jnp.mean(center * center, axis=-1, keepdims=True) + NORM_EPS)
    return (center * scale_inv, scale_inv)


def norm_back(norm_grad, x_hat, scale_inv, gain):
    scaled = norm_grad * gain
    return scale_inv * (
        scaled
        - jnp.mean(scaled, axis=-1, keepdims=True)
        - x_hat * jnp.mean(scaled * x_hat, axis=-1, keepdims=True)
    )


def dot(left, right):
    return jnp.dot(left, right, preferred_element_type=F32)


def cross_dot(left, right):
    return lax.dot_general(left, right, (((0,), (0,)), ((), ())), preferred_element_type=F32)


def trans_dot(left, right):
    return lax.dot_general(left, right, (((1,), (1,)), ((), ())), preferred_element_type=F32)


def flip(x):
    return x.astype(F32).T


def load_rows(order_ref, src_ref, dst_ref, nb, rb):
    for k in range(nb):
        dst_ref[k * rb : (k + 1) * rb, :] = src_ref[order_ref[k]]


def half_masks(shape):
    lane = lax.broadcasted_iota(jnp.int32, shape, 1)
    return (lane < HD, lane >= HD)


def distances(b, segr_ref, segc_ref):
    w0 = max(0, b - REACH) * BLK
    w1 = (b + 1) * BLK
    keys = w0 + lax.broadcasted_iota(jnp.int32, (w1 - w0, BLK), 0)
    rows = b * BLK + lax.broadcasted_iota(jnp.int32, (w1 - w0, BLK), 1)
    same = segc_ref[w0:w1, :] == segr_ref[:, b * BLK : (b + 1) * BLK]
    gap = rows - keys
    dist = jnp.where(same & (gap >= 0), gap.astype(F32), 1e30)
    return w0, w1, dist


def attn_fwd_kernel(
    order_ref, slope_ref, segr_ref, segc_ref, q_ref, k_ref, v_ref, att_ref, lse_ref,
    q_s, k_s, v_s, vt_s, a_s, *, nb, rb,
):
    pair = pl.program_id(0)
    load_rows(order_ref, q_ref, q_s, nb, rb)
    load_rows(order_ref, k_ref, k_s, nb, rb)
    load_rows(order_ref, v_ref, v_s, nb, rb)
    vt_s[...] = flip(v_s[...]).astype(BF)
    halves = half_masks((BLK, 2 * HD))
    for b in range(L // BLK):
        r0 = b * BLK
        w0, w1, dist = distances(b, segr_ref, segc_ref)
        q_blk = q_s[r0 : r0 + BLK, :] * BF(HD ** (-0.5))
        outs = []
        for h in range(2):
            q_h = jnp.where(halves[h], q_blk, BF(0))
            s = trans_dot(k_s[w0:w1, :], q_h) - slope_ref[2 * pair + h] * dist
            top = jnp.max(s, axis=0, keepdims=True)
            e = jnp.exp(s - top)
            total = jnp.sum(e, axis=0, keepdims=True)
            lse_ref[0, h : h + 1, r0 : r0 + BLK] = top + jnp.log(total)
            prob = (e * (1.0 / total)).astype(BF)
            outs.append(dot(vt_s[h * HD : (h + 1) * HD, w0:w1], prob))
        a_s[r0 : r0 + BLK, :] = jnp.concatenate(outs, axis=0).T.astype(BF)
    for k in range(nb):
        att_ref[order_ref[k]] = a_s[k * rb : (k + 1) * rb, :]


def attn_bwd_kernel(
    order_ref, slope_ref, segr_ref, segc_ref, q_ref, k_ref, v_ref, att_ref, grad_ref, lse_ref,
    out_ref, sum_ref, q_s, k_s, v_s, kt_s, a_s, g_s, dq_s, dk_s, dv_s, *, nb, rb,
):
    pair = pl.program_id(0)
    load_rows(order_ref, q_ref, q_s, nb, rb)
    load_rows(order_ref, k_ref, k_s, nb, rb)
    load_rows(order_ref, v_ref, v_s, nb, rb)
    load_rows(order_ref, att_ref, a_s, nb, rb)
    load_rows(order_ref, grad_ref, g_s, nb, rb)
    kt_s[...] = flip(k_s[...]).astype(BF)
    dk_s[...] = jnp.zeros(dk_s.shape, F32)
    dv_s[...] = jnp.zeros(dv_s.shape, F32)
    halves = half_masks((BLK, 2 * HD))
    q_sum = jnp.zeros((1, 2 * HD), F32)
    for b in range(L // BLK):
        r0 = b * BLK
        w0, w1, dist = distances(b, segr_ref, segc_ref)
        q_blk = q_s[r0 : r0 + BLK, :] * BF(HD ** (-0.5))
        g_blk = g_s[r0 : r0 + BLK, :]
        prod = (a_s[r0 : r0 + BLK, :].astype(F32) * g_blk.astype(F32)).T
        probs, grads, q_hs, g_hs, dq_t = [], [], [], [], []
        for h in range(2):
            q_h = jnp.where(halves[h], q_blk, BF(0))
            g_h = jnp.where(halves[h], g_blk, BF(0))
            s = trans_dot(k_s[w0:w1, :], q_h) - slope_ref[2 * pair + h] * dist
            p = jnp.exp(s - lse_ref[0, h : h + 1, r0 : r0 + BLK])
            delta = jnp.sum(prod[h * HD : (h + 1) * HD, :], axis=0, keepdims=True)
            dp = trans_dot(v_s[w0:w1, :], g_h)
            ds = (p * (dp - delta)).astype(BF)
            dq_t.append(dot(kt_s[h * HD : (h + 1) * HD, w0:w1], ds))
            probs.append(p.astype(BF))
            grads.append(ds)
            q_hs.append(q_h)
            g_hs.append(g_h)
        dv_s[w0:w1, :] += dot(jnp.concatenate(probs, axis=1), jnp.concatenate(g_hs, axis=0))
        dk_s[w0:w1, :] += dot(jnp.concatenate(grads, axis=1), jnp.concatenate(q_hs, axis=0))
        dq = jnp.concatenate(dq_t, axis=0).T * HD ** (-0.5)
        q_sum = q_sum + jnp.sum(dq, axis=0, keepdims=True)
        dq_s[r0 : r0 + BLK, :] = dq.astype(BF)
    sum_ref[0, 0:1, :] = q_sum
    sum_ref[0, 1:2, :] = jnp.sum(dv_s[...], axis=0, keepdims=True)
    for k in range(nb):
        rows = slice(k * rb, (k + 1) * rb)
        out_ref[order_ref[k], :, 0 : 2 * HD] = dq_s[rows, :]
        out_ref[order_ref[k], :, 2 * HD : 4 * HD] = dk_s[rows, :].astype(BF)
        out_ref[order_ref[k], :, 4 * HD : 6 * HD] = dv_s[rows, :].astype(BF)


def attn_specs(nb, rb):
    smem = pl.BlockSpec(memory_space=pltpu.SMEM)
    col = lambda which: pl.BlockSpec((nb, rb, 2 * HD), lambda p: (0, 0, 3 * p + which))
    base = [
        smem,
        smem,
        pl.BlockSpec((1, L), lambda p: (0, 0)),
        pl.BlockSpec((L, 1), lambda p: (0, 0)),
        col(0),
        col(1),
        col(2),
    ]
    one = pl.BlockSpec((nb, rb, 2 * HD), lambda p: (0, 0, p))
    lse = pl.BlockSpec((1, 2, L), lambda p: (p, 0, 0))
    return base, one, lse


def attn_fwd(order, slopes, segs, qkv):
    nb, rb, cols = qkv.shape
    pairs = cols // (6 * HD)
    base, one, lse = attn_specs(nb, rb)
    rows = lambda: pltpu.VMEM((L, 2 * HD), BF)
    return pl.pallas_call(
        lambda *refs: attn_fwd_kernel(*refs, nb=nb, rb=rb),
        grid=(pairs,),
        in_specs=base,
        out_specs=[one, lse],
        out_shape=[
            jax.ShapeDtypeStruct((nb, rb, pairs * 2 * HD), BF),
            jax.ShapeDtypeStruct((pairs, 2, L), F32),
        ],
        scratch_shapes=[rows(), rows(), rows(), pltpu.VMEM((2 * HD, L), BF), rows()],
        name="attn_fwd",
        cost_estimate=pl.CostEstimate(
            flops=pairs * 4 * L * L * HD * 4, transcendentals=pairs * L * L, bytes_accessed=1 << 24
        ),
    )(order, slopes, segs.reshape(1, L), segs.reshape(L, 1), qkv, qkv, qkv)


def attn_bwd(order, slopes, segs, qkv, att, att_grad, lse_rows):
    nb, rb, cols = qkv.shape
    pairs = cols // (6 * HD)
    base, one, lse = attn_specs(nb, rb)
    rows = lambda dt=BF: pltpu.VMEM((L, 2 * HD), dt)
    return pl.pallas_call(
        lambda *refs: attn_bwd_kernel(*refs, nb=nb, rb=rb),
        grid=(pairs,),
        in_specs=base + [one, one, lse],
        out_specs=[
            pl.BlockSpec((nb, rb, 6 * HD), lambda p: (0, 0, p)),
            pl.BlockSpec((1, 2, 2 * HD), lambda p: (p, 0, 0)),
        ],
        out_shape=[
            jax.ShapeDtypeStruct((nb, rb, cols), BF),
            jax.ShapeDtypeStruct((pairs, 2, 2 * HD), F32),
        ],
        scratch_shapes=[rows(), rows(), rows(), pltpu.VMEM((2 * HD, L), BF), rows(), rows(),
                        rows(), rows(F32), rows(F32)],
        name="attn_bwd",
        cost_estimate=pl.CostEstimate(
            flops=pairs * 8 * L * L * HD * 4, transcendentals=pairs * L * L, bytes_accessed=1 << 25
        ),
    )(order, slopes, segs.reshape(1, L), segs.reshape(L, 1), qkv, qkv, qkv, att, att_grad, lse_rows)


def gather_vectors(vecs, n_dev):
    flat = jnp.concatenate([v.reshape(-1) for v in vecs])
    spread = jnp.broadcast_to(flat[None, :], (n_dev, flat.shape[0]))
    got = lax.all_to_all(spread, ("dp", "mp"), 0, 0, tiled=True)
    full, at = [], 0
    for v in vecs:
        n = v.size
        part = got[:, at : at + n]
        if v.ndim == 2:
            part = part.reshape(n_dev, v.shape[0], v.shape[1]).transpose(1, 0, 2)
            full.append(part.reshape(v.shape[0], -1))
        else:
            full.append(part.reshape(-1))
        at += n
    return full


def cut_vectors(fulls, n_dev):
    parts, shapes = [], []
    for v in fulls:
        if v.ndim == 2:
            part = v.reshape(v.shape[0], n_dev, -1).transpose(1, 0, 2)
            shapes.append((v.shape[0], v.shape[1] // n_dev))
        else:
            part = v
            shapes.append((v.shape[0] // n_dev,))
        parts.append(part.reshape(n_dev, -1))
    return jnp.concatenate(parts, axis=1), shapes


def share_vectors(flat, shapes):
    outs, at = [], 0
    for shape in shapes:
        n = shape[0] * (shape[1] if len(shape) == 2 else 1)
        outs.append(flat[at : at + n].reshape(shape))
        at += n
    return outs


def scatter_vectors(fulls, n_dev):
    rows, shapes = cut_vectors(fulls, n_dev)
    got = lax.all_to_all(rows, ("dp", "mp"), 0, 0, tiled=True)
    return share_vectors(jnp.sum(got, axis=0), shapes)


def head_slopes(numbers):
    return jnp.exp2(-8.0 * (numbers + 1).astype(F32) / H)


def pair_columns(parts):
    stacked = jnp.stack([p.reshape(p.shape[:-1] + (-1, 2 * HD)) for p in parts], axis=-2)
    return stacked.reshape(stacked.shape[:-3] + (-1,))


def local_any(n_dp, n_mp):
    n_dev = n_dp * n_mp

    def scatter_rows(part):
        return lax.psum_scatter(part.astype(BF), "mp", scatter_dimension=0, tiled=True).astype(F32)

    def scatter_grad(part, dim):
        return lax.psum_scatter(part.astype(BF), "dp", scatter_dimension=dim, tiled=True).astype(F32)

    def local(block_in, out_grad, segment_ids, w_qkv, w_out, w_up, w_down, *vecs):
        model_index = lax.axis_index("mp")
        gain_one, shift_one, qv_all, out_shift, gain_two, shift_two, up_all, down_shift = (
            gather_vectors(vecs, n_dev)
        )
        qkv_full = lax.all_gather(w_qkv, "dp", axis=1, tiled=True)
        out_full = lax.all_gather(w_out, "dp", axis=1, tiled=True)
        up_full = lax.all_gather(w_up, "dp", axis=0, tiled=True)
        down_full = lax.all_gather(w_down, "dp", axis=1, tiled=True)
        head_cols = qkv_full.shape[2]
        hid_cols = up_full.shape[1]
        n_heads = head_cols // HD
        qv_shift = lax.dynamic_slice_in_dim(qv_all, model_index * head_cols, head_cols, 1)
        up_shift = lax.dynamic_slice_in_dim(up_all, model_index * hid_cols, hid_cols, 0)
        slopes = head_slopes(model_index * n_heads + jnp.arange(n_heads, dtype=jnp.int32))
        order = jnp.zeros((1,), jnp.int32)
        w_local = pair_columns([qkv_full[0], qkv_full[1], qkv_full[2]])
        b_local = pair_columns([qv_shift[0], jnp.zeros_like(qv_shift[0]), qv_shift[1]])
        hat_one, inv_one = norm_rows(block_in)
        normed_one = (hat_one * gain_one + shift_one).astype(BF)
        rows_one = lax.all_gather(normed_one, "mp", axis=0, tiled=True)
        qkv = (dot(rows_one, w_local) + b_local).astype(BF)[None]
        att, lse = attn_fwd(order, slopes, segment_ids, qkv)
        resid = block_in + scatter_rows(dot(att[0], out_full)) + out_shift
        hat_two, inv_two = norm_rows(resid)
        normed_two = (hat_two * gain_two + shift_two).astype(BF)
        rows_two = lax.all_gather(normed_two, "mp", axis=0, tiled=True)
        value, slope = gelu_both(dot(rows_two, up_full) + up_shift)
        hidden = value.astype(BF)
        block_out = resid + scatter_rows(dot(hidden, down_full)) + down_shift
        grad_rows = lax.all_gather(out_grad.astype(BF), "mp", axis=0, tiled=True)
        down_share = scatter_grad(cross_dot(hidden, grad_rows), 1)
        pre_grad = trans_dot(grad_rows, down_full) * slope
        pre_low = pre_grad.astype(BF)
        up_share = scatter_grad(cross_dot(rows_two, pre_low), 0)
        two_grad = scatter_rows(trans_dot(pre_low, up_full))
        resid_grad = out_grad + norm_back(two_grad, hat_two, inv_two, gain_two)
        resid_rows = lax.all_gather(resid_grad.astype(BF), "mp", axis=0, tiled=True)
        out_share = scatter_grad(cross_dot(att[0], resid_rows), 1)
        att_grad = trans_dot(resid_rows, out_full).astype(BF)[None]
        d_qkv, sums = attn_bwd(order, slopes, segment_ids, qkv, att, att_grad, lse)
        grad_w = cross_dot(rows_one, d_qkv[0])
        grad_w = grad_w.reshape(grad_w.shape[0], -1, 3, 2 * HD).transpose(2, 0, 1, 3)
        qkv_share = scatter_grad(grad_w.reshape(3, grad_w.shape[1], -1), 1)
        one_grad = scatter_rows(trans_dot(d_qkv[0], w_local))
        in_grad = resid_grad + norm_back(one_grad, hat_one, inv_one, gain_one)
        qv_place = lax.dynamic_update_slice_in_dim(
            jnp.zeros(qv_all.shape, F32),
            sums.transpose(1, 0, 2).reshape(2, -1),
            model_index * head_cols,
            1,
        )
        up_place = lax.dynamic_update_slice_in_dim(
            jnp.zeros(up_all.shape, F32), jnp.sum(pre_grad, axis=0), model_index * hid_cols, 0
        )
        shares = scatter_vectors(
            [
                jnp.sum(one_grad * hat_one, axis=0),
                jnp.sum(one_grad, axis=0),
                qv_place,
                jnp.sum(resid_grad, axis=0),
                jnp.sum(two_grad * hat_two, axis=0),
                jnp.sum(two_grad, axis=0),
                up_place,
                jnp.sum(out_grad, axis=0),
            ],
            n_dev,
        )
        return (block_out, in_grad, qkv_share, out_share, up_share, down_share, *shares)

    return local


CHUNK_OF_T = (0, 3, 1, 2)
T_OF_CHUNK = (0, 2, 3, 1)
PLANE_OF_T = (0, 3, 1, 2)
GROUPS = [[0, 1, 2, 3], [4, 5, 6, 7]]
TO_PLANE = [
    ((4 * y + t) * 4 + z, (4 * y + T_OF_CHUNK[z]) * 4 + PLANE_OF_T[t])
    for y in range(2)
    for t in range(4)
    for z in range(4)
]
FROM_PLANE = [(b, a) for a, b in TO_PLANE]


def swap(x, bits):
    return lax.ppermute(x, "dp", [(i, i ^ bits) for i in range(8)])


def relocate(x):
    return lax.ppermute(x, ("dp", "mp"), TO_PLANE)


def bring_back(x):
    return lax.ppermute(x, ("dp", "mp"), FROM_PLANE)


def gather_t(x, *fill):
    far = swap(x, 2)
    near = swap(x, 1)
    if fill:
        far, *fill = tie(far, *fill)
    rows = jnp.concatenate([x, near, far, swap(far, 1)], axis=0)
    return (rows, *fill) if fill else rows


def scatter_near(part):
    n = part.shape[0] // 4
    low = part.astype(BF)
    near = swap(jnp.concatenate([low[n : 2 * n], low[3 * n :]], axis=0), 1)
    far = (part[2 * n : 3 * n].astype(F32) + near[n:].astype(F32)).astype(BF)
    return part[:n], near[:n], far


def scatter_far(own, near, far):
    far = swap(far, 2)
    return own.astype(F32) + near.astype(F32) + far.astype(F32)


def scatter_t(part):
    return scatter_far(*scatter_near(part))


def exchange_t(x):
    return lax.all_to_all(x, "dp", 0, 0, tiled=True, axis_index_groups=GROUPS)


def exchange_swaps(x, t_index):
    got = [lax.dynamic_index_in_dim(x, t_index ^ j, 0, False) for j in range(4)]
    got = [got[0]] + [swap(got[j], j) for j in (1, 2, 3)]
    return jnp.stack(got)[jnp.arange(4, dtype=jnp.int32) ^ t_index]


def halve_sums(rows, d_index):
    rows = rows.reshape(2, 2, 2, 2, 2, -1)
    z_index = lax.axis_index("mp")
    bits = (d_index & 1, (d_index >> 1) & 1, d_index >> 2, z_index & 1, z_index >> 1)
    moves = (lambda v: swap(v, 1), lambda v: swap(v, 2), lambda v: swap(v, 4),
             lambda v: across(v, 1), lambda v: across(v, 2))
    for axis, bit, move in zip((2, 1, 0, 1, 0), bits, moves):
        keep = lax.dynamic_index_in_dim(rows, bit, axis, False)
        rows = keep + move(lax.dynamic_index_in_dim(rows, 1 - bit, axis, False))
    return rows


def across(x, bits):
    return lax.ppermute(x, "mp", [(i, i ^ bits) for i in range(4)])


def gather_yz(x):
    mine = [x] + [across(x, k) for k in (1, 2, 3)]
    other = [swap(m, 4) for m in mine]
    return mine, other


def by_y(mine, other, y_index):
    mine, other = jnp.concatenate(mine, axis=1), jnp.concatenate(other, axis=1)
    first = jnp.where(y_index == 0, mine, other)
    second = jnp.where(y_index == 0, other, mine)
    return jnp.concatenate([first, second], axis=0)


def send_z(parts):
    return [parts[0]] + [across(parts[k], k) for k in (1, 2, 3)]


def total_z(parts):
    return sum(p.astype(F32) for p in parts).astype(BF)


def tie(*values):
    return lax.optimization_barrier(values)


def local_plane(block_in, out_grad, segment_ids, w_qkv, w_out, w_up, w_down, *vecs):
    n_dev = 32
    d_index = lax.axis_index("dp")
    t_index = d_index % 4
    y_index = d_index // 4
    width = block_in.shape[1]
    sub = width // 2
    rows_d = width // 8

    mean_one = jnp.mean(block_in, axis=-1, keepdims=True)
    center = block_in - mean_one
    inv_one = lax.rsqrt(jnp.mean(center * center, axis=-1, keepdims=True) + NORM_EPS)
    hat_low = relocate((center * inv_one).astype(BF))
    stats = relocate(jnp.concatenate([mean_one.reshape(1, -1), inv_one.reshape(1, -1)], axis=0))
    segs = relocate(segment_ids)

    heads = jnp.concatenate(
        [
            w_qkv.reshape(3, -1, 4, HD).transpose(2, 1, 0, 3).reshape(4, -1, 3 * HD),
            w_out.reshape(4, HD, -1).transpose(0, 2, 1),
        ],
        axis=2,
    )
    heads = lax.all_to_all(jnp.concatenate([heads, heads], axis=0), "dp", 0, 0, tiled=True)
    heads, *vecs = tie(heads, *vecs)
    gain_one, shift_one, qv_all, out_shift, gain_two, shift_two, up_all, down_shift = (
        gather_vectors(vecs, n_dev)
    )
    hat_low, stats, segs, gain_one = tie(hat_low, stats, segs, gain_one)
    hids = jnp.concatenate(
        [
            w_up.reshape(w_up.shape[0], 4, -1).transpose(1, 0, 2),
            w_down.reshape(4, -1, w_down.shape[1]).transpose(0, 2, 1),
        ],
        axis=2,
    )
    hids, shift_one = tie(hids, shift_one)
    hids = exchange_t(hids).reshape(sub, -1)
    out_low, hat_low = tie(out_grad.astype(BF), hat_low)
    grad_low = relocate(out_low)
    hids, grad_low = tie(hids, grad_low)
    mine, other = gather_yz(hids)
    heads = lax.all_gather(heads.reshape(width, 4 * HD), "mp", axis=0, tiled=False)
    heads = heads.reshape(2, 2, width, 4, HD).transpose(2, 0, 3, 1, 4)
    heads = heads.reshape(width, 2, 4, 2 * HD)
    w_local = heads[:, :, :3].reshape(width, -1)
    w_out_t = heads[:, :, 3].reshape(width, -1)
    units = hids.shape[1] // 2
    up_local = by_y([m[:, :units] for m in mine], [m[:, :units] for m in other], y_index)
    down_t = by_y([m[:, units:] for m in mine], [m[:, units:] for m in other], y_index)

    qv_mine = lax.dynamic_index_in_dim(qv_all.reshape(2, 4, 4, HD), t_index, 2, False)
    qv_mine = qv_mine.reshape(2, -1)
    b_local = pair_columns([qv_mine[0], jnp.zeros_like(qv_mine[0]), qv_mine[1]])
    up_shift = lax.dynamic_index_in_dim(up_all.reshape(4, 4, -1), t_index, 1, False)
    z_order = jnp.arange(4, dtype=jnp.int32) ^ lax.axis_index("mp")
    up_shift = up_shift[z_order].reshape(-1)
    slopes = head_slopes(4 * jnp.arange(4, dtype=jnp.int32) + t_index)
    chunk = jnp.asarray(CHUNK_OF_T, jnp.int32)[t_index]
    order = jnp.asarray(T_OF_CHUNK, jnp.int32)[jnp.arange(4, dtype=jnp.int32) ^ chunk]

    hat_one = hat_low.astype(F32)
    mean_here, inv_here = stats[0][:, None], stats[1][:, None]
    block_here = hat_one * (1.0 / inv_here) + mean_here
    rows_one = gather_t((hat_one * gain_one + shift_one).astype(BF))
    grad_low, rows_one = tie(grad_low, rows_one)
    grad_rows = gather_t(grad_low)
    grad_here = grad_low.astype(F32)

    qkv = (dot(rows_one, w_local) + b_local).astype(BF).reshape(4, -1, w_local.shape[1])
    att, lse = attn_fwd(order, slopes, segs, qkv)
    att, grad_rows = tie(att, grad_rows)
    att_rows = att.reshape(-1, att.shape[2])
    att_part = trans_dot(att_rows, w_out_t).astype(BF)
    resid = block_here + scatter_t(att_part) + out_shift
    hat_two, inv_two = norm_rows(resid)
    rows_two = gather_t((hat_two * gain_two + shift_two).astype(BF))
    value, slope = gelu_both(dot(rows_two, up_local) + up_shift)
    hidden = value.astype(BF)
    down_part = trans_dot(hidden, down_t).astype(BF)
    own_d, near_d, far_d = scatter_near(down_part)
    hidden, own_d = tie(hidden, own_d)
    g_down = cross_dot(grad_rows, hidden).astype(BF)
    far_d, g_down, grad_rows = tie(far_d, g_down, grad_rows)
    block_sum = scatter_far(own_d, near_d, far_d)
    pre_grad = dot(grad_rows, down_t) * slope
    pre_low = pre_grad.astype(BF)
    two_part = trans_dot(pre_low, up_local).astype(BF)
    own, near, far = scatter_near(two_part)

    far, pre_low = tie(far, pre_low)
    g_up = cross_dot(rows_two, pre_low).astype(BF)
    block_low = (resid + block_sum + down_shift).astype(BF)

    def to_y(grad):
        halves = grad[:sub], grad[sub:]
        keep = jnp.where(y_index == 0, *halves)
        send = jnp.where(y_index == 0, halves[1], halves[0])
        return keep, swap(send, 4)

    def to_z(keep, got):
        both = (keep.astype(F32) + got.astype(F32)).astype(BF)
        return send_z([both[:, k * units : (k + 1) * units] for k in range(4)])

    down_keep, down_got = to_y(g_down)
    up_keep, up_got = to_y(g_up)
    two_grad, up_keep, block_low = tie(scatter_far(own, near, far), up_keep, block_low)
    block_back = bring_back(block_low)

    resid_grad = grad_here + norm_back(two_grad, hat_two, inv_two, gain_two)
    resid_low = resid_grad.astype(BF)
    resid_rows = gather_t(resid_low)
    resid_rows, down_got = tie(resid_rows, down_got)
    down_parts = to_z(down_keep, down_got)

    att_grad = dot(resid_rows, w_out_t).astype(BF).reshape(att.shape)
    d_qkv, sums = attn_bwd(order, slopes, segs, qkv, att, att_grad, lse)
    d_rows = d_qkv.reshape(-1, d_qkv.shape[2])
    one_part = trans_dot(d_rows, w_local).astype(BF)
    one_part, d_rows, block_back = tie(one_part, d_rows, block_back)
    own, near, far = scatter_near(one_part)
    early = (
        sums,
        jnp.sum(resid_grad, axis=0),
        jnp.sum(two_grad * hat_two, axis=0),
        jnp.sum(two_grad, axis=0),
        jnp.sum(pre_grad, axis=0),
        jnp.sum(out_grad, axis=0),
    )
    far, d_rows, resid_rows, up_got, *early = tie(far, d_rows, resid_rows, up_got, *early)
    sums, resid_sum, two_hat_sum, two_sum, pre_sum, out_sum = early
    up_parts = to_z(up_keep, up_got)
    g_qkv = cross_dot(rows_one, d_rows).astype(BF)
    g_qkv = g_qkv.reshape(2, 4, rows_d, 2, 3, 2, HD)
    g_out = cross_dot(resid_rows, att_rows).astype(BF).reshape(2, 4, rows_d, 2, 1, 2, HD)
    g_head = jnp.concatenate([g_qkv, g_out], axis=4).transpose(0, 1, 3, 5, 2, 4, 6)
    g_head = g_head.reshape(n_dev, rows_d, 4 * HD)
    one_grad = scatter_far(own, near, far)
    g_head = lax.all_to_all(g_head, ("dp", "mp"), 0, 0, tiled=True)
    one_grad, *parts = tie(one_grad, *up_parts, *down_parts)
    in_grad = resid_grad + norm_back(one_grad, hat_one, inv_here, gain_one)
    in_back = bring_back(in_grad.astype(BF))
    g_hid = jnp.concatenate([total_z(parts[:4]), total_z(parts[4:])], axis=1)
    g_hid = exchange_swaps(g_hid.reshape(4, rows_d, 2 * units), t_index).astype(F32)

    mine = jnp.arange(4, dtype=jnp.int32) == t_index
    qv_part = sums.transpose(1, 0, 2).reshape(2, 4, 1, HD)
    qv_place = jnp.where(mine[None, None, :, None], qv_part, 0.0).reshape(2, width)
    up_part = pre_sum.reshape(4, units)[z_order][:, None, :]
    up_place = jnp.where(mine[None, :, None], up_part, 0.0).reshape(-1)
    sums = [
        jnp.sum(one_grad * hat_one, axis=0),
        jnp.sum(one_grad, axis=0),
        qv_place,
        resid_sum,
        two_hat_sum,
        two_sum,
        up_place,
        out_sum,
    ]
    rows, shapes = cut_vectors(sums, n_dev)
    shares = share_vectors(halve_sums(rows, d_index), shapes)
    g_head = jnp.sum(g_head.reshape(2, 4, 4, rows_d, 4, HD).astype(F32), axis=(0, 2))
    qkv_share = g_head[:, :, :3].transpose(2, 1, 0, 3).reshape(w_qkv.shape)
    out_share = g_head[:, :, 3].transpose(0, 2, 1).reshape(w_out.shape)

    up_share = g_hid[..., :units].transpose(1, 0, 2).reshape(w_up.shape)
    down_share = g_hid[..., units:].transpose(0, 2, 1).reshape(w_down.shape)

    block_out = block_back.astype(F32)
    return (block_out, in_back.astype(F32), qkv_share, out_share, up_share, down_share, *shares)


def solution(mesh):
    n_dp, n_mp = mesh.shape["dp"], mesh.shape["mp"]
    plane = (n_dp, n_mp) == (8, 4)
    local = local_plane if plane else local_any(n_dp, n_mp)
    both = ("dp", "mp")
    weights = (P(None, "dp", "mp"), P("mp", "dp"), P("dp", "mp"), P("mp", "dp"))
    vectors = (P(both), P(both), P(None, both), P(both), P(both), P(both), P(both), P(both))
    return jax.shard_map(
        local,
        mesh=mesh,
        in_specs=(P(both, None), P(both, None), P("dp"), *weights, *vectors),
        out_specs=(P(both, None), P(both, None), *weights, *vectors),
        check_vma=False,
    )
```

```python
import jax
import jax.numpy as jnp
from jax import lax
from jax.experimental import pallas as pl
from jax.experimental.pallas import tpu as pltpu
from jax.sharding import PartitionSpec as P


H = 16
HD = 64
L = 1152
BLK = 128
REACH = 5

NORM_EPS = 1e-05
GELU_SCALE = 0.7978845608028654
GELU_CUBE = 0.044715

BF = jnp.bfloat16
F32 = jnp.float32


def gelu_both(pre_act):
    inner = jnp.tanh(GELU_SCALE * (pre_act + GELU_CUBE * pre_act * pre_act * pre_act))
    value = 0.5 * pre_act * (1.0 + inner)
    slope = 0.5 * (1.0 + inner) + 0.5 * pre_act * (1.0 - inner * inner) * GELU_SCALE * (
        1.0 + 3.0 * GELU_CUBE * pre_act * pre_act
    )
    return value, slope


def norm_rows(inputs):
    center = inputs - jnp.mean(inputs, axis=-1, keepdims=True)
    scale_inv = lax.rsqrt(jnp.mean(center * center, axis=-1, keepdims=True) + NORM_EPS)
    return (center * scale_inv, scale_inv)


def norm_back(norm_grad, x_hat, scale_inv, gain):
    scaled = norm_grad * gain
    return scale_inv * (
        scaled
        - jnp.mean(scaled, axis=-1, keepdims=True)
        - x_hat * jnp.mean(scaled * x_hat, axis=-1, keepdims=True)
    )


def dot(left, right):
    return jnp.dot(left, right, preferred_element_type=F32)


def cross_dot(left, right):
    return lax.dot_general(left, right, (((0,), (0,)), ((), ())), preferred_element_type=F32)


def trans_dot(left, right):
    return lax.dot_general(left, right, (((1,), (1,)), ((), ())), preferred_element_type=F32)


def flip(x):
    return x.astype(F32).T


def load_rows(order_ref, src_ref, dst_ref, nb, rb):
    for k in range(nb):
        dst_ref[k * rb : (k + 1) * rb, :] = src_ref[order_ref[k]]


def half_masks(shape):
    lane = lax.broadcasted_iota(jnp.int32, shape, 1)
    return (lane < HD, lane >= HD)


def distances(b, segr_ref, segc_ref):
    w0 = max(0, b - REACH) * BLK
    w1 = (b + 1) * BLK
    keys = w0 + lax.broadcasted_iota(jnp.int32, (w1 - w0, BLK), 0)
    rows = b * BLK + lax.broadcasted_iota(jnp.int32, (w1 - w0, BLK), 1)
    same = segc_ref[w0:w1, :] == segr_ref[:, b * BLK : (b + 1) * BLK]
    gap = rows - keys
    dist = jnp.where(same & (gap >= 0), gap.astype(F32), 1e30)
    return w0, w1, dist


def attn_fwd_kernel(
    order_ref, slope_ref, segr_ref, segc_ref, q_ref, k_ref, v_ref, att_ref, lse_ref,
    q_s, k_s, v_s, vt_s, a_s, *, nb, rb,
):
    pair = pl.program_id(0)
    load_rows(order_ref, q_ref, q_s, nb, rb)
    load_rows(order_ref, k_ref, k_s, nb, rb)
    load_rows(order_ref, v_ref, v_s, nb, rb)
    vt_s[...] = flip(v_s[...]).astype(BF)
    halves = half_masks((BLK, 2 * HD))
    for b in range(L // BLK):
        r0 = b * BLK
        w0, w1, dist = distances(b, segr_ref, segc_ref)
        q_blk = q_s[r0 : r0 + BLK, :] * BF(HD ** (-0.5))
        outs = []
        for h in range(2):
            q_h = jnp.where(halves[h], q_blk, BF(0))
            s = trans_dot(k_s[w0:w1, :], q_h) - slope_ref[2 * pair + h] * dist
            top = jnp.max(s, axis=0, keepdims=True)
            e = jnp.exp(s - top)
            total = jnp.sum(e, axis=0, keepdims=True)
            lse_ref[0, h : h + 1, r0 : r0 + BLK] = top + jnp.log(total)
            prob = (e * (1.0 / total)).astype(BF)
            outs.append(dot(vt_s[h * HD : (h + 1) * HD, w0:w1], prob))
        a_s[r0 : r0 + BLK, :] = jnp.concatenate(outs, axis=0).T.astype(BF)
    for k in range(nb):
        att_ref[order_ref[k]] = a_s[k * rb : (k + 1) * rb, :]


def attn_bwd_kernel(
    order_ref, slope_ref, segr_ref, segc_ref, q_ref, k_ref, v_ref, att_ref, grad_ref, lse_ref,
    out_ref, sum_ref, q_s, k_s, v_s, kt_s, a_s, g_s, dq_s, dk_s, dv_s, *, nb, rb,
):
    pair = pl.program_id(0)
    load_rows(order_ref, q_ref, q_s, nb, rb)
    load_rows(order_ref, k_ref, k_s, nb, rb)
    load_rows(order_ref, v_ref, v_s, nb, rb)
    load_rows(order_ref, att_ref, a_s, nb, rb)
    load_rows(order_ref, grad_ref, g_s, nb, rb)
    kt_s[...] = flip(k_s[...]).astype(BF)
    dk_s[...] = jnp.zeros(dk_s.shape, F32)
    dv_s[...] = jnp.zeros(dv_s.shape, F32)
    halves = half_masks((BLK, 2 * HD))
    q_sum = jnp.zeros((1, 2 * HD), F32)
    for b in range(L // BLK):
        r0 = b * BLK
        w0, w1, dist = distances(b, segr_ref, segc_ref)
        q_blk = q_s[r0 : r0 + BLK, :] * BF(HD ** (-0.5))
        g_blk = g_s[r0 : r0 + BLK, :]
        prod = (a_s[r0 : r0 + BLK, :].astype(F32) * g_blk.astype(F32)).T
        probs, grads, q_hs, g_hs, dq_t = [], [], [], [], []
        for h in range(2):
            q_h = jnp.where(halves[h], q_blk, BF(0))
            g_h = jnp.where(halves[h], g_blk, BF(0))
            s = trans_dot(k_s[w0:w1, :], q_h) - slope_ref[2 * pair + h] * dist
            p = jnp.exp(s - lse_ref[0, h : h + 1, r0 : r0 + BLK])
            delta = jnp.sum(prod[h * HD : (h + 1) * HD, :], axis=0, keepdims=True)
            dp = trans_dot(v_s[w0:w1, :], g_h)
            ds = (p * (dp - delta)).astype(BF)
            dq_t.append(dot(kt_s[h * HD : (h + 1) * HD, w0:w1], ds))
            probs.append(p.astype(BF))
            grads.append(ds)
            q_hs.append(q_h)
            g_hs.append(g_h)
        dv_s[w0:w1, :] += dot(jnp.concatenate(probs, axis=1), jnp.concatenate(g_hs, axis=0))
        dk_s[w0:w1, :] += dot(jnp.concatenate(grads, axis=1), jnp.concatenate(q_hs, axis=0))
        dq = jnp.concatenate(dq_t, axis=0).T * HD ** (-0.5)
        q_sum = q_sum + jnp.sum(dq, axis=0, keepdims=True)
        dq_s[r0 : r0 + BLK, :] = dq.astype(BF)
    sum_ref[0, 0:1, :] = q_sum
    sum_ref[0, 1:2, :] = jnp.sum(dv_s[...], axis=0, keepdims=True)
    for k in range(nb):
        rows = slice(k * rb, (k + 1) * rb)
        out_ref[order_ref[k], :, 0 : 2 * HD] = dq_s[rows, :]
        out_ref[order_ref[k], :, 2 * HD : 4 * HD] = dk_s[rows, :].astype(BF)
        out_ref[order_ref[k], :, 4 * HD : 6 * HD] = dv_s[rows, :].astype(BF)


def attn_specs(nb, rb):
    smem = pl.BlockSpec(memory_space=pltpu.SMEM)
    col = lambda which: pl.BlockSpec((nb, rb, 2 * HD), lambda p: (0, 0, 3 * p + which))
    base = [
        smem,
        smem,
        pl.BlockSpec((1, L), lambda p: (0, 0)),
        pl.BlockSpec((L, 1), lambda p: (0, 0)),
        col(0),
        col(1),
        col(2),
    ]
    one = pl.BlockSpec((nb, rb, 2 * HD), lambda p: (0, 0, p))
    lse = pl.BlockSpec((1, 2, L), lambda p: (p, 0, 0))
    return base, one, lse


def attn_fwd(order, slopes, segs, qkv):
    nb, rb, cols = qkv.shape
    pairs = cols // (6 * HD)
    base, one, lse = attn_specs(nb, rb)
    rows = lambda: pltpu.VMEM((L, 2 * HD), BF)
    return pl.pallas_call(
        lambda *refs: attn_fwd_kernel(*refs, nb=nb, rb=rb),
        grid=(pairs,),
        in_specs=base,
        out_specs=[one, lse],
        out_shape=[
            jax.ShapeDtypeStruct((nb, rb, pairs * 2 * HD), BF),
            jax.ShapeDtypeStruct((pairs, 2, L), F32),
        ],
        scratch_shapes=[rows(), rows(), rows(), pltpu.VMEM((2 * HD, L), BF), rows()],
        name="attn_fwd",
        cost_estimate=pl.CostEstimate(
            flops=pairs * 4 * L * L * HD * 4, transcendentals=pairs * L * L, bytes_accessed=1 << 24
        ),
    )(order, slopes, segs.reshape(1, L), segs.reshape(L, 1), qkv, qkv, qkv)


def attn_bwd(order, slopes, segs, qkv, att, att_grad, lse_rows):
    nb, rb, cols = qkv.shape
    pairs = cols // (6 * HD)
    base, one, lse = attn_specs(nb, rb)
    rows = lambda dt=BF: pltpu.VMEM((L, 2 * HD), dt)
    return pl.pallas_call(
        lambda *refs: attn_bwd_kernel(*refs, nb=nb, rb=rb),
        grid=(pairs,),
        in_specs=base + [one, one, lse],
        out_specs=[
            pl.BlockSpec((nb, rb, 6 * HD), lambda p: (0, 0, p)),
            pl.BlockSpec((1, 2, 2 * HD), lambda p: (p, 0, 0)),
        ],
        out_shape=[
            jax.ShapeDtypeStruct((nb, rb, cols), BF),
            jax.ShapeDtypeStruct((pairs, 2, 2 * HD), F32),
        ],
        scratch_shapes=[rows(), rows(), rows(), pltpu.VMEM((2 * HD, L), BF), rows(), rows(),
                        rows(), rows(F32), rows(F32)],
        name="attn_bwd",
        cost_estimate=pl.CostEstimate(
            flops=pairs * 8 * L * L * HD * 4, transcendentals=pairs * L * L, bytes_accessed=1 << 25
        ),
    )(order, slopes, segs.reshape(1, L), segs.reshape(L, 1), qkv, qkv, qkv, att, att_grad, lse_rows)


def gather_vectors(vecs, n_dev):
    flat = jnp.concatenate([v.reshape(-1) for v in vecs])
    spread = jnp.broadcast_to(flat[None, :], (n_dev, flat.shape[0]))
    got = lax.all_to_all(spread, ("dp", "mp"), 0, 0, tiled=True)
    full, at = [], 0
    for v in vecs:
        n = v.size
        part = got[:, at : at + n]
        if v.ndim == 2:
            part = part.reshape(n_dev, v.shape[0], v.shape[1]).transpose(1, 0, 2)
            full.append(part.reshape(v.shape[0], -1))
        else:
            full.append(part.reshape(-1))
        at += n
    return full


def cut_vectors(fulls, n_dev):
    parts, shapes = [], []
    for v in fulls:
        if v.ndim == 2:
            part = v.reshape(v.shape[0], n_dev, -1).transpose(1, 0, 2)
            shapes.append((v.shape[0], v.shape[1] // n_dev))
        else:
            part = v
            shapes.append((v.shape[0] // n_dev,))
        parts.append(part.reshape(n_dev, -1))
    return jnp.concatenate(parts, axis=1), shapes


def share_vectors(flat, shapes):
    outs, at = [], 0
    for shape in shapes:
        n = shape[0] * (shape[1] if len(shape) == 2 else 1)
        outs.append(flat[at : at + n].reshape(shape))
        at += n
    return outs


def scatter_vectors(fulls, n_dev):
    rows, shapes = cut_vectors(fulls, n_dev)
    got = lax.all_to_all(rows, ("dp", "mp"), 0, 0, tiled=True)
    return share_vectors(jnp.sum(got, axis=0), shapes)


def head_slopes(numbers):
    return jnp.exp2(-8.0 * (numbers + 1).astype(F32) / H)


def pair_columns(parts):
    stacked = jnp.stack([p.reshape(p.shape[:-1] + (-1, 2 * HD)) for p in parts], axis=-2)
    return stacked.reshape(stacked.shape[:-3] + (-1,))


def local_any(n_dp, n_mp):
    n_dev = n_dp * n_mp

    def scatter_rows(part):
        return lax.psum_scatter(part.astype(BF), "mp", scatter_dimension=0, tiled=True).astype(F32)

    def scatter_grad(part, dim):
        return lax.psum_scatter(part.astype(BF), "dp", scatter_dimension=dim, tiled=True).astype(F32)

    def local(block_in, out_grad, segment_ids, w_qkv, w_out, w_up, w_down, *vecs):
        model_index = lax.axis_index("mp")
        gain_one, shift_one, qv_all, out_shift, gain_two, shift_two, up_all, down_shift = (
            gather_vectors(vecs, n_dev)
        )
        qkv_full = lax.all_gather(w_qkv, "dp", axis=1, tiled=True)
        out_full = lax.all_gather(w_out, "dp", axis=1, tiled=True)
        up_full = lax.all_gather(w_up, "dp", axis=0, tiled=True)
        down_full = lax.all_gather(w_down, "dp", axis=1, tiled=True)
        head_cols = qkv_full.shape[2]
        hid_cols = up_full.shape[1]
        n_heads = head_cols // HD
        qv_shift = lax.dynamic_slice_in_dim(qv_all, model_index * head_cols, head_cols, 1)
        up_shift = lax.dynamic_slice_in_dim(up_all, model_index * hid_cols, hid_cols, 0)
        slopes = head_slopes(model_index * n_heads + jnp.arange(n_heads, dtype=jnp.int32))
        order = jnp.zeros((1,), jnp.int32)
        w_local = pair_columns([qkv_full[0], qkv_full[1], qkv_full[2]])
        b_local = pair_columns([qv_shift[0], jnp.zeros_like(qv_shift[0]), qv_shift[1]])
        hat_one, inv_one = norm_rows(block_in)
        normed_one = (hat_one * gain_one + shift_one).astype(BF)
        rows_one = lax.all_gather(normed_one, "mp", axis=0, tiled=True)
        qkv = (dot(rows_one, w_local) + b_local).astype(BF)[None]
        att, lse = attn_fwd(order, slopes, segment_ids, qkv)
        resid = block_in + scatter_rows(dot(att[0], out_full)) + out_shift
        hat_two, inv_two = norm_rows(resid)
        normed_two = (hat_two * gain_two + shift_two).astype(BF)
        rows_two = lax.all_gather(normed_two, "mp", axis=0, tiled=True)
        value, slope = gelu_both(dot(rows_two, up_full) + up_shift)
        hidden = value.astype(BF)
        block_out = resid + scatter_rows(dot(hidden, down_full)) + down_shift
        grad_rows = lax.all_gather(out_grad.astype(BF), "mp", axis=0, tiled=True)
        down_share = scatter_grad(cross_dot(hidden, grad_rows), 1)
        pre_grad = trans_dot(grad_rows, down_full) * slope
        pre_low = pre_grad.astype(BF)
        up_share = scatter_grad(cross_dot(rows_two, pre_low), 0)
        two_grad = scatter_rows(trans_dot(pre_low, up_full))
        resid_grad = out_grad + norm_back(two_grad, hat_two, inv_two, gain_two)
        resid_rows = lax.all_gather(resid_grad.astype(BF), "mp", axis=0, tiled=True)
        out_share = scatter_grad(cross_dot(att[0], resid_rows), 1)
        att_grad = trans_dot(resid_rows, out_full).astype(BF)[None]
        d_qkv, sums = attn_bwd(order, slopes, segment_ids, qkv, att, att_grad, lse)
        grad_w = cross_dot(rows_one, d_qkv[0])
        grad_w = grad_w.reshape(grad_w.shape[0], -1, 3, 2 * HD).transpose(2, 0, 1, 3)
        qkv_share = scatter_grad(grad_w.reshape(3, grad_w.shape[1], -1), 1)
        one_grad = scatter_rows(trans_dot(d_qkv[0], w_local))
        in_grad = resid_grad + norm_back(one_grad, hat_one, inv_one, gain_one)
        qv_place = lax.dynamic_update_slice_in_dim(
            jnp.zeros(qv_all.shape, F32),
            sums.transpose(1, 0, 2).reshape(2, -1),
            model_index * head_cols,
            1,
        )
        up_place = lax.dynamic_update_slice_in_dim(
            jnp.zeros(up_all.shape, F32), jnp.sum(pre_grad, axis=0), model_index * hid_cols, 0
        )
        shares = scatter_vectors(
            [
                jnp.sum(one_grad * hat_one, axis=0),
                jnp.sum(one_grad, axis=0),
                qv_place,
                jnp.sum(resid_grad, axis=0),
                jnp.sum(two_grad * hat_two, axis=0),
                jnp.sum(two_grad, axis=0),
                up_place,
                jnp.sum(out_grad, axis=0),
            ],
            n_dev,
        )
        return (block_out, in_grad, qkv_share, out_share, up_share, down_share, *shares)

    return local


CHUNK_OF_T = (0, 3, 1, 2)
T_OF_CHUNK = (0, 2, 3, 1)
PLANE_OF_T = (0, 3, 1, 2)
GROUPS = [[0, 1, 2, 3], [4, 5, 6, 7]]
TO_PLANE = [
    ((4 * y + t) * 4 + z, (4 * y + T_OF_CHUNK[z]) * 4 + PLANE_OF_T[t])
    for y in range(2)
    for t in range(4)
    for z in range(4)
]
FROM_PLANE = [(b, a) for a, b in TO_PLANE]


def swap(x, bits):
    return lax.ppermute(x, "dp", [(i, i ^ bits) for i in range(8)])


def relocate(x):
    return lax.ppermute(x, ("dp", "mp"), TO_PLANE)


def bring_back(x):
    return lax.ppermute(x, ("dp", "mp"), FROM_PLANE)


def gather_t(x, near_fill=()):
    far = swap(x, 2)
    near, *fill = tie(swap(x, 1), *near_fill)
    rows = jnp.concatenate([x, near, far, swap(far, 1)], axis=0)
    return (rows, *fill) if fill else rows


def scatter_near(part):
    n = part.shape[0] // 4
    low = part.astype(BF)
    near = swap(jnp.concatenate([low[n : 2 * n], low[3 * n :]], axis=0), 1)
    far = (part[2 * n : 3 * n].astype(F32) + near[n:].astype(F32)).astype(BF)
    return part[:n], near[:n], far


def scatter_far(own, near, far):
    far = swap(far, 2)
    return own.astype(F32) + near.astype(F32) + far.astype(F32)


def exchange_t(x):
    return lax.all_to_all(x, "dp", 0, 0, tiled=True, axis_index_groups=GROUPS)


def exchange_swaps(x, t_index):
    got = [lax.dynamic_index_in_dim(x, t_index ^ j, 0, False) for j in range(4)]
    got = [got[0]] + [swap(got[j], j) for j in (1, 2, 3)]
    return jnp.stack(got)[jnp.arange(4, dtype=jnp.int32) ^ t_index]


def halve_sums(rows, d_index):
    rows = rows.reshape(2, 2, 2, 2, 2, -1)
    z_index = lax.axis_index("mp")
    bits = (d_index & 1, (d_index >> 1) & 1, d_index >> 2, z_index & 1, z_index >> 1)
    moves = (lambda v: swap(v, 1), lambda v: swap(v, 2), lambda v: swap(v, 4),
             lambda v: across(v, 1), lambda v: across(v, 2))
    for axis, bit, move in zip((2, 1, 0, 1, 0), bits, moves):
        keep = lax.dynamic_index_in_dim(rows, bit, axis, False)
        rows = keep + move(lax.dynamic_index_in_dim(rows, 1 - bit, axis, False))
    return rows


def across(x, bits):
    return lax.ppermute(x, "mp", [(i, i ^ bits) for i in range(4)])


def by_y(mine, other, y_index):
    mine, other = jnp.concatenate(mine, axis=1), jnp.concatenate(other, axis=1)
    first = jnp.where(y_index == 0, mine, other)
    second = jnp.where(y_index == 0, other, mine)
    return jnp.concatenate([first, second], axis=0)


def send_z(parts):
    return [parts[0]] + [across(parts[k], k) for k in (1, 2, 3)]


def total_z(parts):
    return sum(p.astype(F32) for p in parts).astype(BF)


def tie(*values):
    return lax.optimization_barrier(values)


def local_plane(block_in, out_grad, segment_ids, w_qkv, w_out, w_up, w_down, *vecs):
    n_dev = 32
    d_index = lax.axis_index("dp")
    t_index = d_index % 4
    y_index = d_index // 4
    width = block_in.shape[1]
    sub = width // 2
    rows_d = width // 8

    mean_one = jnp.mean(block_in, axis=-1, keepdims=True)
    center = block_in - mean_one
    inv_one = lax.rsqrt(jnp.mean(center * center, axis=-1, keepdims=True) + NORM_EPS)
    hat_low = relocate((center * inv_one).astype(BF))
    stats = relocate(jnp.concatenate([mean_one.reshape(1, -1), inv_one.reshape(1, -1)], axis=0))
    segs = relocate(segment_ids)

    heads = jnp.concatenate(
        [
            w_qkv.reshape(3, -1, 4, HD).transpose(2, 1, 0, 3).reshape(4, -1, 3 * HD),
            w_out.reshape(4, HD, -1).transpose(0, 2, 1),
        ],
        axis=2,
    )
    hids = jnp.concatenate(
        [
            w_up.reshape(w_up.shape[0], 4, -1).transpose(1, 0, 2),
            w_down.reshape(4, -1, w_down.shape[1]).transpose(0, 2, 1),
        ],
        axis=2,
    )
    both = exchange_t(jnp.concatenate([heads, hids], axis=2)).reshape(sub, -1)
    both, *vecs = tie(both, *vecs)
    gain_one, shift_one, qv_all, out_shift, gain_two, shift_two, up_all, down_shift = (
        gather_vectors(vecs, n_dev)
    )
    hat_low, stats, segs, gain_one = tie(hat_low, stats, segs, gain_one)
    heads, hids = both[:, : 4 * HD], both[:, 4 * HD :]
    heads_mine = [heads] + [across(heads, k) for k in (1, 2, 3)]
    out_low, hat_low = tie(out_grad.astype(BF), hat_low)
    grad_low = relocate(out_low)
    mine = [hids] + [across(hids, k) for k in (1, 2, 3)]
    other = [swap(hids, 4)]

    qv_mine = lax.dynamic_index_in_dim(qv_all.reshape(2, 4, 4, HD), t_index, 2, False)
    z_order = jnp.arange(4, dtype=jnp.int32) ^ lax.axis_index("mp")
    qv_mine = qv_mine[:, z_order].reshape(2, -1)
    b_local = pair_columns([qv_mine[0], jnp.zeros_like(qv_mine[0]), qv_mine[1]])
    up_shift = lax.dynamic_index_in_dim(up_all.reshape(4, 4, -1), t_index, 1, False)
    up_shift = up_shift[z_order].reshape(-1)
    slopes = head_slopes(4 * z_order + t_index)
    chunk = jnp.asarray(CHUNK_OF_T, jnp.int32)[t_index]
    order = jnp.asarray(T_OF_CHUNK, jnp.int32)[jnp.arange(4, dtype=jnp.int32) ^ chunk]

    hat_one = hat_low.astype(F32)
    mean_here, inv_here = stats[0][:, None], stats[1][:, None]
    block_here = hat_one * (1.0 / inv_here) + mean_here
    rows_one, *heads_mine[1:] = gather_t(
        (hat_one * gain_one + shift_one).astype(BF), near_fill=heads_mine[1:]
    )
    heads_other = [swap(heads, 4)]
    heads_other = heads_other + [swap(m, 4) for m in heads_mine[1:]]
    heads_mine = [h.reshape(sub, 4, HD) for h in heads_mine]
    heads_other = [h.reshape(sub, 4, HD) for h in heads_other]
    qkv_order = [(2 * p + k, which) for p in range(2) for which in range(3) for k in range(2)]
    w_local = by_y(
        [heads_mine[k][:, w] for k, w in qkv_order],
        [heads_other[k][:, w] for k, w in qkv_order],
        y_index,
    )
    w_out_t = by_y([h[:, 3] for h in heads_mine], [h[:, 3] for h in heads_other], y_index)
    w_local, w_out_t = tie(w_local, w_out_t)
    qkv = (dot(rows_one, w_local) + b_local).astype(BF)
    grad_low, qkv = tie(grad_low, qkv)
    grad_rows = gather_t(grad_low)
    grad_here = grad_low.astype(F32)
    qkv = qkv.reshape(4, -1, w_local.shape[1])
    att, lse = attn_fwd(order, slopes, segs, qkv)
    att_rows = att.reshape(-1, att.shape[2])
    att_part = trans_dot(att_rows, w_out_t).astype(BF)
    own, near, far = scatter_near(att_part)
    att_sum = own.astype(F32) + near.astype(F32)
    att_sum, *mine[1:] = tie(att_sum, *mine[1:])
    att_sum = att_sum + swap(far, 2).astype(F32)
    other = other + [swap(m, 4) for m in mine[1:]]
    units = hids.shape[1] // 2
    up_local = by_y([m[:, :units] for m in mine], [m[:, :units] for m in other], y_index)
    down_t = by_y([m[:, units:] for m in mine], [m[:, units:] for m in other], y_index)
    up_local, down_t = tie(up_local, down_t)
    resid = block_here + att_sum + out_shift
    hat_two, inv_two = norm_rows(resid)
    rows_two = gather_t((hat_two * gain_two + shift_two).astype(BF))
    rows_two, grad_rows = tie(rows_two, grad_rows)
    value, slope = gelu_both(dot(rows_two, up_local) + up_shift)
    hidden = value.astype(BF)
    down_part = trans_dot(hidden, down_t).astype(BF)
    own_d, near_d, far_d = scatter_near(down_part)
    hidden, own_d = tie(hidden, own_d)
    g_down = cross_dot(grad_rows, hidden).astype(BF)
    far_d, g_down, grad_rows = tie(far_d, g_down, grad_rows)
    block_sum = swap(far_d, 2)
    pre_grad = dot(grad_rows, down_t) * slope
    pre_low = pre_grad.astype(BF)
    two_part = trans_dot(pre_low, up_local).astype(BF)
    own, near, far = scatter_near(two_part)

    far, pre_low = tie(far, pre_low)
    g_up = cross_dot(rows_two, pre_low).astype(BF)
    g_up, block_sum = tie(g_up, block_sum)
    block_sum = own_d.astype(F32) + near_d.astype(F32) + block_sum.astype(F32)
    block_low = (resid + block_sum + down_shift).astype(BF)

    def to_y(grad):
        halves = grad[:sub], grad[sub:]
        keep = jnp.where(y_index == 0, *halves)
        send = jnp.where(y_index == 0, halves[1], halves[0])
        return keep, swap(send, 4)

    def to_z(keep, got):
        both = (keep.astype(F32) + got.astype(F32)).astype(BF)
        return send_z([both[:, k * units : (k + 1) * units] for k in range(4)])

    down_keep, down_got = to_y(g_down)
    up_keep, up_got = to_y(g_up)
    two_grad, up_keep, block_low = tie(scatter_far(own, near, far), up_keep, block_low)

    resid_grad = grad_here + norm_back(two_grad, hat_two, inv_two, gain_two)
    resid_low = resid_grad.astype(BF)
    resid_rows, down_got = gather_t(resid_low, near_fill=[down_got])
    resid_rows, block_low = tie(resid_rows, block_low)
    block_back = bring_back(block_low)
    down_parts = to_z(down_keep, down_got)

    att_grad = dot(resid_rows, w_out_t).astype(BF).reshape(att.shape)
    d_qkv, sums = attn_bwd(order, slopes, segs, qkv, att, att_grad, lse)
    d_rows = d_qkv.reshape(-1, d_qkv.shape[2])
    one_part = trans_dot(d_rows, w_local).astype(BF)
    one_part, d_rows = tie(one_part, d_rows)
    g_qkv = cross_dot(rows_one, d_rows).astype(BF)
    own, near, far = scatter_near(one_part)
    early = (
        sums,
        jnp.sum(resid_grad, axis=0),
        jnp.sum(two_grad * hat_two, axis=0),
        jnp.sum(two_grad, axis=0),
        jnp.sum(pre_grad, axis=0),
        jnp.sum(out_grad, axis=0),
    )
    far, g_qkv, resid_rows, up_got, *early = tie(far, g_qkv, resid_rows, up_got, *early)
    sums, resid_sum, two_hat_sum, two_sum, pre_sum, out_sum = early
    up_parts = to_z(up_keep, up_got)
    qkv_keep, qkv_got = to_y(g_qkv)
    g_out = cross_dot(resid_rows, att_rows).astype(BF)
    out_keep, out_got = to_y(g_out)
    one_grad = scatter_far(own, near, far)
    one_grad, block_back, *parts = tie(one_grad, block_back, *up_parts, *down_parts)
    in_grad = resid_grad + norm_back(one_grad, hat_one, inv_here, gain_one)
    in_back = bring_back(in_grad.astype(BF))
    one_sum = jnp.sum(one_grad, axis=0)
    one_sum, qkv_got, out_got = tie(one_sum, qkv_got, out_got)
    both = (qkv_keep.astype(F32) + qkv_got.astype(F32)).astype(BF).reshape(sub, 2, 3, 2, HD)
    both_out = (out_keep.astype(F32) + out_got.astype(F32)).astype(BF).reshape(sub, 2, 1, 2, HD)
    both = jnp.concatenate([both, both_out], axis=2)
    head_parts = send_z([both[:, k // 2, :, k % 2].reshape(sub, 4 * HD) for k in range(4)])
    g_hid = jnp.concatenate([total_z(parts[:4]), total_z(parts[4:])], axis=1)
    g_hid = exchange_swaps(g_hid.reshape(4, rows_d, 2 * units), t_index).astype(F32)

    mine = jnp.arange(4, dtype=jnp.int32) == t_index
    qv_part = sums.transpose(1, 0, 2).reshape(2, 4, HD)[:, z_order][:, :, None, :]
    qv_place = jnp.where(mine[None, None, :, None], qv_part, 0.0).reshape(2, width)
    up_part = pre_sum.reshape(4, units)[z_order][:, None, :]
    up_place = jnp.where(mine[None, :, None], up_part, 0.0).reshape(-1)
    sums = [
        jnp.sum(one_grad * hat_one, axis=0),
        jnp.sum(one_grad, axis=0),
        qv_place,
        resid_sum,
        two_hat_sum,
        two_sum,
        up_place,
        out_sum,
    ]
    rows, shapes = cut_vectors(sums, n_dev)
    shares = share_vectors(halve_sums(rows, d_index), shapes)
    g_head = exchange_swaps(total_z(head_parts).reshape(4, rows_d, 4 * HD), t_index)
    g_head = g_head.astype(F32).reshape(4, rows_d, 4, HD)
    qkv_share = g_head[:, :, :3].transpose(2, 1, 0, 3).reshape(w_qkv.shape)
    out_share = g_head[:, :, 3].transpose(0, 2, 1).reshape(w_out.shape)

    up_share = g_hid[..., :units].transpose(1, 0, 2).reshape(w_up.shape)
    down_share = g_hid[..., units:].transpose(0, 2, 1).reshape(w_down.shape)

    block_out = block_back.astype(F32)
    return (block_out, in_back.astype(F32), qkv_share, out_share, up_share, down_share, *shares)


def solution(mesh):
    n_dp, n_mp = mesh.shape["dp"], mesh.shape["mp"]
    plane = (n_dp, n_mp) == (8, 4)
    local = local_plane if plane else local_any(n_dp, n_mp)
    both = ("dp", "mp")
    weights = (P(None, "dp", "mp"), P("mp", "dp"), P("dp", "mp"), P("mp", "dp"))
    vectors = (P(both), P(both), P(None, both), P(both), P(both), P(both), P(both), P(both))
    return jax.shard_map(
        local,
        mesh=mesh,
        in_specs=(P(both, None), P(both, None), P("dp"), *weights, *vectors),
        out_specs=(P(both, None), P(both, None), *weights, *vectors),
        check_vma=False,
    )
```

```python
import jax
import jax.numpy as jnp
from jax import lax
from jax.experimental import pallas as pl
from jax.experimental.pallas import tpu as pltpu
from jax.sharding import PartitionSpec as P


H = 16
HD = 64
L = 1152
BLK = 128
REACH = 5

NORM_EPS = 1e-05
GELU_SCALE = 0.7978845608028654
GELU_CUBE = 0.044715

BF = jnp.bfloat16
F32 = jnp.float32


def gelu_both(pre_act):
    inner = jnp.tanh(GELU_SCALE * (pre_act + GELU_CUBE * pre_act * pre_act * pre_act))
    value = 0.5 * pre_act * (1.0 + inner)
    slope = 0.5 * (1.0 + inner) + 0.5 * pre_act * (1.0 - inner * inner) * GELU_SCALE * (
        1.0 + 3.0 * GELU_CUBE * pre_act * pre_act
    )
    return value, slope


def norm_rows(inputs):
    center = inputs - jnp.mean(inputs, axis=-1, keepdims=True)
    scale_inv = lax.rsqrt(jnp.mean(center * center, axis=-1, keepdims=True) + NORM_EPS)
    return (center * scale_inv, scale_inv)


def norm_back(norm_grad, x_hat, scale_inv, gain):
    scaled = norm_grad * gain
    return scale_inv * (
        scaled
        - jnp.mean(scaled, axis=-1, keepdims=True)
        - x_hat * jnp.mean(scaled * x_hat, axis=-1, keepdims=True)
    )


def dot(left, right):
    return jnp.dot(left, right, preferred_element_type=F32)


def cross_dot(left, right):
    return lax.dot_general(left, right, (((0,), (0,)), ((), ())), preferred_element_type=F32)


def trans_dot(left, right):
    return lax.dot_general(left, right, (((1,), (1,)), ((), ())), preferred_element_type=F32)


def flip(x):
    return x.astype(F32).T


def load_rows(order_ref, src_ref, dst_ref, nb, rb):
    for k in range(nb):
        dst_ref[k * rb : (k + 1) * rb, :] = src_ref[order_ref[k]]


def half_masks(shape):
    lane = lax.broadcasted_iota(jnp.int32, shape, 1)
    return (lane < HD, lane >= HD)


def distances(b, segr_ref, segc_ref):
    w0 = max(0, b - REACH) * BLK
    w1 = (b + 1) * BLK
    keys = w0 + lax.broadcasted_iota(jnp.int32, (w1 - w0, BLK), 0)
    rows = b * BLK + lax.broadcasted_iota(jnp.int32, (w1 - w0, BLK), 1)
    same = segc_ref[w0:w1, :] == segr_ref[:, b * BLK : (b + 1) * BLK]
    gap = rows - keys
    dist = jnp.where(same & (gap >= 0), gap.astype(F32), 1e30)
    return w0, w1, dist


def attn_fwd_kernel(
    order_ref, slope_ref, segr_ref, segc_ref, q_ref, k_ref, v_ref, att_ref, lse_ref,
    q_s, k_s, v_s, vt_s, a_s, *, nb, rb,
):
    pair = pl.program_id(0)
    load_rows(order_ref, q_ref, q_s, nb, rb)
    load_rows(order_ref, k_ref, k_s, nb, rb)
    load_rows(order_ref, v_ref, v_s, nb, rb)
    vt_s[...] = flip(v_s[...]).astype(BF)
    halves = half_masks((BLK, 2 * HD))
    for b in range(L // BLK):
        r0 = b * BLK
        w0, w1, dist = distances(b, segr_ref, segc_ref)
        q_blk = q_s[r0 : r0 + BLK, :] * BF(HD ** (-0.5))
        outs = []
        for h in range(2):
            q_h = jnp.where(halves[h], q_blk, BF(0))
            s = trans_dot(k_s[w0:w1, :], q_h) - slope_ref[2 * pair + h] * dist
            top = jnp.max(s, axis=0, keepdims=True)
            e = jnp.exp(s - top)
            total = jnp.sum(e, axis=0, keepdims=True)
            lse_ref[0, h : h + 1, r0 : r0 + BLK] = top + jnp.log(total)
            prob = (e * (1.0 / total)).astype(BF)
            outs.append(dot(vt_s[h * HD : (h + 1) * HD, w0:w1], prob))
        a_s[r0 : r0 + BLK, :] = jnp.concatenate(outs, axis=0).T.astype(BF)
    for k in range(nb):
        att_ref[order_ref[k]] = a_s[k * rb : (k + 1) * rb, :]


def attn_bwd_kernel(
    order_ref, slope_ref, segr_ref, segc_ref, q_ref, k_ref, v_ref, att_ref, grad_ref, lse_ref,
    out_ref, sum_ref, q_s, k_s, v_s, kt_s, a_s, g_s, dq_s, dk_s, dv_s, *, nb, rb,
):
    pair = pl.program_id(0)
    load_rows(order_ref, q_ref, q_s, nb, rb)
    load_rows(order_ref, k_ref, k_s, nb, rb)
    load_rows(order_ref, v_ref, v_s, nb, rb)
    load_rows(order_ref, att_ref, a_s, nb, rb)
    load_rows(order_ref, grad_ref, g_s, nb, rb)
    kt_s[...] = flip(k_s[...]).astype(BF)
    dk_s[...] = jnp.zeros(dk_s.shape, F32)
    dv_s[...] = jnp.zeros(dv_s.shape, F32)
    halves = half_masks((BLK, 2 * HD))
    q_sum = jnp.zeros((1, 2 * HD), F32)
    for b in range(L // BLK):
        r0 = b * BLK
        w0, w1, dist = distances(b, segr_ref, segc_ref)
        q_blk = q_s[r0 : r0 + BLK, :] * BF(HD ** (-0.5))
        g_blk = g_s[r0 : r0 + BLK, :]
        prod = (a_s[r0 : r0 + BLK, :].astype(F32) * g_blk.astype(F32)).T
        probs, grads, q_hs, g_hs, dq_t = [], [], [], [], []
        for h in range(2):
            q_h = jnp.where(halves[h], q_blk, BF(0))
            g_h = jnp.where(halves[h], g_blk, BF(0))
            s = trans_dot(k_s[w0:w1, :], q_h) - slope_ref[2 * pair + h] * dist
            p = jnp.exp(s - lse_ref[0, h : h + 1, r0 : r0 + BLK])
            delta = jnp.sum(prod[h * HD : (h + 1) * HD, :], axis=0, keepdims=True)
            dp = trans_dot(v_s[w0:w1, :], g_h)
            ds = (p * (dp - delta)).astype(BF)
            dq_t.append(dot(kt_s[h * HD : (h + 1) * HD, w0:w1], ds))
            probs.append(p.astype(BF))
            grads.append(ds)
            q_hs.append(q_h)
            g_hs.append(g_h)
        dv_s[w0:w1, :] += dot(jnp.concatenate(probs, axis=1), jnp.concatenate(g_hs, axis=0))
        dk_s[w0:w1, :] += dot(jnp.concatenate(grads, axis=1), jnp.concatenate(q_hs, axis=0))
        dq = jnp.concatenate(dq_t, axis=0).T * HD ** (-0.5)
        q_sum = q_sum + jnp.sum(dq, axis=0, keepdims=True)
        dq_s[r0 : r0 + BLK, :] = dq.astype(BF)
    sum_ref[0, 0:1, :] = q_sum
    sum_ref[0, 1:2, :] = jnp.sum(dv_s[...], axis=0, keepdims=True)
    for k in range(nb):
        rows = slice(k * rb, (k + 1) * rb)
        out_ref[order_ref[k], :, 0 : 2 * HD] = dq_s[rows, :]
        out_ref[order_ref[k], :, 2 * HD : 4 * HD] = dk_s[rows, :].astype(BF)
        out_ref[order_ref[k], :, 4 * HD : 6 * HD] = dv_s[rows, :].astype(BF)


def attn_specs(nb, rb):
    smem = pl.BlockSpec(memory_space=pltpu.SMEM)
    col = lambda which: pl.BlockSpec((nb, rb, 2 * HD), lambda p: (0, 0, 3 * p + which))
    base = [
        smem,
        smem,
        pl.BlockSpec((1, L), lambda p: (0, 0)),
        pl.BlockSpec((L, 1), lambda p: (0, 0)),
        col(0),
        col(1),
        col(2),
    ]
    one = pl.BlockSpec((nb, rb, 2 * HD), lambda p: (0, 0, p))
    lse = pl.BlockSpec((1, 2, L), lambda p: (p, 0, 0))
    return base, one, lse


def attn_fwd(order, slopes, segs, qkv):
    nb, rb, cols = qkv.shape
    pairs = cols // (6 * HD)
    base, one, lse = attn_specs(nb, rb)
    rows = lambda: pltpu.VMEM((L, 2 * HD), BF)
    return pl.pallas_call(
        lambda *refs: attn_fwd_kernel(*refs, nb=nb, rb=rb),
        grid=(pairs,),
        in_specs=base,
        out_specs=[one, lse],
        out_shape=[
            jax.ShapeDtypeStruct((nb, rb, pairs * 2 * HD), BF),
            jax.ShapeDtypeStruct((pairs, 2, L), F32),
        ],
        scratch_shapes=[rows(), rows(), rows(), pltpu.VMEM((2 * HD, L), BF), rows()],
        name="attn_fwd",
        cost_estimate=pl.CostEstimate(
            flops=pairs * 4 * L * L * HD * 4, transcendentals=pairs * L * L, bytes_accessed=1 << 24
        ),
    )(order, slopes, segs.reshape(1, L), segs.reshape(L, 1), qkv, qkv, qkv)


def attn_bwd(order, slopes, segs, qkv, att, att_grad, lse_rows):
    nb, rb, cols = qkv.shape
    pairs = cols // (6 * HD)
    base, one, lse = attn_specs(nb, rb)
    rows = lambda dt=BF: pltpu.VMEM((L, 2 * HD), dt)
    return pl.pallas_call(
        lambda *refs: attn_bwd_kernel(*refs, nb=nb, rb=rb),
        grid=(pairs,),
        in_specs=base + [one, one, lse],
        out_specs=[
            pl.BlockSpec((nb, rb, 6 * HD), lambda p: (0, 0, p)),
            pl.BlockSpec((1, 2, 2 * HD), lambda p: (p, 0, 0)),
        ],
        out_shape=[
            jax.ShapeDtypeStruct((nb, rb, cols), BF),
            jax.ShapeDtypeStruct((pairs, 2, 2 * HD), F32),
        ],
        scratch_shapes=[rows(), rows(), rows(), pltpu.VMEM((2 * HD, L), BF), rows(), rows(),
                        rows(), rows(F32), rows(F32)],
        name="attn_bwd",
        cost_estimate=pl.CostEstimate(
            flops=pairs * 8 * L * L * HD * 4, transcendentals=pairs * L * L, bytes_accessed=1 << 25
        ),
    )(order, slopes, segs.reshape(1, L), segs.reshape(L, 1), qkv, qkv, qkv, att, att_grad, lse_rows)


def gather_vectors(vecs, n_dev):
    flat = jnp.concatenate([v.reshape(-1) for v in vecs])
    spread = jnp.broadcast_to(flat[None, :], (n_dev, flat.shape[0]))
    got = lax.all_to_all(spread, ("dp", "mp"), 0, 0, tiled=True)
    full, at = [], 0
    for v in vecs:
        n = v.size
        part = got[:, at : at + n]
        if v.ndim == 2:
            part = part.reshape(n_dev, v.shape[0], v.shape[1]).transpose(1, 0, 2)
            full.append(part.reshape(v.shape[0], -1))
        else:
            full.append(part.reshape(-1))
        at += n
    return full


def cut_vectors(fulls, n_dev):
    parts, shapes = [], []
    for v in fulls:
        if v.ndim == 2:
            part = v.reshape(v.shape[0], n_dev, -1).transpose(1, 0, 2)
            shapes.append((v.shape[0], v.shape[1] // n_dev))
        else:
            part = v
            shapes.append((v.shape[0] // n_dev,))
        parts.append(part.reshape(n_dev, -1))
    return jnp.concatenate(parts, axis=1), shapes


def share_vectors(flat, shapes):
    outs, at = [], 0
    for shape in shapes:
        n = shape[0] * (shape[1] if len(shape) == 2 else 1)
        outs.append(flat[at : at + n].reshape(shape))
        at += n
    return outs


def scatter_vectors(fulls, n_dev):
    rows, shapes = cut_vectors(fulls, n_dev)
    got = lax.all_to_all(rows, ("dp", "mp"), 0, 0, tiled=True)
    return share_vectors(jnp.sum(got, axis=0), shapes)


def head_slopes(numbers):
    return jnp.exp2(-8.0 * (numbers + 1).astype(F32) / H)


def pair_columns(parts):
    stacked = jnp.stack([p.reshape(p.shape[:-1] + (-1, 2 * HD)) for p in parts], axis=-2)
    return stacked.reshape(stacked.shape[:-3] + (-1,))


def local_any(n_dp, n_mp):
    n_dev = n_dp * n_mp

    def scatter_rows(part):
        return lax.psum_scatter(part.astype(BF), "mp", scatter_dimension=0, tiled=True).astype(F32)

    def scatter_grad(part, dim):
        return lax.psum_scatter(part.astype(BF), "dp", scatter_dimension=dim, tiled=True).astype(F32)

    def local(block_in, out_grad, segment_ids, w_qkv, w_out, w_up, w_down, *vecs):
        model_index = lax.axis_index("mp")
        gain_one, shift_one, qv_all, out_shift, gain_two, shift_two, up_all, down_shift = (
            gather_vectors(vecs, n_dev)
        )
        qkv_full = lax.all_gather(w_qkv, "dp", axis=1, tiled=True)
        out_full = lax.all_gather(w_out, "dp", axis=1, tiled=True)
        up_full = lax.all_gather(w_up, "dp", axis=0, tiled=True)
        down_full = lax.all_gather(w_down, "dp", axis=1, tiled=True)
        head_cols = qkv_full.shape[2]
        hid_cols = up_full.shape[1]
        n_heads = head_cols // HD
        qv_shift = lax.dynamic_slice_in_dim(qv_all, model_index * head_cols, head_cols, 1)
        up_shift = lax.dynamic_slice_in_dim(up_all, model_index * hid_cols, hid_cols, 0)
        slopes = head_slopes(model_index * n_heads + jnp.arange(n_heads, dtype=jnp.int32))
        order = jnp.zeros((1,), jnp.int32)
        w_local = pair_columns([qkv_full[0], qkv_full[1], qkv_full[2]])
        b_local = pair_columns([qv_shift[0], jnp.zeros_like(qv_shift[0]), qv_shift[1]])
        hat_one, inv_one = norm_rows(block_in)
        normed_one = (hat_one * gain_one + shift_one).astype(BF)
        rows_one = lax.all_gather(normed_one, "mp", axis=0, tiled=True)
        qkv = (dot(rows_one, w_local) + b_local).astype(BF)[None]
        att, lse = attn_fwd(order, slopes, segment_ids, qkv)
        resid = block_in + scatter_rows(dot(att[0], out_full)) + out_shift
        hat_two, inv_two = norm_rows(resid)
        normed_two = (hat_two * gain_two + shift_two).astype(BF)
        rows_two = lax.all_gather(normed_two, "mp", axis=0, tiled=True)
        value, slope = gelu_both(dot(rows_two, up_full) + up_shift)
        hidden = value.astype(BF)
        block_out = resid + scatter_rows(dot(hidden, down_full)) + down_shift
        grad_rows = lax.all_gather(out_grad.astype(BF), "mp", axis=0, tiled=True)
        down_share = scatter_grad(cross_dot(hidden, grad_rows), 1)
        pre_grad = trans_dot(grad_rows, down_full) * slope
        pre_low = pre_grad.astype(BF)
        up_share = scatter_grad(cross_dot(rows_two, pre_low), 0)
        two_grad = scatter_rows(trans_dot(pre_low, up_full))
        resid_grad = out_grad + norm_back(two_grad, hat_two, inv_two, gain_two)
        resid_rows = lax.all_gather(resid_grad.astype(BF), "mp", axis=0, tiled=True)
        out_share = scatter_grad(cross_dot(att[0], resid_rows), 1)
        att_grad = trans_dot(resid_rows, out_full).astype(BF)[None]
        d_qkv, sums = attn_bwd(order, slopes, segment_ids, qkv, att, att_grad, lse)
        grad_w = cross_dot(rows_one, d_qkv[0])
        grad_w = grad_w.reshape(grad_w.shape[0], -1, 3, 2 * HD).transpose(2, 0, 1, 3)
        qkv_share = scatter_grad(grad_w.reshape(3, grad_w.shape[1], -1), 1)
        one_grad = scatter_rows(trans_dot(d_qkv[0], w_local))
        in_grad = resid_grad + norm_back(one_grad, hat_one, inv_one, gain_one)
        qv_place = lax.dynamic_update_slice_in_dim(
            jnp.zeros(qv_all.shape, F32),
            sums.transpose(1, 0, 2).reshape(2, -1),
            model_index * head_cols,
            1,
        )
        up_place = lax.dynamic_update_slice_in_dim(
            jnp.zeros(up_all.shape, F32), jnp.sum(pre_grad, axis=0), model_index * hid_cols, 0
        )
        shares = scatter_vectors(
            [
                jnp.sum(one_grad * hat_one, axis=0),
                jnp.sum(one_grad, axis=0),
                qv_place,
                jnp.sum(resid_grad, axis=0),
                jnp.sum(two_grad * hat_two, axis=0),
                jnp.sum(two_grad, axis=0),
                up_place,
                jnp.sum(out_grad, axis=0),
            ],
            n_dev,
        )
        return (block_out, in_grad, qkv_share, out_share, up_share, down_share, *shares)

    return local


CHUNK_OF_T = (0, 3, 1, 2)
T_OF_CHUNK = (0, 2, 3, 1)
PLANE_OF_T = (0, 3, 1, 2)
GROUPS = [[0, 1, 2, 3], [4, 5, 6, 7]]
TO_PLANE = [
    ((4 * y + t) * 4 + z, (4 * y + T_OF_CHUNK[z]) * 4 + PLANE_OF_T[t])
    for y in range(2)
    for t in range(4)
    for z in range(4)
]
FROM_PLANE = [(b, a) for a, b in TO_PLANE]


def swap(x, bits):
    return lax.ppermute(x, "dp", [(i, i ^ bits) for i in range(8)])


def relocate(x):
    return lax.ppermute(x, ("dp", "mp"), TO_PLANE)


def bring_back(x):
    return lax.ppermute(x, ("dp", "mp"), FROM_PLANE)


def gather_t(x, near_fill=()):
    far = swap(x, 2)
    near, *fill = tie(swap(x, 1), *near_fill)
    rows = jnp.concatenate([x, near, far, swap(far, 1)], axis=0)
    return (rows, *fill) if fill else rows


def scatter_near(part):
    n = part.shape[0] // 4
    low = part.astype(BF)
    near = swap(jnp.concatenate([low[n : 2 * n], low[3 * n :]], axis=0), 1)
    far = (part[2 * n : 3 * n].astype(F32) + near[n:].astype(F32)).astype(BF)
    return part[:n], near[:n], far


def scatter_far(own, near, far):
    far = swap(far, 2)
    return own.astype(F32) + near.astype(F32) + far.astype(F32)


def exchange_t(x):
    return lax.all_to_all(x, "dp", 0, 0, tiled=True, axis_index_groups=GROUPS)


def exchange_swaps(x, t_index):
    got = [lax.dynamic_index_in_dim(x, t_index ^ j, 0, False) for j in range(4)]
    got = [got[0]] + [swap(got[j], j) for j in (1, 2, 3)]
    return jnp.stack(got)[jnp.arange(4, dtype=jnp.int32) ^ t_index]


def halve_sums(rows, d_index):
    rows = rows.reshape(2, 2, 2, 2, 2, -1)
    z_index = lax.axis_index("mp")
    bits = (d_index & 1, (d_index >> 1) & 1, d_index >> 2, z_index & 1, z_index >> 1)
    moves = (lambda v: swap(v, 1), lambda v: swap(v, 2), lambda v: swap(v, 4),
             lambda v: across(v, 1), lambda v: across(v, 2))
    for axis, bit, move in zip((2, 1, 0, 1, 0), bits, moves):
        keep = lax.dynamic_index_in_dim(rows, bit, axis, False)
        rows = keep + move(lax.dynamic_index_in_dim(rows, 1 - bit, axis, False))
    return rows


def across(x, bits):
    return lax.ppermute(x, "mp", [(i, i ^ bits) for i in range(4)])


def by_y(mine, other, y_index):
    mine, other = jnp.concatenate(mine, axis=1), jnp.concatenate(other, axis=1)
    first = jnp.where(y_index == 0, mine, other)
    second = jnp.where(y_index == 0, other, mine)
    return jnp.concatenate([first, second], axis=0)


def head_weights_kernel(y_ref, *refs, n):
    qkv_ref, out_ref = refs[8:]

    def write(half, rows):
        for p in range(2):
            low, high = refs[4 * half + 2 * p][...], refs[4 * half + 2 * p + 1][...]
            for w in range(4):
                cols = slice(w * HD, (w + 1) * HD)
                both = jnp.concatenate([low[:, cols], high[:, cols]], axis=1)
                if w < 3:
                    qkv_ref[rows, (3 * p + w) * 2 * HD : (3 * p + w + 1) * 2 * HD] = both
                else:
                    out_ref[rows, p * 2 * HD : (p + 1) * 2 * HD] = both

    for y in range(2):

        @pl.when(y_ref[0] == y)
        def _():
            for half in range(2):
                write(half, slice((y ^ half) * n, ((y ^ half) + 1) * n))


def head_weights(y_index, mine, other):
    n = mine[0].shape[0]
    vmem = pl.BlockSpec(memory_space=pltpu.VMEM)
    return pl.pallas_call(
        lambda *refs: head_weights_kernel(*refs, n=n),
        in_specs=[pl.BlockSpec(memory_space=pltpu.SMEM)] + [vmem] * 8,
        out_specs=[vmem, vmem],
        out_shape=[
            jax.ShapeDtypeStruct((2 * n, 12 * HD), BF),
            jax.ShapeDtypeStruct((2 * n, 4 * HD), BF),
        ],
        name="head_weights",
    )(y_index.reshape(1), *mine, *other)


def send_z(parts):
    return [parts[0]] + [across(parts[k], k) for k in (1, 2, 3)]


def total_z(parts):
    return sum(p.astype(F32) for p in parts).astype(BF)


def tie(*values):
    return lax.optimization_barrier(values)


def local_plane(block_in, out_grad, segment_ids, w_qkv, w_out, w_up, w_down, *vecs):
    n_dev = 32
    d_index = lax.axis_index("dp")
    t_index = d_index % 4
    y_index = d_index // 4
    width = block_in.shape[1]
    sub = width // 2
    rows_d = width // 8

    mean_one = jnp.mean(block_in, axis=-1, keepdims=True)
    center = block_in - mean_one
    inv_one = lax.rsqrt(jnp.mean(center * center, axis=-1, keepdims=True) + NORM_EPS)
    hat_low = relocate((center * inv_one).astype(BF))
    stats = relocate(jnp.concatenate([mean_one.reshape(1, -1), inv_one.reshape(1, -1)], axis=0))
    segs = relocate(segment_ids)

    gain_one, shift_one, qv_all, out_shift, gain_two, shift_two, up_all, down_shift = (
        gather_vectors(vecs, n_dev)
    )

    heads = jnp.concatenate(
        [
            w_qkv.reshape(3, -1, 4, HD).transpose(2, 1, 0, 3).reshape(4, -1, 3 * HD),
            w_out.reshape(4, HD, -1).transpose(0, 2, 1),
        ],
        axis=2,
    )
    hids = jnp.concatenate(
        [
            w_up.reshape(w_up.shape[0], 4, -1).transpose(1, 0, 2),
            w_down.reshape(4, -1, w_down.shape[1]).transpose(0, 2, 1),
        ],
        axis=2,
    )
    both, shift_one = tie(jnp.concatenate([heads, hids], axis=2), shift_one)
    both = exchange_t(both).reshape(sub, -1)
    hat_low, stats, segs, gain_one = tie(hat_low, stats, segs, gain_one)
    heads, hids = both[:, : 4 * HD], both[:, 4 * HD :]
    heads_mine = [heads] + [across(heads, k) for k in (1, 2, 3)]
    out_low, hat_low = tie(out_grad.astype(BF), hat_low)
    grad_low = relocate(out_low)
    mine = [hids] + [across(hids, k) for k in (1, 2, 3)]
    other = [swap(hids, 4)]

    qv_mine = lax.dynamic_index_in_dim(qv_all.reshape(2, 4, 4, HD), t_index, 2, False)
    z_order = jnp.arange(4, dtype=jnp.int32) ^ lax.axis_index("mp")
    qv_mine = qv_mine[:, z_order].reshape(2, -1)
    b_local = pair_columns([qv_mine[0], jnp.zeros_like(qv_mine[0]), qv_mine[1]])
    up_shift = lax.dynamic_index_in_dim(up_all.reshape(4, 4, -1), t_index, 1, False)
    up_shift = up_shift[z_order].reshape(-1)
    slopes = head_slopes(4 * z_order + t_index)
    chunk = jnp.asarray(CHUNK_OF_T, jnp.int32)[t_index]
    order = jnp.asarray(T_OF_CHUNK, jnp.int32)[jnp.arange(4, dtype=jnp.int32) ^ chunk]

    hat_one = hat_low.astype(F32)
    mean_here, inv_here = stats[0][:, None], stats[1][:, None]
    block_here = hat_one * (1.0 / inv_here) + mean_here
    rows_one, *heads_mine[1:] = gather_t(
        (hat_one * gain_one + shift_one).astype(BF), near_fill=heads_mine[1:]
    )
    heads_other = [swap(heads, 4)]
    heads_other = heads_other + [swap(m, 4) for m in heads_mine[1:]]
    w_local, w_out_t = head_weights(y_index, heads_mine, heads_other)
    qkv = (dot(rows_one, w_local) + b_local).astype(BF)
    grad_rows = gather_t(grad_low)
    grad_here = grad_low.astype(F32)
    qkv = qkv.reshape(4, -1, w_local.shape[1])
    att, lse = attn_fwd(order, slopes, segs, qkv)
    att_rows = att.reshape(-1, att.shape[2])
    att_part = trans_dot(att_rows, w_out_t).astype(BF)
    own, near, far = scatter_near(att_part)
    att_sum = own.astype(F32) + near.astype(F32)
    att_sum, *mine[1:] = tie(att_sum, *mine[1:])
    att_sum = att_sum + swap(far, 2).astype(F32)
    other = other + [swap(m, 4) for m in mine[1:]]
    units = hids.shape[1] // 2
    up_local = by_y([m[:, :units] for m in mine], [m[:, :units] for m in other], y_index)
    down_t = by_y([m[:, units:] for m in mine], [m[:, units:] for m in other], y_index)
    up_local, down_t = tie(up_local, down_t)
    resid = block_here + att_sum + out_shift
    hat_two, inv_two = norm_rows(resid)
    rows_two = gather_t((hat_two * gain_two + shift_two).astype(BF))
    value, slope = gelu_both(dot(rows_two, up_local) + up_shift)
    hidden = value.astype(BF)
    hidden, grad_rows = tie(hidden, grad_rows)
    down_part = trans_dot(hidden, down_t).astype(BF)
    own_d, near_d, far_d = scatter_near(down_part)
    hidden, own_d = tie(hidden, own_d)
    g_down = cross_dot(grad_rows, hidden).astype(BF)
    far_d, g_down, grad_rows = tie(far_d, g_down, grad_rows)
    block_sum = swap(far_d, 2)
    pre_grad = dot(grad_rows, down_t) * slope
    pre_low = pre_grad.astype(BF)
    two_part = trans_dot(pre_low, up_local).astype(BF)
    own, near, far = scatter_near(two_part)

    far, pre_low = tie(far, pre_low)
    g_up = cross_dot(rows_two, pre_low).astype(BF)
    g_up, block_sum = tie(g_up, block_sum)
    block_sum = own_d.astype(F32) + near_d.astype(F32) + block_sum.astype(F32)
    block_low = (resid + block_sum + down_shift).astype(BF)

    def to_y(grad):
        halves = grad[:sub], grad[sub:]
        keep = jnp.where(y_index == 0, *halves)
        send = jnp.where(y_index == 0, halves[1], halves[0])
        return keep, swap(send, 4)

    def to_z(keep, got):
        both = (keep.astype(F32) + got.astype(F32)).astype(BF)
        return send_z([both[:, k * units : (k + 1) * units] for k in range(4)])

    down_keep, down_got = to_y(g_down)
    up_keep, up_got = to_y(g_up)
    two_grad, up_keep, block_low = tie(scatter_far(own, near, far), up_keep, block_low)

    resid_grad = grad_here + norm_back(two_grad, hat_two, inv_two, gain_two)
    resid_low = resid_grad.astype(BF)
    resid_rows, down_got = gather_t(resid_low, near_fill=[down_got])
    resid_rows, block_low = tie(resid_rows, block_low)
    block_back = bring_back(block_low)
    down_parts = to_z(down_keep, down_got)

    att_grad = dot(resid_rows, w_out_t).astype(BF).reshape(att.shape)
    d_qkv, sums = attn_bwd(order, slopes, segs, qkv, att, att_grad, lse)
    d_rows = d_qkv.reshape(-1, d_qkv.shape[2])
    one_part = trans_dot(d_rows, w_local).astype(BF)
    one_part, d_rows = tie(one_part, d_rows)
    g_qkv = cross_dot(rows_one, d_rows).astype(BF)
    own, near, far = scatter_near(one_part)
    early = (
        sums,
        jnp.sum(resid_grad, axis=0),
        jnp.sum(two_grad * hat_two, axis=0),
        jnp.sum(two_grad, axis=0),
        jnp.sum(pre_grad, axis=0),
        jnp.sum(out_grad, axis=0),
    )
    far, g_qkv, resid_rows, up_got, *early = tie(far, g_qkv, resid_rows, up_got, *early)
    sums, resid_sum, two_hat_sum, two_sum, pre_sum, out_sum = early
    up_parts = to_z(up_keep, up_got)
    qkv_keep, qkv_got = to_y(g_qkv)
    g_out = cross_dot(resid_rows, att_rows).astype(BF)
    out_keep, out_got = to_y(g_out)
    one_grad = scatter_far(own, near, far)
    one_grad, block_back = tie(one_grad, block_back)
    in_grad = resid_grad + norm_back(one_grad, hat_one, inv_here, gain_one)
    in_back = bring_back(in_grad.astype(BF))
    one_sum = jnp.sum(one_grad, axis=0)
    one_sum, qkv_got, out_got, *parts = tie(one_sum, qkv_got, out_got, *up_parts, *down_parts)
    both = (qkv_keep.astype(F32) + qkv_got.astype(F32)).astype(BF).reshape(sub, 2, 3, 2, HD)
    both_out = (out_keep.astype(F32) + out_got.astype(F32)).astype(BF).reshape(sub, 2, 1, 2, HD)
    both = jnp.concatenate([both, both_out], axis=2)
    head_parts = send_z([both[:, k // 2, :, k % 2].reshape(sub, 4 * HD) for k in range(4)])
    g_hid = jnp.concatenate([total_z(parts[:4]), total_z(parts[4:])], axis=1)
    g_hid = exchange_swaps(g_hid.reshape(4, rows_d, 2 * units), t_index).astype(F32)

    mine = jnp.arange(4, dtype=jnp.int32) == t_index
    qv_part = sums.transpose(1, 0, 2).reshape(2, 4, HD)[:, z_order][:, :, None, :]
    qv_place = jnp.where(mine[None, None, :, None], qv_part, 0.0).reshape(2, width)
    up_part = pre_sum.reshape(4, units)[z_order][:, None, :]
    up_place = jnp.where(mine[None, :, None], up_part, 0.0).reshape(-1)
    sums = [
        jnp.sum(one_grad * hat_one, axis=0),
        jnp.sum(one_grad, axis=0),
        qv_place,
        resid_sum,
        two_hat_sum,
        two_sum,
        up_place,
        out_sum,
    ]
    rows, shapes = cut_vectors(sums, n_dev)
    shares = share_vectors(halve_sums(rows, d_index), shapes)
    g_head = exchange_swaps(total_z(head_parts).reshape(4, rows_d, 4 * HD), t_index)
    g_head = g_head.astype(F32).reshape(4, rows_d, 4, HD)
    qkv_share = g_head[:, :, :3].transpose(2, 1, 0, 3).reshape(w_qkv.shape)
    out_share = g_head[:, :, 3].transpose(0, 2, 1).reshape(w_out.shape)

    up_share = g_hid[..., :units].transpose(1, 0, 2).reshape(w_up.shape)
    down_share = g_hid[..., units:].transpose(0, 2, 1).reshape(w_down.shape)

    block_out = block_back.astype(F32)
    return (block_out, in_back.astype(F32), qkv_share, out_share, up_share, down_share, *shares)


def solution(mesh):
    n_dp, n_mp = mesh.shape["dp"], mesh.shape["mp"]
    plane = (n_dp, n_mp) == (8, 4)
    local = local_plane if plane else local_any(n_dp, n_mp)
    both = ("dp", "mp")
    weights = (P(None, "dp", "mp"), P("mp", "dp"), P("dp", "mp"), P("mp", "dp"))
    vectors = (P(both), P(both), P(None, both), P(both), P(both), P(both), P(both), P(both))
    return jax.shard_map(
        local,
        mesh=mesh,
        in_specs=(P(both, None), P(both, None), P("dp"), *weights, *vectors),
        out_specs=(P(both, None), P(both, None), *weights, *vectors),
        check_vma=False,
    )
```

```python
import jax
import jax.numpy as jnp
from jax import lax
from jax.experimental import pallas as pl
from jax.experimental.pallas import tpu as pltpu
from jax.sharding import PartitionSpec as P


H = 16
HD = 64
L = 1152
BLK = 128
REACH = 5

NORM_EPS = 1e-05
GELU_SCALE = 0.7978845608028654
GELU_CUBE = 0.044715

BF = jnp.bfloat16
F32 = jnp.float32


def gelu_both(pre_act):
    inner = jnp.tanh(GELU_SCALE * (pre_act + GELU_CUBE * pre_act * pre_act * pre_act))
    value = 0.5 * pre_act * (1.0 + inner)
    slope = 0.5 * (1.0 + inner) + 0.5 * pre_act * (1.0 - inner * inner) * GELU_SCALE * (
        1.0 + 3.0 * GELU_CUBE * pre_act * pre_act
    )
    return value, slope


def norm_rows(inputs):
    center = inputs - jnp.mean(inputs, axis=-1, keepdims=True)
    scale_inv = lax.rsqrt(jnp.mean(center * center, axis=-1, keepdims=True) + NORM_EPS)
    return (center * scale_inv, scale_inv)


def norm_back(norm_grad, x_hat, scale_inv, gain):
    scaled = norm_grad * gain
    return scale_inv * (
        scaled
        - jnp.mean(scaled, axis=-1, keepdims=True)
        - x_hat * jnp.mean(scaled * x_hat, axis=-1, keepdims=True)
    )


def dot(left, right):
    return jnp.dot(left, right, preferred_element_type=F32)


def cross_dot(left, right):
    return lax.dot_general(left, right, (((0,), (0,)), ((), ())), preferred_element_type=F32)


def trans_dot(left, right):
    return lax.dot_general(left, right, (((1,), (1,)), ((), ())), preferred_element_type=F32)


def flip(x):
    return x.astype(F32).T


def load_rows(order_ref, src_ref, dst_ref, nb, rb):
    for k in range(nb):
        dst_ref[k * rb : (k + 1) * rb, :] = src_ref[order_ref[k]]


def half_masks(shape):
    lane = lax.broadcasted_iota(jnp.int32, shape, 1)
    return (lane < HD, lane >= HD)


def distances(b, segr_ref, segc_ref):
    w0 = max(0, b - REACH) * BLK
    w1 = (b + 1) * BLK
    keys = w0 + lax.broadcasted_iota(jnp.int32, (w1 - w0, BLK), 0)
    rows = b * BLK + lax.broadcasted_iota(jnp.int32, (w1 - w0, BLK), 1)
    same = segc_ref[w0:w1, :] == segr_ref[:, b * BLK : (b + 1) * BLK]
    gap = rows - keys
    dist = jnp.where(same & (gap >= 0), gap.astype(F32), 1e30)
    return w0, w1, dist


def attn_fwd_kernel(
    order_ref, slope_ref, segr_ref, segc_ref, q_ref, k_ref, v_ref, att_ref, lse_ref,
    q_s, k_s, v_s, vt_s, a_s, *, nb, rb,
):
    pair = pl.program_id(0)
    load_rows(order_ref, q_ref, q_s, nb, rb)
    load_rows(order_ref, k_ref, k_s, nb, rb)
    load_rows(order_ref, v_ref, v_s, nb, rb)
    vt_s[...] = flip(v_s[...]).astype(BF)
    halves = half_masks((BLK, 2 * HD))
    for b in range(L // BLK):
        r0 = b * BLK
        w0, w1, dist = distances(b, segr_ref, segc_ref)
        q_blk = q_s[r0 : r0 + BLK, :] * BF(HD ** (-0.5))
        outs = []
        for h in range(2):
            q_h = jnp.where(halves[h], q_blk, BF(0))
            s = trans_dot(k_s[w0:w1, :], q_h) - slope_ref[2 * pair + h] * dist
            top = jnp.max(s, axis=0, keepdims=True)
            e = jnp.exp(s - top)
            total = jnp.sum(e, axis=0, keepdims=True)
            lse_ref[0, h : h + 1, r0 : r0 + BLK] = top + jnp.log(total)
            prob = (e * (1.0 / total)).astype(BF)
            outs.append(dot(vt_s[h * HD : (h + 1) * HD, w0:w1], prob))
        a_s[r0 : r0 + BLK, :] = jnp.concatenate(outs, axis=0).T.astype(BF)
    for k in range(nb):
        att_ref[order_ref[k]] = a_s[k * rb : (k + 1) * rb, :]


def attn_bwd_kernel(
    order_ref, slope_ref, segr_ref, segc_ref, q_ref, k_ref, v_ref, att_ref, grad_ref, lse_ref,
    out_ref, sum_ref, q_s, k_s, v_s, kt_s, a_s, g_s, dq_s, dk_s, dv_s, *, nb, rb,
):
    pair = pl.program_id(0)
    load_rows(order_ref, q_ref, q_s, nb, rb)
    load_rows(order_ref, k_ref, k_s, nb, rb)
    load_rows(order_ref, v_ref, v_s, nb, rb)
    load_rows(order_ref, att_ref, a_s, nb, rb)
    load_rows(order_ref, grad_ref, g_s, nb, rb)
    kt_s[...] = flip(k_s[...]).astype(BF)
    dk_s[...] = jnp.zeros(dk_s.shape, F32)
    dv_s[...] = jnp.zeros(dv_s.shape, F32)
    halves = half_masks((BLK, 2 * HD))
    q_sum = jnp.zeros((1, 2 * HD), F32)
    for b in range(L // BLK):
        r0 = b * BLK
        w0, w1, dist = distances(b, segr_ref, segc_ref)
        q_blk = q_s[r0 : r0 + BLK, :] * BF(HD ** (-0.5))
        g_blk = g_s[r0 : r0 + BLK, :]
        prod = (a_s[r0 : r0 + BLK, :].astype(F32) * g_blk.astype(F32)).T
        probs, grads, q_hs, g_hs, dq_t = [], [], [], [], []
        for h in range(2):
            q_h = jnp.where(halves[h], q_blk, BF(0))
            g_h = jnp.where(halves[h], g_blk, BF(0))
            s = trans_dot(k_s[w0:w1, :], q_h) - slope_ref[2 * pair + h] * dist
            p = jnp.exp(s - lse_ref[0, h : h + 1, r0 : r0 + BLK])
            delta = jnp.sum(prod[h * HD : (h + 1) * HD, :], axis=0, keepdims=True)
            dp = trans_dot(v_s[w0:w1, :], g_h)
            ds = (p * (dp - delta)).astype(BF)
            dq_t.append(dot(kt_s[h * HD : (h + 1) * HD, w0:w1], ds))
            probs.append(p.astype(BF))
            grads.append(ds)
            q_hs.append(q_h)
            g_hs.append(g_h)
        dv_s[w0:w1, :] += dot(jnp.concatenate(probs, axis=1), jnp.concatenate(g_hs, axis=0))
        dk_s[w0:w1, :] += dot(jnp.concatenate(grads, axis=1), jnp.concatenate(q_hs, axis=0))
        dq = jnp.concatenate(dq_t, axis=0).T * HD ** (-0.5)
        q_sum = q_sum + jnp.sum(dq, axis=0, keepdims=True)
        dq_s[r0 : r0 + BLK, :] = dq.astype(BF)
    sum_ref[0, 0:1, :] = q_sum
    sum_ref[0, 1:2, :] = jnp.sum(dv_s[...], axis=0, keepdims=True)
    for k in range(nb):
        rows = slice(k * rb, (k + 1) * rb)
        out_ref[order_ref[k], :, 0 : 2 * HD] = dq_s[rows, :]
        out_ref[order_ref[k], :, 2 * HD : 4 * HD] = dk_s[rows, :].astype(BF)
        out_ref[order_ref[k], :, 4 * HD : 6 * HD] = dv_s[rows, :].astype(BF)


def attn_specs(nb, rb):
    smem = pl.BlockSpec(memory_space=pltpu.SMEM)
    col = lambda which: pl.BlockSpec((nb, rb, 2 * HD), lambda p: (0, 0, 3 * p + which))
    base = [
        smem,
        smem,
        pl.BlockSpec((1, L), lambda p: (0, 0)),
        pl.BlockSpec((L, 1), lambda p: (0, 0)),
        col(0),
        col(1),
        col(2),
    ]
    one = pl.BlockSpec((nb, rb, 2 * HD), lambda p: (0, 0, p))
    lse = pl.BlockSpec((1, 2, L), lambda p: (p, 0, 0))
    return base, one, lse


def attn_fwd(order, slopes, segs, qkv):
    nb, rb, cols = qkv.shape
    pairs = cols // (6 * HD)
    base, one, lse = attn_specs(nb, rb)
    rows = lambda: pltpu.VMEM((L, 2 * HD), BF)
    return pl.pallas_call(
        lambda *refs: attn_fwd_kernel(*refs, nb=nb, rb=rb),
        grid=(pairs,),
        in_specs=base,
        out_specs=[one, lse],
        out_shape=[
            jax.ShapeDtypeStruct((nb, rb, pairs * 2 * HD), BF),
            jax.ShapeDtypeStruct((pairs, 2, L), F32),
        ],
        scratch_shapes=[rows(), rows(), rows(), pltpu.VMEM((2 * HD, L), BF), rows()],
        name="attn_fwd",
        cost_estimate=pl.CostEstimate(
            flops=pairs * 4 * L * L * HD * 4, transcendentals=pairs * L * L, bytes_accessed=1 << 24
        ),
    )(order, slopes, segs.reshape(1, L), segs.reshape(L, 1), qkv, qkv, qkv)


def attn_bwd(order, slopes, segs, qkv, att, att_grad, lse_rows):
    nb, rb, cols = qkv.shape
    pairs = cols // (6 * HD)
    base, one, lse = attn_specs(nb, rb)
    rows = lambda dt=BF: pltpu.VMEM((L, 2 * HD), dt)
    return pl.pallas_call(
        lambda *refs: attn_bwd_kernel(*refs, nb=nb, rb=rb),
        grid=(pairs,),
        in_specs=base + [one, one, lse],
        out_specs=[
            pl.BlockSpec((nb, rb, 6 * HD), lambda p: (0, 0, p)),
            pl.BlockSpec((1, 2, 2 * HD), lambda p: (p, 0, 0)),
        ],
        out_shape=[
            jax.ShapeDtypeStruct((nb, rb, cols), BF),
            jax.ShapeDtypeStruct((pairs, 2, 2 * HD), F32),
        ],
        scratch_shapes=[rows(), rows(), rows(), pltpu.VMEM((2 * HD, L), BF), rows(), rows(),
                        rows(), rows(F32), rows(F32)],
        name="attn_bwd",
        cost_estimate=pl.CostEstimate(
            flops=pairs * 8 * L * L * HD * 4, transcendentals=pairs * L * L, bytes_accessed=1 << 25
        ),
    )(order, slopes, segs.reshape(1, L), segs.reshape(L, 1), qkv, qkv, qkv, att, att_grad, lse_rows)


def gather_vectors(vecs, n_dev):
    flat = jnp.concatenate([v.reshape(-1) for v in vecs])
    spread = jnp.broadcast_to(flat[None, :], (n_dev, flat.shape[0]))
    got = lax.all_to_all(spread, ("dp", "mp"), 0, 0, tiled=True)
    full, at = [], 0
    for v in vecs:
        n = v.size
        part = got[:, at : at + n]
        if v.ndim == 2:
            part = part.reshape(n_dev, v.shape[0], v.shape[1]).transpose(1, 0, 2)
            full.append(part.reshape(v.shape[0], -1))
        else:
            full.append(part.reshape(-1))
        at += n
    return full


def cut_vectors(fulls, n_dev):
    parts, shapes = [], []
    for v in fulls:
        if v.ndim == 2:
            part = v.reshape(v.shape[0], n_dev, -1).transpose(1, 0, 2)
            shapes.append((v.shape[0], v.shape[1] // n_dev))
        else:
            part = v
            shapes.append((v.shape[0] // n_dev,))
        parts.append(part.reshape(n_dev, -1))
    return jnp.concatenate(parts, axis=1), shapes


def share_vectors(flat, shapes):
    outs, at = [], 0
    for shape in shapes:
        n = shape[0] * (shape[1] if len(shape) == 2 else 1)
        outs.append(flat[at : at + n].reshape(shape))
        at += n
    return outs


def scatter_vectors(fulls, n_dev):
    rows, shapes = cut_vectors(fulls, n_dev)
    got = lax.all_to_all(rows, ("dp", "mp"), 0, 0, tiled=True)
    return share_vectors(jnp.sum(got, axis=0), shapes)


def head_slopes(numbers):
    return jnp.exp2(-8.0 * (numbers + 1).astype(F32) / H)


def pair_columns(parts):
    stacked = jnp.stack([p.reshape(p.shape[:-1] + (-1, 2 * HD)) for p in parts], axis=-2)
    return stacked.reshape(stacked.shape[:-3] + (-1,))


def local_any(n_dp, n_mp):
    n_dev = n_dp * n_mp

    def scatter_rows(part):
        return lax.psum_scatter(part.astype(BF), "mp", scatter_dimension=0, tiled=True).astype(F32)

    def scatter_grad(part, dim):
        return lax.psum_scatter(part.astype(BF), "dp", scatter_dimension=dim, tiled=True).astype(F32)

    def local(block_in, out_grad, segment_ids, w_qkv, w_out, w_up, w_down, *vecs):
        model_index = lax.axis_index("mp")
        gain_one, shift_one, qv_all, out_shift, gain_two, shift_two, up_all, down_shift = (
            gather_vectors(vecs, n_dev)
        )
        qkv_full = lax.all_gather(w_qkv, "dp", axis=1, tiled=True)
        out_full = lax.all_gather(w_out, "dp", axis=1, tiled=True)
        up_full = lax.all_gather(w_up, "dp", axis=0, tiled=True)
        down_full = lax.all_gather(w_down, "dp", axis=1, tiled=True)
        head_cols = qkv_full.shape[2]
        hid_cols = up_full.shape[1]
        n_heads = head_cols // HD
        qv_shift = lax.dynamic_slice_in_dim(qv_all, model_index * head_cols, head_cols, 1)
        up_shift = lax.dynamic_slice_in_dim(up_all, model_index * hid_cols, hid_cols, 0)
        slopes = head_slopes(model_index * n_heads + jnp.arange(n_heads, dtype=jnp.int32))
        order = jnp.zeros((1,), jnp.int32)
        w_local = pair_columns([qkv_full[0], qkv_full[1], qkv_full[2]])
        b_local = pair_columns([qv_shift[0], jnp.zeros_like(qv_shift[0]), qv_shift[1]])
        hat_one, inv_one = norm_rows(block_in)
        normed_one = (hat_one * gain_one + shift_one).astype(BF)
        rows_one = lax.all_gather(normed_one, "mp", axis=0, tiled=True)
        qkv = (dot(rows_one, w_local) + b_local).astype(BF)[None]
        att, lse = attn_fwd(order, slopes, segment_ids, qkv)
        resid = block_in + scatter_rows(dot(att[0], out_full)) + out_shift
        hat_two, inv_two = norm_rows(resid)
        normed_two = (hat_two * gain_two + shift_two).astype(BF)
        rows_two = lax.all_gather(normed_two, "mp", axis=0, tiled=True)
        value, slope = gelu_both(dot(rows_two, up_full) + up_shift)
        hidden = value.astype(BF)
        block_out = resid + scatter_rows(dot(hidden, down_full)) + down_shift
        grad_rows = lax.all_gather(out_grad.astype(BF), "mp", axis=0, tiled=True)
        down_share = scatter_grad(cross_dot(hidden, grad_rows), 1)
        pre_grad = trans_dot(grad_rows, down_full) * slope
        pre_low = pre_grad.astype(BF)
        up_share = scatter_grad(cross_dot(rows_two, pre_low), 0)
        two_grad = scatter_rows(trans_dot(pre_low, up_full))
        resid_grad = out_grad + norm_back(two_grad, hat_two, inv_two, gain_two)
        resid_rows = lax.all_gather(resid_grad.astype(BF), "mp", axis=0, tiled=True)
        out_share = scatter_grad(cross_dot(att[0], resid_rows), 1)
        att_grad = trans_dot(resid_rows, out_full).astype(BF)[None]
        d_qkv, sums = attn_bwd(order, slopes, segment_ids, qkv, att, att_grad, lse)
        grad_w = cross_dot(rows_one, d_qkv[0])
        grad_w = grad_w.reshape(grad_w.shape[0], -1, 3, 2 * HD).transpose(2, 0, 1, 3)
        qkv_share = scatter_grad(grad_w.reshape(3, grad_w.shape[1], -1), 1)
        one_grad = scatter_rows(trans_dot(d_qkv[0], w_local))
        in_grad = resid_grad + norm_back(one_grad, hat_one, inv_one, gain_one)
        qv_place = lax.dynamic_update_slice_in_dim(
            jnp.zeros(qv_all.shape, F32),
            sums.transpose(1, 0, 2).reshape(2, -1),
            model_index * head_cols,
            1,
        )
        up_place = lax.dynamic_update_slice_in_dim(
            jnp.zeros(up_all.shape, F32), jnp.sum(pre_grad, axis=0), model_index * hid_cols, 0
        )
        shares = scatter_vectors(
            [
                jnp.sum(one_grad * hat_one, axis=0),
                jnp.sum(one_grad, axis=0),
                qv_place,
                jnp.sum(resid_grad, axis=0),
                jnp.sum(two_grad * hat_two, axis=0),
                jnp.sum(two_grad, axis=0),
                up_place,
                jnp.sum(out_grad, axis=0),
            ],
            n_dev,
        )
        return (block_out, in_grad, qkv_share, out_share, up_share, down_share, *shares)

    return local


CHUNK_OF_T = (0, 3, 1, 2)
T_OF_CHUNK = (0, 2, 3, 1)
PLANE_OF_T = (0, 3, 1, 2)
GROUPS = [[0, 1, 2, 3], [4, 5, 6, 7]]
TO_PLANE = [
    ((4 * y + t) * 4 + z, (4 * y + T_OF_CHUNK[z]) * 4 + PLANE_OF_T[t])
    for y in range(2)
    for t in range(4)
    for z in range(4)
]
FROM_PLANE = [(b, a) for a, b in TO_PLANE]


def swap(x, bits):
    return lax.ppermute(x, "dp", [(i, i ^ bits) for i in range(8)])


def relocate(x):
    return lax.ppermute(x, ("dp", "mp"), TO_PLANE)


def bring_back(x):
    return lax.ppermute(x, ("dp", "mp"), FROM_PLANE)


def gather_t(x, near_fill=()):
    far = swap(x, 2)
    near, *fill = tie(swap(x, 1), *near_fill)
    rows = jnp.concatenate([x, near, far, swap(far, 1)], axis=0)
    return (rows, *fill) if fill else rows


def scatter_near(part):
    n = part.shape[0] // 4
    low = part.astype(BF)
    near = swap(jnp.concatenate([low[n : 2 * n], low[3 * n :]], axis=0), 1)
    far = (part[2 * n : 3 * n].astype(F32) + near[n:].astype(F32)).astype(BF)
    return part[:n], near[:n], far


def scatter_far(own, near, far):
    far = swap(far, 2)
    return own.astype(F32) + near.astype(F32) + far.astype(F32)


def exchange_t(x):
    return lax.all_to_all(x, "dp", 0, 0, tiled=True, axis_index_groups=GROUPS)


def exchange_swaps(x, t_index):
    got = [lax.dynamic_index_in_dim(x, t_index ^ j, 0, False) for j in range(4)]
    got = [got[0]] + [swap(got[j], j) for j in (1, 2, 3)]
    return jnp.stack(got)[jnp.arange(4, dtype=jnp.int32) ^ t_index]


def halve_sums(rows, d_index):
    rows = rows.reshape(2, 2, 2, 2, 2, -1)
    z_index = lax.axis_index("mp")
    bits = (d_index & 1, (d_index >> 1) & 1, d_index >> 2, z_index & 1, z_index >> 1)
    moves = (lambda v: swap(v, 1), lambda v: swap(v, 2), lambda v: swap(v, 4),
             lambda v: across(v, 1), lambda v: across(v, 2))
    for axis, bit, move in zip((2, 1, 0, 1, 0), bits, moves):
        keep = lax.dynamic_index_in_dim(rows, bit, axis, False)
        rows = keep + move(lax.dynamic_index_in_dim(rows, 1 - bit, axis, False))
    return rows


def across(x, bits):
    return lax.ppermute(x, "mp", [(i, i ^ bits) for i in range(4)])


def by_y(mine, other, y_index):
    mine, other = jnp.concatenate(mine, axis=1), jnp.concatenate(other, axis=1)
    first = jnp.where(y_index == 0, mine, other)
    second = jnp.where(y_index == 0, other, mine)
    return jnp.concatenate([first, second], axis=0)


def head_weights_kernel(y_ref, *refs, n):
    qkv_ref, out_ref = refs[8:]

    def write(half, rows):
        for p in range(2):
            low, high = refs[4 * half + 2 * p][...], refs[4 * half + 2 * p + 1][...]
            for w in range(4):
                cols = slice(w * HD, (w + 1) * HD)
                both = jnp.concatenate([low[:, cols], high[:, cols]], axis=1)
                if w < 3:
                    qkv_ref[rows, (3 * p + w) * 2 * HD : (3 * p + w + 1) * 2 * HD] = both
                else:
                    out_ref[rows, p * 2 * HD : (p + 1) * 2 * HD] = both

    for y in range(2):

        @pl.when(y_ref[0] == y)
        def _():
            for half in range(2):
                write(half, slice((y ^ half) * n, ((y ^ half) + 1) * n))


def head_weights(y_index, mine, other):
    n = mine[0].shape[0]
    vmem = pl.BlockSpec(memory_space=pltpu.VMEM)
    return pl.pallas_call(
        lambda *refs: head_weights_kernel(*refs, n=n),
        in_specs=[pl.BlockSpec(memory_space=pltpu.SMEM)] + [vmem] * 8,
        out_specs=[vmem, vmem],
        out_shape=[
            jax.ShapeDtypeStruct((2 * n, 12 * HD), BF),
            jax.ShapeDtypeStruct((2 * n, 4 * HD), BF),
        ],
        name="head_weights",
    )(y_index.reshape(1), *mine, *other)


def send_z(parts):
    return [parts[0]] + [across(parts[k], k) for k in (1, 2, 3)]


def total_z(parts):
    return sum(p.astype(F32) for p in parts).astype(BF)


def tie(*values):
    return lax.optimization_barrier(values)


def local_plane(block_in, out_grad, segment_ids, w_qkv, w_out, w_up, w_down, *vecs):
    n_dev = 32
    d_index = lax.axis_index("dp")
    t_index = d_index % 4
    y_index = d_index // 4
    width = block_in.shape[1]
    sub = width // 2
    rows_d = width // 8

    mean_one = jnp.mean(block_in, axis=-1, keepdims=True)
    center = block_in - mean_one
    inv_one = lax.rsqrt(jnp.mean(center * center, axis=-1, keepdims=True) + NORM_EPS)
    hat_low = relocate((center * inv_one).astype(BF))
    stats = relocate(jnp.concatenate([mean_one.reshape(1, -1), inv_one.reshape(1, -1)], axis=0))
    segs = relocate(segment_ids)

    gain_one, shift_one, qv_all, out_shift, gain_two, shift_two, up_all, down_shift = (
        gather_vectors(vecs, n_dev)
    )

    heads = jnp.concatenate(
        [
            w_qkv.reshape(3, -1, 4, HD).transpose(2, 1, 0, 3).reshape(4, -1, 3 * HD),
            w_out.reshape(4, HD, -1).transpose(0, 2, 1),
        ],
        axis=2,
    )
    hids = jnp.concatenate(
        [
            w_up.reshape(w_up.shape[0], 4, -1).transpose(1, 0, 2),
            w_down.reshape(4, -1, w_down.shape[1]).transpose(0, 2, 1),
        ],
        axis=2,
    )
    both, shift_one = tie(jnp.concatenate([heads, hids], axis=2), shift_one)
    both = exchange_t(both).reshape(sub, -1)
    hat_low, stats, segs, gain_one = tie(hat_low, stats, segs, gain_one)
    heads, hids = both[:, : 4 * HD], both[:, 4 * HD :]
    heads_mine = [heads] + [across(heads, k) for k in (1, 2, 3)]
    out_low, hat_low = tie(out_grad.astype(BF), hat_low)
    grad_low = relocate(out_low)
    mine = [hids] + [across(hids, k) for k in (1, 2, 3)]
    other = [swap(hids, 4)]

    qv_mine = lax.dynamic_index_in_dim(qv_all.reshape(2, 4, 4, HD), t_index, 2, False)
    z_order = jnp.arange(4, dtype=jnp.int32) ^ lax.axis_index("mp")
    qv_mine = qv_mine[:, z_order].reshape(2, -1)
    b_local = pair_columns([qv_mine[0], jnp.zeros_like(qv_mine[0]), qv_mine[1]])
    up_shift = lax.dynamic_index_in_dim(up_all.reshape(4, 4, -1), t_index, 1, False)
    up_shift = up_shift[z_order].reshape(-1)
    slopes = head_slopes(4 * z_order + t_index)
    chunk = jnp.asarray(CHUNK_OF_T, jnp.int32)[t_index]
    order = jnp.asarray(T_OF_CHUNK, jnp.int32)[jnp.arange(4, dtype=jnp.int32) ^ chunk]

    hat_one = hat_low.astype(F32)
    mean_here, inv_here = stats[0][:, None], stats[1][:, None]
    block_here = hat_one * (1.0 / inv_here) + mean_here
    rows_one, *heads_mine[1:] = gather_t(
        (hat_one * gain_one + shift_one).astype(BF), near_fill=heads_mine[1:]
    )
    heads_other = [swap(heads, 4)]
    heads_other = heads_other + [swap(m, 4) for m in heads_mine[1:]]
    w_local, w_out_t = head_weights(y_index, heads_mine, heads_other)
    qkv = (dot(rows_one, w_local) + b_local).astype(BF)
    qkv = qkv.reshape(4, -1, w_local.shape[1])
    att, lse = attn_fwd(order, slopes, segs, qkv)
    att_rows = att.reshape(-1, att.shape[2])
    att_part = trans_dot(att_rows, w_out_t).astype(BF)
    own, near, far = scatter_near(att_part)
    att_sum = own.astype(F32) + near.astype(F32)
    att_sum, *mine[1:] = tie(att_sum, *mine[1:])
    att_sum = att_sum + swap(far, 2).astype(F32)
    other = other + [swap(m, 4) for m in mine[1:]]
    units = hids.shape[1] // 2
    up_local = by_y([m[:, :units] for m in mine], [m[:, :units] for m in other], y_index)
    down_t = by_y([m[:, units:] for m in mine], [m[:, units:] for m in other], y_index)
    up_local, down_t = tie(up_local, down_t)
    resid = block_here + att_sum + out_shift
    hat_two, inv_two = norm_rows(resid)
    normed = (hat_two * gain_two + shift_two).astype(BF)
    far = swap(normed, 2)
    near = swap(normed, 1)
    far, grad_low = tie(far, grad_low)
    rows_two = jnp.concatenate([normed, near, far, swap(far, 1)], axis=0)
    grad_rows = gather_t(grad_low)
    grad_here = grad_low.astype(F32)
    pre_act = dot(rows_two, up_local)
    value, slope = gelu_both(pre_act + up_shift)
    hidden = value.astype(BF)
    hidden, grad_rows = tie(hidden, grad_rows)
    down_part = trans_dot(hidden, down_t).astype(BF)
    own_d, near_d, far_d = scatter_near(down_part)
    hidden, own_d = tie(hidden, own_d)
    g_down = cross_dot(grad_rows, hidden).astype(BF)
    far_d, g_down, grad_rows = tie(far_d, g_down, grad_rows)
    block_sum = swap(far_d, 2)
    pre_grad = dot(grad_rows, down_t) * slope
    pre_low = pre_grad.astype(BF)
    two_part = trans_dot(pre_low, up_local).astype(BF)
    own, near, far = scatter_near(two_part)

    far, pre_low = tie(far, pre_low)
    g_up = cross_dot(rows_two, pre_low).astype(BF)
    g_up, block_sum = tie(g_up, block_sum)
    block_sum = own_d.astype(F32) + near_d.astype(F32) + block_sum.astype(F32)
    block_low = (resid + block_sum + down_shift).astype(BF)

    def to_y(grad):
        halves = grad[:sub], grad[sub:]
        keep = jnp.where(y_index == 0, *halves)
        send = jnp.where(y_index == 0, halves[1], halves[0])
        return keep, swap(send, 4)

    def to_z(keep, got):
        both = (keep.astype(F32) + got.astype(F32)).astype(BF)
        return send_z([both[:, k * units : (k + 1) * units] for k in range(4)])

    down_keep, down_got = to_y(g_down)
    up_keep, up_got = to_y(g_up)
    two_grad, up_keep, block_low = tie(scatter_far(own, near, far), up_keep, block_low)

    resid_grad = grad_here + norm_back(two_grad, hat_two, inv_two, gain_two)
    resid_low = resid_grad.astype(BF)
    resid_rows, down_got = gather_t(resid_low, near_fill=[down_got])
    resid_rows, block_low = tie(resid_rows, block_low)
    block_back = bring_back(block_low)
    down_parts = to_z(down_keep, down_got)

    att_grad = dot(resid_rows, w_out_t).astype(BF).reshape(att.shape)
    d_qkv, sums = attn_bwd(order, slopes, segs, qkv, att, att_grad, lse)
    d_rows = d_qkv.reshape(-1, d_qkv.shape[2])
    one_part = trans_dot(d_rows, w_local).astype(BF)
    one_part, d_rows = tie(one_part, d_rows)
    g_qkv = cross_dot(rows_one, d_rows).astype(BF)
    own, near, far = scatter_near(one_part)
    early = (
        sums,
        jnp.sum(resid_grad, axis=0),
        jnp.sum(two_grad * hat_two, axis=0),
        jnp.sum(two_grad, axis=0),
        jnp.sum(pre_grad, axis=0),
        jnp.sum(out_grad, axis=0),
    )
    far, g_qkv, resid_rows, up_got, *early = tie(far, g_qkv, resid_rows, up_got, *early)
    sums, resid_sum, two_hat_sum, two_sum, pre_sum, out_sum = early
    up_parts = to_z(up_keep, up_got)
    qkv_keep, qkv_got = to_y(g_qkv)
    g_out = cross_dot(resid_rows, att_rows).astype(BF)
    out_keep, out_got = to_y(g_out)
    one_grad = scatter_far(own, near, far)
    one_grad, block_back = tie(one_grad, block_back)
    in_grad = resid_grad + norm_back(one_grad, hat_one, inv_here, gain_one)
    in_back = bring_back(in_grad.astype(BF))
    one_sum = jnp.sum(one_grad, axis=0)
    one_sum, qkv_got, out_got, *parts = tie(one_sum, qkv_got, out_got, *up_parts, *down_parts)
    both = (qkv_keep.astype(F32) + qkv_got.astype(F32)).astype(BF).reshape(sub, 2, 3, 2, HD)
    both_out = (out_keep.astype(F32) + out_got.astype(F32)).astype(BF).reshape(sub, 2, 1, 2, HD)
    both = jnp.concatenate([both, both_out], axis=2)
    head_parts = send_z([both[:, k // 2, :, k % 2].reshape(sub, 4 * HD) for k in range(4)])
    g_hid = jnp.concatenate([total_z(parts[:4]), total_z(parts[4:])], axis=1)
    g_hid = exchange_swaps(g_hid.reshape(4, rows_d, 2 * units), t_index).astype(F32)

    mine = jnp.arange(4, dtype=jnp.int32) == t_index
    qv_part = sums.transpose(1, 0, 2).reshape(2, 4, HD)[:, z_order][:, :, None, :]
    qv_place = jnp.where(mine[None, None, :, None], qv_part, 0.0).reshape(2, width)
    up_part = pre_sum.reshape(4, units)[z_order][:, None, :]
    up_place = jnp.where(mine[None, :, None], up_part, 0.0).reshape(-1)
    sums = [
        jnp.sum(one_grad * hat_one, axis=0),
        jnp.sum(one_grad, axis=0),
        qv_place,
        resid_sum,
        two_hat_sum,
        two_sum,
        up_place,
        out_sum,
    ]
    rows, shapes = cut_vectors(sums, n_dev)
    shares = share_vectors(halve_sums(rows, d_index), shapes)
    g_head = exchange_swaps(total_z(head_parts).reshape(4, rows_d, 4 * HD), t_index)
    g_head = g_head.astype(F32).reshape(4, rows_d, 4, HD)
    qkv_share = g_head[:, :, :3].transpose(2, 1, 0, 3).reshape(w_qkv.shape)
    out_share = g_head[:, :, 3].transpose(0, 2, 1).reshape(w_out.shape)

    up_share = g_hid[..., :units].transpose(1, 0, 2).reshape(w_up.shape)
    down_share = g_hid[..., units:].transpose(0, 2, 1).reshape(w_down.shape)

    block_out = block_back.astype(F32)
    return (block_out, in_back.astype(F32), qkv_share, out_share, up_share, down_share, *shares)


def solution(mesh):
    n_dp, n_mp = mesh.shape["dp"], mesh.shape["mp"]
    plane = (n_dp, n_mp) == (8, 4)
    local = local_plane if plane else local_any(n_dp, n_mp)
    both = ("dp", "mp")
    weights = (P(None, "dp", "mp"), P("mp", "dp"), P("dp", "mp"), P("mp", "dp"))
    vectors = (P(both), P(both), P(None, both), P(both), P(both), P(both), P(both), P(both))
    return jax.shard_map(
        local,
        mesh=mesh,
        in_specs=(P(both, None), P(both, None), P("dp"), *weights, *vectors),
        out_specs=(P(both, None), P(both, None), *weights, *vectors),
        check_vma=False,
    )
```
